32 devices in a mesh: star: 8 (over y, x, core), row: 4 (over z).
Axes of the slice: x: 2, y: 2, z: 4, core: 2. Of those that a mesh axis runs over, the one named last changes fastest.
Arguments:
- feature_maps: bfloat16 [64, 1024, 1024], P(None, 'row'), may hold values from -6 to 6
- coef_table: bfloat16 [64, 64], replicated, may hold values from -0.119628906 to 0.119628906
- star_counts: int32 [8], replicated, may hold values from 1 to 12, 32 in all
- star_cells: int32 [8, 12], replicated, may hold values from 0 to 63
- star_bands: int32 [8, 12], replicated, may hold values from 0 to 7
- psf_cotangent: bfloat16 [96, 1024, 1024], P('star', 'row'), may hold values from -6 to 6
Outputs:
- map_grad: float32 [64, 1024, 1024], P('star', 'row')
- coef_grad: float32 [64, 64], replicated
The draws below stay inside these ranges and needn't reach their ends.
Inputs may be any that keep to these rules, and one draw needn't show every extreme that they name: The live stars of group g fill its slots 0 to star_counts[g] - 1; the counts sum to 32, and some group has exactly 12.
All inputs are finite; a program needn't handle non-finite values.
Results may differ from the reference program's by a relative error of at most 0.008.
Values may be sent and summed in bfloat16 or wider, within the bound.
A program may use at most 192 MiB of HBM per device.

```python
import math
import jax
import jax.numpy as jnp
import numpy as np
from jax import lax

PUPIL = 1024
MAPS = 64
CELLS = 64
BANDS = 8
SLOT = 12
TOTAL = 32
N_STAR = 8


def spread_values(key, limit, length):
    first_key, second_key = jax.random.split(key)
    values = jax.random.randint(first_key, (length,), 0, limit, dtype=jnp.int32)
    places = jax.random.permutation(second_key, length)
    values = values.at[places[0]].set(limit - 1)
    return values.at[places[1]].set(0)


def draw_star_cells(key, part):
    return spread_values(jax.random.fold_in(key, 11), CELLS, N_STAR * SLOT).reshape(N_STAR, SLOT)


def draw_star_bands(key, part):
    return spread_values(jax.random.fold_in(key, 23), BANDS, N_STAR * SLOT).reshape(N_STAR, SLOT)


def steps_of(stream_key, extent, shards, smallest, largest):
    def one(axis_at, blocks):
        draws = jax.random.uniform(jax.random.fold_in(jax.random.fold_in(stream_key, 6), axis_at), (blocks,), jnp.float32, smallest / len(shards), largest / len(shards))
        return jnp.repeat(jnp.exp(draws), extent[axis_at] // blocks).reshape((-1,) + (1,) * (len(extent) - axis_at - 1))

    factor_of = one(*shards[0])
    for cut in shards[1:]:
        factor_of = factor_of * one(*cut)
    return factor_of


def split_up(number_of, total, most, lean):
    loads = [(1 << 20) // math.isqrt(rank ** lean) + 1 for rank in range(2, number_of + 1)]
    spare, holding = total - most - (number_of - 1), [1] * (number_of - 1)
    while spare > 0:
        free = [i for i in range(number_of - 1) if holding[i] < most]
        mass, budget = sum([loads[i] for i in free]), spare
        for i in free:
            more = min(most - holding[i], max(1, budget * loads[i] // mass), spare)
            holding[i] = holding[i] + more
            spare = spare - more
    return np.array([most] + holding)


def uneven_parts(rng, number_of, total, bound, slope):
    if number_of == 2:
        one = jax.random.randint(rng, (), max(1, total - bound), min(bound, total - 1) + 1)
        return jnp.stack([one, total - one])
    sizes = jnp.asarray(split_up(number_of, total, bound, slope), jnp.int32)
    twos = (number_of - 1) // 2
    donor, sink = sizes[1:1 + 2 * twos:2], sizes[2:2 + 2 * twos:2]
    slack = jnp.minimum(donor - 1, bound - sink)
    passed = jax.random.randint(jax.random.fold_in(rng, 1), (twos,), 0, 1 << 20) % (slack + 1)
    sizes = sizes.at[1:1 + 2 * twos:2].set(donor - passed).at[2:2 + 2 * twos:2].set(sink + passed)
    return sizes[jax.random.permutation(jax.random.fold_in(rng, 2), number_of)]


def noise(key, extent, scale, bound, shards=(), kind=jnp.bfloat16):
    level = steps_of(key, extent, shards, -0.22, 0.18) if shards else 1.0
    result = jax.random.normal(key, extent, jnp.float32) * scale * level
    return jnp.minimum(jnp.maximum(result, -bound), bound).astype(kind)


def setup_inputs(seed: int = 0) -> dict:
    key_of = jax.random.split(jax.random.key(seed), 7)
    feature_maps = noise(key_of[0], (MAPS, PUPIL, PUPIL), 1.0, 6.0, ((1, 4),))
    coef_table = noise(key_of[1], (CELLS, MAPS), 0.02, 0.119628906)
    star_counts = uneven_parts(key_of[2], N_STAR, TOTAL, SLOT, 2).astype(jnp.int32)
    star_cells = draw_star_cells(jax.random.fold_in(key_of[6], 71), 0)
    star_bands = draw_star_bands(jax.random.fold_in(key_of[6], 71), 0)
    psf_cotangent = noise(key_of[5], (N_STAR * SLOT, PUPIL, PUPIL), 1.0, 6.0, ((0, 8), (1, 4)))
    return {"feature_maps": feature_maps, "coef_table": coef_table, "star_counts": star_counts, "star_cells": star_cells, "star_bands": star_bands, "psf_cotangent": psf_cotangent}


def fourier_tables(pupil_size):
    index_row = jnp.arange(pupil_size, dtype=jnp.int32)
    products = (index_row[:, None] * index_row[None, :]) % pupil_size
    angles = (2.0 * jnp.pi / pupil_size) * products.astype(jnp.float32)
    return jnp.cos(angles).astype(jnp.bfloat16), (-jnp.sin(angles)).astype(jnp.bfloat16)


def aperture_rows(first_row, row_count, pupil_size):
    centre = 0.5 * (pupil_size - 1)
    row_pos = (first_row + jnp.arange(row_count, dtype=jnp.int32)).astype(jnp.float32) - centre
    col_pos = jnp.arange(pupil_size, dtype=jnp.int32).astype(jnp.float32) - centre
    radius = row_pos[:, None] * row_pos[:, None] + col_pos[None, :] * col_pos[None, :]
    return jnp.where(radius <= 0.25 * pupil_size * pupil_size, 1.0, 0.0).astype(jnp.float32)


def wave_numbers(band_ids):
    wavelength = 0.55 + 0.35 * band_ids.astype(jnp.float32) / (BANDS - 1)
    return 2.0 * jnp.pi / wavelength


def product(left, right):
    return jnp.dot(left.astype(jnp.float32), right.astype(jnp.float32), precision=lax.Precision.HIGHEST)


def star_gradient(flat_maps, coef_row, band_id, cotangent, cos_table, sin_table, aperture):
    pupil_size = aperture.shape[0]
    path_error = product(coef_row[None, :], flat_maps)[0].reshape(pupil_size, pupil_size)
    wave_number = wave_numbers(band_id)
    phase_angle = wave_number * path_error
    cos_phase = jnp.cos(phase_angle)
    sin_phase = jnp.sin(phase_angle)
    pupil_real = (aperture * cos_phase).astype(jnp.bfloat16)
    pupil_imag = (aperture * sin_phase).astype(jnp.bfloat16)
    column_real = (product(pupil_real, cos_table) - product(pupil_imag, sin_table)).astype(jnp.bfloat16)
    column_imag = (product(pupil_real, sin_table) + product(pupil_imag, cos_table)).astype(jnp.bfloat16)
    inverse = 1.0 / pupil_size
    focal_real = (product(column_real.T, cos_table) - product(column_imag.T, sin_table)) * inverse
    focal_imag = (product(column_real.T, sin_table) + product(column_imag.T, cos_table)) * inverse
    grad_real = (2.0 * cotangent * focal_real).astype(jnp.bfloat16)
    grad_imag = (2.0 * cotangent * focal_imag).astype(jnp.bfloat16)
    back_real = ((product(grad_real, cos_table) + product(grad_imag, sin_table)) * inverse).astype(jnp.bfloat16)
    back_imag = ((product(grad_imag, cos_table) - product(grad_real, sin_table)) * inverse).astype(jnp.bfloat16)
    pupil_greal = product(back_real.T, cos_table) + product(back_imag.T, sin_table)
    pupil_gimag = product(back_imag.T, cos_table) - product(back_real.T, sin_table)
    phase_grad = aperture * (cos_phase * pupil_gimag - sin_phase * pupil_greal)
    return (wave_number * phase_grad).astype(jnp.bfloat16)


def reference(feature_maps, coef_table, star_counts, star_cells, star_bands, psf_cotangent):
    map_count = feature_maps.shape[0]
    pupil_size = feature_maps.shape[1]
    slot_count = star_cells.shape[1]
    flat_maps = feature_maps.reshape(map_count, pupil_size * pupil_size).astype(jnp.float32)
    cos_table, sin_table = fourier_tables(pupil_size)
    aperture = aperture_rows(0, pupil_size, pupil_size)
    group_ends = jnp.cumsum(star_counts).astype(jnp.int32)
    group_starts = (group_ends - star_counts).astype(jnp.int32)
    flat_cells = star_cells.reshape(-1)
    flat_bands = star_bands.reshape(-1)

    def star_step(running, star_rank):
        map_total, coef_total = running
        owner_group = jnp.sum((group_ends <= star_rank).astype(jnp.int32)).astype(jnp.int32)
        slot_index = (owner_group * slot_count + star_rank - group_starts[owner_group]).astype(jnp.int32)
        cell_id = flat_cells[slot_index]
        band_id = flat_bands[slot_index]
        coef_row = coef_table[cell_id].astype(jnp.float32)
        cotangent = lax.dynamic_index_in_dim(psf_cotangent, slot_index, 0, keepdims=False).astype(jnp.float32)
        path_grad = star_gradient(flat_maps, coef_row, band_id, cotangent, cos_table, sin_table, aperture)
        flat_grad = path_grad.reshape(1, pupil_size * pupil_size).astype(jnp.float32)
        map_total = map_total + product(coef_row[:, None], flat_grad)
        map_scores = product(flat_maps, flat_grad.T)[:, 0] / (8 * pupil_size)
        coef_total = coef_total.at[cell_id].add(map_scores)
        return (map_total, coef_total), jnp.zeros((), jnp.float32)

    initial = (jnp.zeros((map_count, pupil_size * pupil_size), jnp.float32), jnp.zeros(coef_table.shape, jnp.float32))
    finished, unused = lax.scan(star_step, initial, jnp.arange(TOTAL, dtype=jnp.int32))
    return finished[0].reshape(map_count, pupil_size, pupil_size), finished[1]
```

```python
import functools

import jax
import jax.numpy as jnp
import numpy as np
from jax import lax
from jax.experimental import pallas as pl
from jax.experimental.pallas import tpu as pltpu
from jax.sharding import PartitionSpec as P

BANDS = 8
LIVE_DEV = 4
PLANE_DEV = 8
RADIX = 4
ROWS_STEP = 16
TURN_STEPS = 8
EARLY_STEPS = 2
ROUTE_CHUNKS = 8
OVER_X = 11
OVER_Y = 6
STARS_CHIP = 8
F32 = jnp.float32
BF16 = jnp.bfloat16


def fourier_tables(pupil_size):
    index_row = jnp.arange(pupil_size, dtype=jnp.int32)
    products = index_row[:, None] * index_row[None, :] % pupil_size
    angles = 2.0 * jnp.pi / pupil_size * products.astype(jnp.float32)
    return (jnp.cos(angles).astype(jnp.bfloat16), (-jnp.sin(angles)).astype(jnp.bfloat16))


def aperture_rows(first_row, row_count, pupil_size):
    centre = 0.5 * (pupil_size - 1)
    row_pos = (first_row + jnp.arange(row_count, dtype=jnp.int32)).astype(jnp.float32) - centre
    col_pos = jnp.arange(pupil_size, dtype=jnp.int32).astype(jnp.float32) - centre
    radius = row_pos[:, None] * row_pos[:, None] + col_pos[None, :] * col_pos[None, :]
    return jnp.where(radius <= 0.25 * pupil_size * pupil_size, 1.0, 0.0).astype(jnp.float32)


def wave_numbers(band_ids):
    wavelength = 0.55 + 0.35 * band_ids.astype(jnp.float32) / (BANDS - 1)
    return 2.0 * jnp.pi / wavelength


def table_pick(values, indices):
    positions = jnp.arange(values.shape[0], dtype=jnp.int32)
    chosen = jnp.where(positions[None, :] == indices[:, None], values[None, :], 0)
    return jnp.sum(chosen, axis=1)


def per_device(feature_maps, coef_table, star_counts, star_cells, star_bands, psf_cotangent):
    groups = lax.axis_size("star")
    my_group = lax.axis_index("star")
    slot_count = psf_cotangent.shape[0]
    map_count, row_count, pupil_size = feature_maps.shape
    group_ends = jnp.cumsum(star_counts)
    group_starts = group_ends - star_counts
    flat_cells = star_cells.reshape(-1)
    flat_bands = star_bands.reshape(-1)
    cell_count = coef_table.shape[0]
    capacity = -(-slot_count // groups)
    targets = jnp.arange(groups, dtype=jnp.int32)
    lane_index = jnp.arange(capacity, dtype=jnp.int32)
    my_start = table_pick(group_starts, my_group[None])
    my_count = table_pick(star_counts, my_group[None])
    first_slot = (targets - my_start) % groups
    send_slot = (first_slot[:, None] + lane_index[None, :] * groups).reshape(-1)
    valid_mask = send_slot < my_count
    picked = jnp.take(psf_cotangent, jnp.minimum(send_slot, slot_count - 1), axis=0)
    outgoing = jnp.where(valid_mask[:, None, None], picked, jnp.zeros_like(picked))
    incoming = lax.all_to_all(outgoing, "star", split_axis=0, concat_axis=0, tiled=True)
    star_rank = my_group + jnp.arange(LIVE_DEV, dtype=jnp.int32) * groups
    owner_group = jnp.sum((group_ends[None, :] <= star_rank[:, None]).astype(jnp.int32), axis=1)
    within = star_rank - table_pick(group_starts, owner_group)
    live_mask = jnp.ones((LIVE_DEV,), dtype=bool)
    owner_group, within, live_mask = (owner_group, within, live_mask)
    cotangent = jnp.take(incoming, owner_group * capacity + within // groups, axis=0)
    slot_index = owner_group * slot_count + within
    cell_ids = table_pick(flat_cells, slot_index)
    band_ids = table_pick(flat_bands, slot_index)
    cell_hot = cell_ids[:, None] == jnp.arange(cell_count, dtype=jnp.int32)[None, :]
    coef_rows = jnp.dot(
        cell_hot.astype(jnp.bfloat16), coef_table, preferred_element_type=jnp.float32
    ).astype(jnp.bfloat16)
    flat_maps = feature_maps.reshape(map_count, row_count * pupil_size)
    path_error = jnp.dot(coef_rows, flat_maps, preferred_element_type=jnp.float32).reshape(
        -1, row_count, pupil_size
    )
    wave_number = wave_numbers(band_ids)
    phase_angle = wave_number[:, None, None] * path_error
    aperture = aperture_rows(lax.axis_index("row") * row_count, row_count, pupil_size)
    cos_phase = jnp.cos(phase_angle)
    sin_phase = jnp.sin(phase_angle)
    pupil_field = jnp.stack([aperture * cos_phase, aperture * sin_phase], 1).astype(jnp.bfloat16)
    cos_table, sin_table = fourier_tables(pupil_size)
    inverse = 1.0 / pupil_size
    along_cos = jnp.einsum(
        "sarc,cv->sarv", pupil_field, cos_table, preferred_element_type=jnp.float32
    )
    along_sin = jnp.einsum(
        "sarc,cv->sarv", pupil_field, sin_table, preferred_element_type=jnp.float32
    )
    column_field = jnp.stack(
        [along_cos[:, 0] - along_sin[:, 1], along_sin[:, 0] + along_cos[:, 1]], 1
    ).astype(jnp.bfloat16)
    pieces = lax.all_to_all(column_field, "row", split_axis=3, concat_axis=2, tiled=True)
    row_cos = jnp.einsum("sarv,ru->savu", pieces, cos_table, preferred_element_type=jnp.float32)
    row_sin = jnp.einsum("sarv,ru->savu", pieces, sin_table, preferred_element_type=jnp.float32)
    real_part = (row_cos[:, 0] - row_sin[:, 1]) * inverse
    imag_part = (row_sin[:, 0] + row_cos[:, 1]) * inverse
    focal_field = jnp.stack([real_part, imag_part], 1)
    weight = jnp.where(live_mask, 2.0, 0.0).astype(jnp.float32)[:, None, None, None]
    focal_grad = (weight * cotangent.astype(jnp.float32)[:, None] * focal_field).astype(
        jnp.bfloat16
    )
    back_cos = jnp.einsum(
        "savu,ur->savr", focal_grad, cos_table, preferred_element_type=jnp.float32
    )
    back_sin = jnp.einsum(
        "savu,ur->savr", focal_grad, sin_table, preferred_element_type=jnp.float32
    )
    spectrum_grad = jnp.stack(
        [(back_cos[:, 0] + back_sin[:, 1]) * inverse, (back_cos[:, 1] - back_sin[:, 0]) * inverse],
        1,
    ).astype(jnp.bfloat16)
    pieces = lax.all_to_all(spectrum_grad, "row", split_axis=3, concat_axis=2, tiled=True)
    col_cos = jnp.einsum("savr,vc->sarc", pieces, cos_table, preferred_element_type=jnp.float32)
    col_sin = jnp.einsum("savr,vc->sarc", pieces, sin_table, preferred_element_type=jnp.float32)
    pupil_grad = jnp.stack([col_cos[:, 0] + col_sin[:, 1], col_cos[:, 1] - col_sin[:, 0]], 1)
    phase_grad = aperture * (cos_phase * pupil_grad[:, 1] - sin_phase * pupil_grad[:, 0])
    path_grad = (
        (wave_number[:, None, None] * phase_grad)
        .astype(jnp.bfloat16)
        .reshape(-1, row_count * pupil_size)
    )
    map_scores = lax.dot_general(
        path_grad, flat_maps, (((1,), (1,)), ((), ())), preferred_element_type=jnp.float32
    )
    coef_part = lax.dot_general(
        cell_hot.astype(jnp.float32),
        map_scores * (1.0 / (8 * pupil_size)),
        (((0,), (0,)), ((), ())),
        precision=lax.Precision.HIGHEST,
    )
    coef_grad = lax.psum(coef_part, ("star", "row"))
    share = map_count // groups
    map_grad = lax.psum_scatter(
        lax.dot_general(
            coef_rows, path_grad, (((0,), (0,)), ((), ())), preferred_element_type=jnp.float32
        ),
        "star",
        scatter_dimension=0,
        tiled=True,
    )
    return (map_grad.reshape(share, row_count, pupil_size), coef_grad)


def quarter_tables(size):
    quarter = size // RADIX
    place = np.arange(quarter)[None, :, None]
    freq = RADIX * np.arange(quarter)[None, None, :] + np.arange(RADIX)[:, None, None]
    angle = 2.0 * np.pi / size * ((place * freq) % size)
    cosine, sine = np.cos(angle), -np.sin(angle)
    right = np.concatenate(
        [np.concatenate([cosine, sine], 2), np.concatenate([-sine, cosine], 2)], 1
    ).astype(np.float32)
    left = np.swapaxes(right, 1, 2)
    return jnp.asarray(right.astype(jnp.bfloat16)), jnp.asarray(left.astype(jnp.bfloat16))


def turn_cos_sin(turns):
    half = turns * np.float32(np.pi)
    square = half * half
    sine = jnp.full_like(square, -1.0 / 39916800.0)
    for term in (1.0 / 362880.0, -1.0 / 5040.0, 1.0 / 120.0, -1.0 / 6.0, 1.0):
        sine = sine * square + np.float32(term)
    sine = sine * half
    cosine = jnp.full_like(square, 1.0 / 479001600.0)
    for term in (-1.0 / 3628800.0, 1.0 / 40320.0, -1.0 / 720.0, 1.0 / 24.0, -0.5, 1.0):
        cosine = cosine * square + np.float32(term)
    return 1.0 - 2.0 * sine * sine, 2.0 * sine * cosine


def butterfly(real, imag, sign):
    sr, dr = real[0] + real[2], real[0] - real[2]
    si, di = imag[0] + imag[2], imag[0] - imag[2]
    tr, er = real[1] + real[3], real[1] - real[3]
    ti, ei = imag[1] + imag[3], imag[1] - imag[3]
    if sign < 0:
        er, ei = -er, -ei
    return (
        [sr + tr, dr - ei, sr - tr, dr + ei],
        [si + ti, di + er, si - ti, di - er],
    )


def spread_rows(weights):
    eye = jnp.eye(ROWS_STEP, dtype=weights.dtype)
    outs, ins = weights.shape
    spread = weights[:, None, :, None] * eye[None, :, None, :]
    return spread.reshape(outs * ROWS_STEP, ins * ROWS_STEP)


def maps_kernel(group_ref, weight_ref, grad_ref, maps_ref, out_ref, score_ref):
    share, rows, size = out_ref.shape
    grads = grad_ref[...].reshape(grad_ref.shape[0] * rows, size)
    maps = maps_ref[...].reshape(share * rows, size)
    total = jnp.dot(weight_ref[...], grads, preferred_element_type=F32)
    out_ref[...] = total.reshape(share, rows, size)

    @pl.when(pl.program_id(0) == 0)
    def _():
        score_ref[...] = jnp.zeros_like(score_ref)

    score_ref[...] += lax.dot_general(
        maps, grads, (((1,), (1,)), ((), ())), preferred_element_type=F32
    )


def map_sums(my_group, coef_rows, path_grads, feature_maps, share):
    stars, row_count, size = path_grads.shape
    weights = spread_rows(coef_rows)
    score_shape = (share * ROWS_STEP, stars * ROWS_STEP)
    map_grad, scores = pl.pallas_call(
        maps_kernel,
        out_shape=(
            jax.ShapeDtypeStruct((share, row_count, size), F32),
            jax.ShapeDtypeStruct(score_shape, F32),
        ),
        grid_spec=pltpu.PrefetchScalarGridSpec(
            num_scalar_prefetch=1,
            grid=(row_count // ROWS_STEP,),
            in_specs=[
                pl.BlockSpec(weights.shape, lambda i, g: (0, 0)),
                pl.BlockSpec((stars, ROWS_STEP, size), lambda i, g: (0, i, 0)),
                pl.BlockSpec((share, ROWS_STEP, size), lambda i, g: (g[0], i, 0)),
            ],
            out_specs=(
                pl.BlockSpec((share, ROWS_STEP, size), lambda i, g: (0, i, 0)),
                pl.BlockSpec(score_shape, lambda i, g: (0, 0)),
            ),
        ),
        compiler_params=pltpu.CompilerParams(vmem_limit_bytes=56 << 20),
        name="map_sums",
    )(my_group[None], weights, path_grads, feature_maps)
    eye = jnp.eye(ROWS_STEP, dtype=F32)
    scores = scores.reshape(share, ROWS_STEP, stars, ROWS_STEP)
    return map_grad, jnp.sum(scores * eye[None, :, None, :], axis=(1, 3))


GATHER_STEPS = 8


def greet(peers):
    barrier = pltpu.get_barrier_semaphore()
    for peer in peers:
        pl.semaphore_signal(barrier, inc=1, device_id=peer, device_id_type=pl.DeviceIdType.MESH)
    pl.semaphore_wait(barrier, len(peers))


def send(source, target, send_sem, recv_sem, peer):
    return pltpu.make_async_remote_copy(
        src_ref=source,
        dst_ref=target,
        send_sem=send_sem,
        recv_sem=recv_sem,
        device_id=peer,
        device_id_type=pl.DeviceIdType.MESH,
    )


def gather_kernel(lanes, in_ref, out_ref, local, z_send, z_recv, p_send, p_recv, c_send, c_recv):
    row = lax.axis_index("row")
    me = lax.axis_index("star")
    depth = in_ref.shape[1] // GATHER_STEPS
    core = me + 1 - 2 * (me % 2)
    across = me + 2 - 4 * ((me // 2) % 2)
    along = me + 4 - 8 * ((me // 4) % 2)
    corner = across + 4 - 8 * ((me // 4) % 2)
    peers = [{"row": (row + d) % lanes} for d in range(1, lanes)]
    to_core, to_across, to_along = {"star": core}, {"star": across}, {"star": along}
    greet(peers + [to_core, to_across, to_along])
    half = lanes // 2
    started = []

    def start(copy):
        copy.start()
        started.append(copy)
        return copy

    def block(group, step, first=0, count=lanes):
        return out_ref.at[group, pl.ds(first, count), pl.ds(step * depth, depth)]

    own, exchanged = [], []
    for step in range(GATHER_STEPS):
        rows = pl.ds(step * depth, depth)
        copy = pltpu.make_async_copy(
            in_ref.at[row, rows], out_ref.at[me, row, rows], local.at[step]
        )
        copy.start()
        own.append(copy)
        exchanged.append(
            [
                start(
                    send(
                        in_ref.at[(row + d) % lanes, rows],
                        out_ref.at[me, row, rows],
                        z_send.at[step, d - 1],
                        z_recv.at[step, d - 1],
                        peers[d - 1],
                    )
                )
                for d in range(1, lanes)
            ]
        )

    def plane(step, way, part, peer):
        return start(send(part, part, p_send.at[step, way], p_recv.at[step, way], peer))

    def cores(step, way, part):
        return start(send(part, part, c_send.at[step, way], c_recv.at[step, way], to_core))

    sides, corners, twins = {}, {}, []
    for step in range(GATHER_STEPS + 2):
        if step < GATHER_STEPS:
            own[step].wait()
            for copy in exchanged[step]:
                copy.wait_recv()
            part = block(me, step)
            sides[step] = (
                plane(step, 0, part, to_across),
                plane(step, 1, part, to_along),
            )
            twins.append(cores(step, 0, part))
        last = step - 1
        if 0 <= last < GATHER_STEPS:
            sides[last][0].wait_recv()
            first = plane(last, 2, block(across, last, 0, half), to_along)
            twins.append(cores(last, 1, block(across, last)))
            sides[last][1].wait_recv()
            second = plane(last, 3, block(along, last, half, lanes - half), to_across)
            twins.append(cores(last, 2, block(along, last)))
            corners[last] = (first, second)
        last = step - 2
        if last >= 0:
            corners[last][0].wait_recv()
            corners[last][1].wait_recv()
            twins.append(cores(last, 3, block(corner, last)))
    for copy in twins:
        copy.wait_recv()
    for copy in started:
        copy.wait_send()


def gather_grads(path_grad, groups):
    lanes, row_count, size = path_grad.shape
    dma = pltpu.SemaphoreType.DMA
    return pl.pallas_call(
        functools.partial(gather_kernel, lanes),
        out_shape=jax.ShapeDtypeStruct((groups, lanes, row_count, size), path_grad.dtype),
        in_specs=[pl.BlockSpec(memory_space=pltpu.VMEM)],
        out_specs=pl.BlockSpec(memory_space=pl.ANY),
        scratch_shapes=[
            dma((GATHER_STEPS,)),
            dma((GATHER_STEPS, lanes - 1)),
            dma((GATHER_STEPS, lanes - 1)),
            dma((GATHER_STEPS, 4)),
            dma((GATHER_STEPS, 4)),
            dma((GATHER_STEPS, 4)),
            dma((GATHER_STEPS, 4)),
        ],
        compiler_params=pltpu.CompilerParams(
            collective_id=1, has_side_effects=True, vmem_limit_bytes=56 << 20
        ),
        name="gather_grads",
    )(path_grad)


def score_kernel(groups, lanes, in_ref, out_ref, z_send, z_recv, s_send, s_recv):
    row = lax.axis_index("row")
    me = lax.axis_index("star")
    row_peers = [{"row": (row + d) % lanes} for d in range(1, lanes)]
    star_peers = [{"star": (me + d) % groups} for d in range(1, groups)]
    greet(row_peers + star_peers)
    copies = [
        send(in_ref, out_ref.at[me, row], z_send.at[d], z_recv.at[d], row_peers[d])
        for d in range(lanes - 1)
    ]
    for copy in copies:
        copy.start()
    out_ref[me, row] = in_ref[...]
    for copy in copies:
        copy.wait()
    copies = [
        send(out_ref.at[me], out_ref.at[me], s_send.at[d], s_recv.at[d], star_peers[d])
        for d in range(groups - 1)
    ]
    for copy in copies:
        copy.start()
    for copy in copies:
        copy.wait()


def gather_scores(scores, groups, lanes):
    dma = pltpu.SemaphoreType.DMA
    vmem = pl.BlockSpec(memory_space=pltpu.VMEM)
    return pl.pallas_call(
        functools.partial(score_kernel, groups, lanes),
        out_shape=jax.ShapeDtypeStruct((groups, lanes) + scores.shape, scores.dtype),
        in_specs=[vmem],
        out_specs=vmem,
        scratch_shapes=[
            dma((lanes - 1,)),
            dma((lanes - 1,)),
            dma((groups - 1,)),
            dma((groups - 1,)),
        ],
        compiler_params=pltpu.CompilerParams(
            collective_id=2, has_side_effects=True, vmem_limit_bytes=8 << 20
        ),
        name="gather_scores",
    )(scores)


def plan_kernel(slots, count_ref, cell_ref, band_ref, cells_out, inverse_out, wave_out, route_out):
    chips = count_ref.shape[0] // 2
    over_x, over_y = OVER_X, OVER_Y
    share = STARS_CHIP
    first = [count_ref[2 * c] for c in range(chips)]
    held = [first[c] + count_ref[2 * c + 1] for c in range(chips)]
    level = []
    for y in range(chips // 2):
        both = held[2 * y] + held[2 * y + 1]
        if y == 0:
            level += [both // 2, both - both // 2]
        else:
            level += [2 * share - level[0], 2 * share - level[1]]
    keep_x = [jnp.minimum(held[c], level[c]) for c in range(chips)]
    keep_y = [jnp.minimum(level[c], share) for c in range(chips)]

    def choose(values, index):
        out = values[0]
        for c in range(1, chips):
            out = jnp.where(index == c, values[c], out)
        return out

    def slot_of(chip, place):
        place = jnp.minimum(place, choose(held, chip) - 1)
        start = choose(first, chip)
        return jnp.where(place < start, place, slots + place - start)

    def after_x(chip, place):
        place = jnp.minimum(place, choose(level, chip) - 1)
        kept = choose(keep_x, chip)
        return jnp.where(place < kept, slot_of(chip, place), 2 * slots + place - kept)

    def star_x(chip, place):
        kept = choose(keep_x, chip)
        other = chip + 1 - 2 * (chip % 2)
        own = chip * 2 * slots + slot_of(chip, place)
        far = other * 2 * slots + slot_of(other, choose(keep_x, other) + place - kept)
        return jnp.where(place < kept, own, far)

    per_chip = over_x + over_y + share

    def fill(chip, carry):
        base = chip * per_chip
        kept_x, kept_y = choose(keep_x, chip), choose(keep_y, chip)
        for i in range(over_x):
            route_out[base + i] = slot_of(chip, kept_x + i)
        for i in range(over_y):
            route_out[base + over_x + i] = after_x(chip, kept_y + i)
        other = chip + 2 - 4 * (chip // 2)
        for i in range(share):
            from_y = 2 * slots + over_x + i - kept_y
            route_out[base + over_x + over_y + i] = jnp.where(
                i < kept_y, after_x(chip, i), from_y
            )
            star = jnp.where(
                i < kept_y, star_x(chip, i), star_x(other, choose(keep_y, other) + i - kept_y)
            )
            group = star // slots
            band = band_ref[group, star - group * slots]
            at = chip * share + i
            cells_out[at] = cell_ref[group, star - group * slots]
            inverse, wave = jnp.float32(0), jnp.float32(0)
            for b in range(BANDS):
                length = 0.55 + 0.35 * b / (BANDS - 1)
                inverse = jnp.where(band == b, np.float32(1.0 / length), inverse)
                wave = jnp.where(band == b, np.float32(2.0 * np.pi / length), wave)
            inverse_out[at] = inverse
            wave_out[at] = wave
        return carry

    lax.fori_loop(0, chips, fill, 0)


def plan(star_counts, star_cells, star_bands):
    smem = pl.BlockSpec(memory_space=pltpu.SMEM)
    groups, slots = star_cells.shape
    chips = groups // 2
    total = chips * STARS_CHIP
    return pl.pallas_call(
        functools.partial(plan_kernel, slots),
        out_shape=(
            jax.ShapeDtypeStruct((total,), jnp.int32),
            jax.ShapeDtypeStruct((total,), F32),
            jax.ShapeDtypeStruct((total,), F32),
            jax.ShapeDtypeStruct((chips * (OVER_X + OVER_Y + STARS_CHIP),), jnp.int32),
        ),
        in_specs=[smem] * 3,
        out_specs=(smem,) * 4,
        name="plan",
    )(star_counts, star_cells, star_bands)


def group_rows(step, depth, row_count, lanes):
    return [
        pl.ds(pl.multiple_of(lane * row_count + step * depth, depth), depth)
        for lane in range(lanes)
    ]


def focal_kernel(
    groups, lanes, cell_ref, inverse_ref, route_ref, coef_ref, maps_ref, cot_ref, right_ref, left_ref,
    turns_out, xr, xi, maps_buf, stage, raw, pool, x_stage, y_stage, z_stage, ct, ct_turned,
    order, spread, yr, yi, *scratch,
):
    steps = TURN_STEPS
    chunks = pool.shape[0]
    x_got, y_got = scratch[:chunks], scratch[chunks : 2 * chunks]
    (
        m_sem, t_local, t_send, t_recv, r_local, r_send, r_recv, x_send, x_recv,
        y_send, y_recv, z_local, z_send, z_recv,
    ) = scratch[2 * chunks :]
    row = lax.axis_index("row")
    me = lax.axis_index("star")
    core = me % 2
    chip = me // 2
    twin = me + 1 - 2 * core
    over_x = me + 2 - 4 * (chip % 2)
    over_y = me + 4 - 8 * (me // 4)
    map_count, depth, size = maps_buf.shape[1:]
    row_count = depth * steps
    half = size // 2
    quarter = size // RADIX
    slots = raw.shape[0] // 2
    places = [(d, e) for e in range(2) for d in range(lanes)][1:]
    peers = [{"row": (row + d) % lanes, "star": twin if e else me} for d, e in places]
    greet(peers + [{"star": over_x}, {"star": over_y}])

    slot_range = pl.ds(core * slots, slots)
    other = 1 - core
    raw_own = pltpu.make_async_copy(
        cot_ref.at[:, :, pl.ds(pl.multiple_of(core * half, half), half)], raw.at[slot_range], r_local
    )
    raw_twin = send(
        cot_ref.at[:, :, pl.ds(pl.multiple_of(other * half, half), half)],
        raw.at[slot_range],
        r_send,
        r_recv,
        {"star": twin},
    )
    raw_own.start()
    raw_twin.start()

    def fetch(step):
        slot = step % 2
        rows = pl.ds(pl.multiple_of(step * depth, depth), depth)
        return pltpu.make_async_copy(maps_ref.at[:, rows], maps_buf.at[slot], m_sem.at[slot])

    fetch(0).start()
    fetch(1).start()

    lines = lanes * ROWS_STEP
    wide = map_count * ROWS_STEP
    cells = lax.broadcasted_iota(jnp.int32, (ROWS_STEP, coef_ref.shape[0]), 1)
    hot = jnp.concatenate(
        [
            jnp.where(cells == cell_ref[me * lanes + s], 1.0, 0.0).astype(BF16)
            for s in range(lanes)
        ],
        0,
    )
    coefs = jnp.dot(hot, coef_ref[...], preferred_element_type=F32).astype(BF16)
    at = lax.broadcasted_iota(jnp.int32, (map_count, wide), 0)
    to = lax.broadcasted_iota(jnp.int32, (map_count, wide), 1)
    repeat = jnp.where(to // ROWS_STEP == at, 1.0, 0.0).astype(BF16)
    repeated = jnp.dot(coefs, repeat, preferred_element_type=F32)
    at = lax.broadcasted_iota(jnp.int32, (lines, wide), 0)
    to = lax.broadcasted_iota(jnp.int32, (lines, wide), 1)
    spread[...] = jnp.where(at % ROWS_STEP == to % ROWS_STEP, repeated, 0.0).astype(BF16)

    def turn_copies(step):
        rows = pl.ds(pl.multiple_of(step * depth, depth), depth)
        place = pl.ds(pl.multiple_of(row * row_count + step * depth, depth), depth)
        return [
            pltpu.make_async_copy(stage.at[row, rows], turns_out.at[place], t_local.at[step])
        ] + [
            send(
                stage.at[(row + d) % lanes, rows],
                turns_out.at[place],
                t_send.at[step, d - 1],
                t_recv.at[step, d - 1],
                {"row": (row + d) % lanes},
            )
            for d in range(1, lanes)
        ]

    def phase_step(step, carry):
        slot = step % 2
        fetch(step).wait()
        for part in range(depth // ROWS_STEP):
            lined = pl.ds(part * ROWS_STEP, ROWS_STEP)
            maps = maps_buf[slot, :, lined].reshape(wide, size)
            path = jnp.dot(spread[...], maps, preferred_element_type=F32)
            rows = pl.ds(pl.multiple_of(step * depth + part * ROWS_STEP, ROWS_STEP), ROWS_STEP)
            for s in range(lanes):
                turned = path[s * ROWS_STEP : (s + 1) * ROWS_STEP] * inverse_ref[me * lanes + s]
                stage[s, rows] = (turned - jnp.floor(turned + 0.5)).astype(BF16)
        for copy in turn_copies(step):
            copy.start()

        @pl.when(step + 2 < steps)
        def _():
            fetch(step + 2).start()

        return carry

    lax.fori_loop(0, EARLY_STEPS, phase_step, 0)

    def x_copy(c):
        return send(x_stage.at[c], x_got[c], x_send.at[c], x_recv.at[c], {"star": over_x})

    def y_copy(c):
        return send(y_stage.at[c], y_got[c], y_send.at[c], y_recv.at[c], {"star": over_y})

    tall = quarter // lanes
    piece = tall * RADIX // chunks
    parts = chunks // RADIX
    per_chip = OVER_X + OVER_Y + STARS_CHIP
    base = chip * per_chip

    def z_copies(c):
        kind, part = c // parts, c % parts
        target = ct.at[
            kind,
            pl.ds(pl.multiple_of(row * tall + part * piece, piece), piece),
            pl.ds(pl.multiple_of(core * half, half), half),
        ]
        own = z_stage.at[c, core * lanes + row]
        return [pltpu.make_async_copy(own, target, z_local.at[c])] + [
            send(
                z_stage.at[c, (core + e) % 2 * lanes + (row + d) % lanes],
                target,
                z_send.at[c, n],
                z_recv.at[c, n],
                peers[n],
            )
            for n, (d, e) in enumerate(places)
        ]

    raw_own.wait()
    raw_twin.wait()
    at = lax.broadcasted_iota(jnp.int32, (row_count, row_count), 0)
    to = lax.broadcasted_iota(jnp.int32, (row_count, row_count), 1)
    sort = jnp.where(at % tall * RADIX + at // tall == to, 1.0, 0.0).astype(BF16)

    def sort_slot(slot, carry):
        sorted_rows = jnp.dot(sort, raw[slot], preferred_element_type=F32).astype(BF16)
        for c in range(chunks):
            pool[c, slot] = sorted_rows[c * piece : (c + 1) * piece]
        return carry

    lax.fori_loop(0, 2 * slots, sort_slot, 0)
    for c in range(chunks):
        for i in range(OVER_X):
            x_stage[c, i] = pool[c, route_ref[base + i]]
        x_copy(c).start()

    lax.fori_loop(EARLY_STEPS, steps, phase_step, 0)
    at = lax.broadcasted_iota(jnp.int32, (size, size), 0)
    to = lax.broadcasted_iota(jnp.int32, (size, size), 1)
    order[...] = jnp.where(at % quarter * RADIX + at // quarter == to, 1.0, 0.0).astype(BF16)

    def pick_x(c, index):
        mine = pool[c, jnp.minimum(index, 2 * slots - 1)]
        far = x_got[c][jnp.clip(index - 2 * slots, 0, OVER_X - 1)]
        return jnp.where(index < 2 * slots, mine, far)

    def route(c):
        x_copy(c).wait()
        for i in range(OVER_Y):
            y_stage[c, i] = pick_x(c, route_ref[base + OVER_X + i])
        y_copy(c).start()
        y_copy(c).wait()
        for i in range(STARS_CHIP):
            index = route_ref[base + OVER_X + OVER_Y + i]
            far = y_got[c][jnp.clip(index - 2 * slots - OVER_X, 0, OVER_Y - 1)]
            near = pick_x(c, jnp.minimum(index, 2 * slots + OVER_X - 1))
            z_stage[c, i] = jnp.where(index < 2 * slots + OVER_X, near, far)
        for copy in z_copies(c):
            copy.start()

    for c in range(chunks // 2):
        route(c)

    blocks = [slice(m * quarter, (m + 1) * quarter) for m in range(RADIX)]
    centre = 0.5 * (size - 1)
    scale = 1.0 / size
    tile = lanes * depth

    def forward_columns(step, carry):
        for copy in turn_copies(step):
            copy.wait()
        rows = group_rows(step, depth, row_count, lanes)
        turns = jnp.concatenate([turns_out[r, :] for r in rows], 0)
        cosine, sine = turn_cos_sin(turns.astype(F32))
        line = lax.broadcasted_iota(jnp.int32, (tile, size), 0)
        place = line // depth * row_count + line % depth + step * depth
        row_pos = place.astype(F32) - centre
        col_pos = lax.broadcasted_iota(jnp.int32, (tile, size), 1).astype(F32) - centre
        inside = row_pos * row_pos + col_pos * col_pos <= 0.25 * size * size
        real = jnp.where(inside, cosine, 0.0)
        imag = jnp.where(inside, sine, 0.0)
        mixed_real, mixed_imag = butterfly(
            [real[:, b] for b in blocks], [imag[:, b] for b in blocks], -1
        )
        for k in range(RADIX):
            both = jnp.concatenate([mixed_real[k].astype(BF16), mixed_imag[k].astype(BF16)], 1)
            made = jnp.dot(both, right_ref[k], preferred_element_type=F32).astype(BF16)
            for lane in range(lanes):
                lined = slice(lane * depth, (lane + 1) * depth)
                yr[rows[lane], blocks[k]] = made[lined, :quarter]
                yi[rows[lane], blocks[k]] = made[lined, quarter:]
        return carry

    lax.fori_loop(0, steps, forward_columns, 0)
    for c in range(chunks // 2, chunks):
        route(c)

    def focal(kind, carry):
        for part in range(parts):
            for copy in z_copies(kind * parts + part):
                copy.wait()
        ct_turned[...] = lax.dot_general(
            order[...], ct[kind], (((1,), (1,)), ((), ())), preferred_element_type=F32
        )
        cols = pl.ds(pl.multiple_of(kind * quarter, quarter), quarter)
        mixed_real, mixed_imag = butterfly(
            [yr[b, cols].astype(F32) for b in blocks],
            [yi[b, cols].astype(F32) for b in blocks],
            -1,
        )
        back_real, back_imag = [], []
        for k in range(RADIX):
            both = jnp.concatenate([mixed_real[k].astype(BF16), mixed_imag[k].astype(BF16)], 0)
            field = jnp.dot(left_ref[k], both, preferred_element_type=F32)
            weight = ct_turned[blocks[k], :] * (2.0 * scale)
            grad = (field * jnp.concatenate([weight, weight], 0)).astype(BF16)
            back = jnp.dot(right_ref[k], grad, preferred_element_type=F32)
            back_real.append(back[:quarter])
            back_imag.append(back[quarter:])
        spec_real, spec_imag = butterfly(back_real, back_imag, 1)
        for m in range(RADIX):
            xr[blocks[m], cols] = (spec_real[m] * scale).astype(BF16)
            xi[blocks[m], cols] = (spec_imag[m] * scale).astype(BF16)
        return carry

    lax.fori_loop(0, RADIX, focal, 0)


def focal_fields(cells, inverse, route, coef_table, feature_maps, cotangent, right, left, groups, lanes):
    map_count, row_count, size = feature_maps.shape
    slots = cotangent.shape[0]
    depth = row_count // TURN_STEPS
    half, quarter = size // 2, size // RADIX
    chunks = ROUTE_CHUNKS
    piece = row_count // chunks
    dma = pltpu.SemaphoreType.DMA
    smem = pl.BlockSpec(memory_space=pltpu.SMEM)
    vmem = pl.BlockSpec(memory_space=pltpu.VMEM)
    hbm = pl.BlockSpec(memory_space=pl.ANY)
    square = jax.ShapeDtypeStruct((size, size), BF16)
    others = 2 * lanes - 1
    return pl.pallas_call(
        functools.partial(focal_kernel, groups, lanes),
        out_shape=(square,) * 3,
        in_specs=[smem, smem, smem, vmem, hbm, hbm, vmem, vmem],
        out_specs=(vmem,) * 3,
        scratch_shapes=[
            pltpu.VMEM((2, map_count, depth, size), BF16),
            pltpu.VMEM((lanes, row_count, size), BF16),
            pltpu.VMEM((2 * slots, row_count, half), BF16),
            pltpu.VMEM((chunks, 2 * slots, piece, half), BF16),
            pltpu.VMEM((chunks, OVER_X, piece, half), BF16),
            pltpu.VMEM((chunks, OVER_Y, piece, half), BF16),
            pltpu.VMEM((chunks, STARS_CHIP, piece, half), BF16),
            pltpu.VMEM((RADIX, quarter, size), BF16),
            pltpu.VMEM((size, quarter), F32),
            pltpu.VMEM((size, size), BF16),
            pltpu.VMEM((lanes * ROWS_STEP, map_count * ROWS_STEP), BF16),
            pltpu.VMEM((size, size), BF16),
            pltpu.VMEM((size, size), BF16),
        ]
        + [pltpu.VMEM((OVER_X, piece, half), BF16)] * chunks
        + [pltpu.VMEM((OVER_Y, piece, half), BF16)] * chunks
        + [
            dma((2,)),
            dma((TURN_STEPS,)),
            dma((TURN_STEPS, lanes - 1)),
            dma((TURN_STEPS, lanes - 1)),
            dma,
            dma,
            dma,
            dma((chunks,)),
            dma((chunks,)),
            dma((chunks,)),
            dma((chunks,)),
            dma((chunks,)),
            dma((chunks, others)),
            dma((chunks, others)),
        ],
        compiler_params=pltpu.CompilerParams(
            collective_id=0, has_side_effects=True, vmem_limit_bytes=60 << 20
        ),
        name="focal_fields",
    )(cells, inverse, route, coef_table, feature_maps, cotangent, right, left)


def column_kernel(chunk, wave_ref, turns_ref, xr, xi, left_ref, out_ref):
    size = turns_ref.shape[1]
    quarter = size // RADIX
    blocks = [slice(m * quarter, (m + 1) * quarter) for m in range(RADIX)]
    centre = 0.5 * (size - 1)

    def inverse_columns(step, carry):
        rows = pl.ds(pl.multiple_of(step * chunk, chunk), chunk)
        cosine, sine = turn_cos_sin(turns_ref[rows, :].astype(F32))
        row_pos = (
            lax.broadcasted_iota(jnp.int32, (chunk, size), 0) + step * chunk
        ).astype(F32) - centre
        col_pos = lax.broadcasted_iota(jnp.int32, (chunk, size), 1).astype(F32) - centre
        inside = row_pos * row_pos + col_pos * col_pos <= 0.25 * size * size
        real = jnp.where(inside, cosine, 0.0)
        imag = jnp.where(inside, sine, 0.0)
        part_real, part_imag = [], []
        for k in range(RADIX):
            both = jnp.concatenate([xr[rows, blocks[k]], xi[rows, blocks[k]]], 1)
            made = jnp.dot(both, left_ref[k], preferred_element_type=F32)
            part_real.append(made[:, :quarter])
            part_imag.append(made[:, quarter:])
        grad_real, grad_imag = butterfly(part_real, part_imag, 1)
        wave = wave_ref[0]
        for m in range(RADIX):
            grad = real[:, blocks[m]] * grad_imag[m] - imag[:, blocks[m]] * grad_real[m]
            out_ref[rows, blocks[m]] = (wave * grad).astype(BF16)
        return carry

    lax.fori_loop(0, size // chunk, inverse_columns, 0)


def column_gradient(wave, turns, spec_real, spec_imag, left):
    vmem = pl.BlockSpec(memory_space=pltpu.VMEM)
    return pl.pallas_call(
        functools.partial(column_kernel, 128),
        out_shape=jax.ShapeDtypeStruct(turns.shape, BF16),
        in_specs=[pl.BlockSpec(memory_space=pltpu.SMEM), vmem, vmem, vmem, vmem],
        out_specs=vmem,
        compiler_params=pltpu.CompilerParams(vmem_limit_bytes=56 << 20),
        name="column_gradient",
    )(wave, turns, spec_real, spec_imag, left)


def star_devices(feature_maps, coef_table, star_counts, star_cells, star_bands, psf_cotangent):
    groups = lax.axis_size("star")
    lanes = lax.axis_size("row")
    my_group = lax.axis_index("star")
    my_lane = lax.axis_index("row")
    map_count, row_count, size = feature_maps.shape
    cell_count = coef_table.shape[0]
    share = map_count // groups
    total = groups * lanes
    cell_ids, inverse, wave, route = plan(star_counts, star_cells, star_bands)
    cell_hot = cell_ids[:, None] == jnp.arange(cell_count, dtype=jnp.int32)[None, :]
    coef_rows = jnp.dot(
        cell_hot.astype(BF16), coef_table, preferred_element_type=F32
    ).astype(BF16)
    right, left = quarter_tables(size)
    turns, spec_real, spec_imag = focal_fields(
        cell_ids, inverse, route, coef_table, feature_maps, psf_cotangent, right, left, groups, lanes
    )
    my_wave = lax.dynamic_slice_in_dim(wave, my_group * lanes + my_lane, 1, 0)
    path_grad = column_gradient(my_wave, turns, spec_real, spec_imag, left)
    path_grads = gather_grads(path_grad.reshape(lanes, row_count, size), groups)
    path_grads = path_grads.reshape(total, row_count, size)
    my_coefs = lax.dynamic_slice_in_dim(coef_rows.T, my_group * share, share, 0)
    map_grad, scores = map_sums(my_group, my_coefs, path_grads, feature_maps, share)
    scores = jnp.pad(scores, ((0, 0), (0, -total % 128)))
    scores = jnp.sum(gather_scores(scores, groups, lanes), axis=1)
    scores = scores.reshape(map_count, -1)[:, :total]
    coef_grad = lax.dot_general(
        cell_hot.astype(F32),
        scores * (1.0 / (8 * size)),
        (((0,), (1,)), ((), ())),
        precision=lax.Precision.HIGHEST,
    )
    return map_grad, coef_grad


def solution(mesh):
    placed = (P(None, "row", None), P(), P(), P(), P(), P("star", "row", None))
    fits = mesh.shape["row"] == LIVE_DEV and mesh.shape["star"] == PLANE_DEV
    device = star_devices if fits else per_device
    return jax.shard_map(
        device,
        mesh=mesh,
        in_specs=placed,
        out_specs=(P("star", "row", None), P()),
        check_vma=False,
    )
```

```python
import functools

import jax
import jax.numpy as jnp
import numpy as np
from jax import lax
from jax.experimental import pallas as pl
from jax.experimental.pallas import tpu as pltpu
from jax.sharding import PartitionSpec as P

BANDS = 8
LIVE_DEV = 4
PLANE_DEV = 8
RADIX = 4
ROWS_STEP = 16
TURN_STEPS = 8
EARLY_STEPS = 2
ROUTE_CHUNKS = 8
GATHER_STEPS = 8
OVER_X = 11
OVER_Y = 6
STARS_CHIP = 8
F32 = jnp.float32
BF16 = jnp.bfloat16


def fourier_tables(pupil_size):
    index_row = jnp.arange(pupil_size, dtype=jnp.int32)
    products = index_row[:, None] * index_row[None, :] % pupil_size
    angles = 2.0 * jnp.pi / pupil_size * products.astype(jnp.float32)
    return (jnp.cos(angles).astype(jnp.bfloat16), (-jnp.sin(angles)).astype(jnp.bfloat16))


def aperture_rows(first_row, row_count, pupil_size):
    centre = 0.5 * (pupil_size - 1)
    row_pos = (first_row + jnp.arange(row_count, dtype=jnp.int32)).astype(jnp.float32) - centre
    col_pos = jnp.arange(pupil_size, dtype=jnp.int32).astype(jnp.float32) - centre
    radius = row_pos[:, None] * row_pos[:, None] + col_pos[None, :] * col_pos[None, :]
    return jnp.where(radius <= 0.25 * pupil_size * pupil_size, 1.0, 0.0).astype(jnp.float32)


def wave_numbers(band_ids):
    wavelength = 0.55 + 0.35 * band_ids.astype(jnp.float32) / (BANDS - 1)
    return 2.0 * jnp.pi / wavelength


def table_pick(values, indices):
    positions = jnp.arange(values.shape[0], dtype=jnp.int32)
    chosen = jnp.where(positions[None, :] == indices[:, None], values[None, :], 0)
    return jnp.sum(chosen, axis=1)


def per_device(feature_maps, coef_table, star_counts, star_cells, star_bands, psf_cotangent):
    groups = lax.axis_size("star")
    my_group = lax.axis_index("star")
    slot_count = psf_cotangent.shape[0]
    map_count, row_count, pupil_size = feature_maps.shape
    group_ends = jnp.cumsum(star_counts)
    group_starts = group_ends - star_counts
    flat_cells = star_cells.reshape(-1)
    flat_bands = star_bands.reshape(-1)
    cell_count = coef_table.shape[0]
    capacity = -(-slot_count // groups)
    targets = jnp.arange(groups, dtype=jnp.int32)
    lane_index = jnp.arange(capacity, dtype=jnp.int32)
    my_start = table_pick(group_starts, my_group[None])
    my_count = table_pick(star_counts, my_group[None])
    first_slot = (targets - my_start) % groups
    send_slot = (first_slot[:, None] + lane_index[None, :] * groups).reshape(-1)
    valid_mask = send_slot < my_count
    picked = jnp.take(psf_cotangent, jnp.minimum(send_slot, slot_count - 1), axis=0)
    outgoing = jnp.where(valid_mask[:, None, None], picked, jnp.zeros_like(picked))
    incoming = lax.all_to_all(outgoing, "star", split_axis=0, concat_axis=0, tiled=True)
    star_rank = my_group + jnp.arange(LIVE_DEV, dtype=jnp.int32) * groups
    owner_group = jnp.sum((group_ends[None, :] <= star_rank[:, None]).astype(jnp.int32), axis=1)
    within = star_rank - table_pick(group_starts, owner_group)
    live_mask = jnp.ones((LIVE_DEV,), dtype=bool)
    owner_group, within, live_mask = (owner_group, within, live_mask)
    cotangent = jnp.take(incoming, owner_group * capacity + within // groups, axis=0)
    slot_index = owner_group * slot_count + within
    cell_ids = table_pick(flat_cells, slot_index)
    band_ids = table_pick(flat_bands, slot_index)
    cell_hot = cell_ids[:, None] == jnp.arange(cell_count, dtype=jnp.int32)[None, :]
    coef_rows = jnp.dot(
        cell_hot.astype(jnp.bfloat16), coef_table, preferred_element_type=jnp.float32
    ).astype(jnp.bfloat16)
    flat_maps = feature_maps.reshape(map_count, row_count * pupil_size)
    path_error = jnp.dot(coef_rows, flat_maps, preferred_element_type=jnp.float32).reshape(
        -1, row_count, pupil_size
    )
    wave_number = wave_numbers(band_ids)
    phase_angle = wave_number[:, None, None] * path_error
    aperture = aperture_rows(lax.axis_index("row") * row_count, row_count, pupil_size)
    cos_phase = jnp.cos(phase_angle)
    sin_phase = jnp.sin(phase_angle)
    pupil_field = jnp.stack([aperture * cos_phase, aperture * sin_phase], 1).astype(jnp.bfloat16)
    cos_table, sin_table = fourier_tables(pupil_size)
    inverse = 1.0 / pupil_size
    along_cos = jnp.einsum(
        "sarc,cv->sarv", pupil_field, cos_table, preferred_element_type=jnp.float32
    )
    along_sin = jnp.einsum(
        "sarc,cv->sarv", pupil_field, sin_table, preferred_element_type=jnp.float32
    )
    column_field = jnp.stack(
        [along_cos[:, 0] - along_sin[:, 1], along_sin[:, 0] + along_cos[:, 1]], 1
    ).astype(jnp.bfloat16)
    pieces = lax.all_to_all(column_field, "row", split_axis=3, concat_axis=2, tiled=True)
    row_cos = jnp.einsum("sarv,ru->savu", pieces, cos_table, preferred_element_type=jnp.float32)
    row_sin = jnp.einsum("sarv,ru->savu", pieces, sin_table, preferred_element_type=jnp.float32)
    real_part = (row_cos[:, 0] - row_sin[:, 1]) * inverse
    imag_part = (row_sin[:, 0] + row_cos[:, 1]) * inverse
    focal_field = jnp.stack([real_part, imag_part], 1)
    weight = jnp.where(live_mask, 2.0, 0.0).astype(jnp.float32)[:, None, None, None]
    focal_grad = (weight * cotangent.astype(jnp.float32)[:, None] * focal_field).astype(
        jnp.bfloat16
    )
    back_cos = jnp.einsum(
        "savu,ur->savr", focal_grad, cos_table, preferred_element_type=jnp.float32
    )
    back_sin = jnp.einsum(
        "savu,ur->savr", focal_grad, sin_table, preferred_element_type=jnp.float32
    )
    spectrum_grad = jnp.stack(
        [(back_cos[:, 0] + back_sin[:, 1]) * inverse, (back_cos[:, 1] - back_sin[:, 0]) * inverse],
        1,
    ).astype(jnp.bfloat16)
    pieces = lax.all_to_all(spectrum_grad, "row", split_axis=3, concat_axis=2, tiled=True)
    col_cos = jnp.einsum("savr,vc->sarc", pieces, cos_table, preferred_element_type=jnp.float32)
    col_sin = jnp.einsum("savr,vc->sarc", pieces, sin_table, preferred_element_type=jnp.float32)
    pupil_grad = jnp.stack([col_cos[:, 0] + col_sin[:, 1], col_cos[:, 1] - col_sin[:, 0]], 1)
    phase_grad = aperture * (cos_phase * pupil_grad[:, 1] - sin_phase * pupil_grad[:, 0])
    path_grad = (
        (wave_number[:, None, None] * phase_grad)
        .astype(jnp.bfloat16)
        .reshape(-1, row_count * pupil_size)
    )
    map_scores = lax.dot_general(
        path_grad, flat_maps, (((1,), (1,)), ((), ())), preferred_element_type=jnp.float32
    )
    coef_part = lax.dot_general(
        cell_hot.astype(jnp.float32),
        map_scores * (1.0 / (8 * pupil_size)),
        (((0,), (0,)), ((), ())),
        precision=lax.Precision.HIGHEST,
    )
    coef_grad = lax.psum(coef_part, ("star", "row"))
    share = map_count // groups
    map_grad = lax.psum_scatter(
        lax.dot_general(
            coef_rows, path_grad, (((0,), (0,)), ((), ())), preferred_element_type=jnp.float32
        ),
        "star",
        scatter_dimension=0,
        tiled=True,
    )
    return (map_grad.reshape(share, row_count, pupil_size), coef_grad)


def half_tables(size):
    quarter = size // RADIX
    place = np.arange(quarter)[None, :, None]
    freq = RADIX * np.arange(quarter)[None, None, :] + np.arange(RADIX)[:, None, None]
    angle = 2.0 * np.pi / size * ((place * freq) % size)
    cosine, sine = np.cos(angle), -np.sin(angle)
    right = np.concatenate([cosine, sine], 2).astype(np.float32)
    left = np.concatenate([np.swapaxes(cosine, 1, 2), np.swapaxes(sine, 1, 2)], 2)
    return (
        jnp.asarray(right.astype(jnp.bfloat16)),
        jnp.asarray(left.astype(np.float32).astype(jnp.bfloat16)),
    )


def turn_cos_sin(turns):
    half = turns * np.float32(np.pi)
    square = half * half
    sine = jnp.full_like(square, -1.0 / 39916800.0)
    for term in (1.0 / 362880.0, -1.0 / 5040.0, 1.0 / 120.0, -1.0 / 6.0, 1.0):
        sine = sine * square + np.float32(term)
    sine = sine * half
    cosine = jnp.full_like(square, 1.0 / 479001600.0)
    for term in (-1.0 / 3628800.0, 1.0 / 40320.0, -1.0 / 720.0, 1.0 / 24.0, -0.5, 1.0):
        cosine = cosine * square + np.float32(term)
    return 1.0 - 2.0 * sine * sine, 2.0 * sine * cosine


def butterfly(real, imag, sign):
    sr, dr = real[0] + real[2], real[0] - real[2]
    si, di = imag[0] + imag[2], imag[0] - imag[2]
    tr, er = real[1] + real[3], real[1] - real[3]
    ti, ei = imag[1] + imag[3], imag[1] - imag[3]
    if sign < 0:
        er, ei = -er, -ei
    return (
        [sr + tr, dr - ei, sr - tr, dr + ei],
        [si + ti, di + er, si - ti, di - er],
    )


def greet(peers):
    barrier = pltpu.get_barrier_semaphore()
    for peer in peers:
        pl.semaphore_signal(barrier, inc=1, device_id=peer, device_id_type=pl.DeviceIdType.MESH)
    pl.semaphore_wait(barrier, len(peers))


def send(source, target, send_sem, recv_sem, peer):
    return pltpu.make_async_remote_copy(
        src_ref=source,
        dst_ref=target,
        send_sem=send_sem,
        recv_sem=recv_sem,
        device_id=peer,
        device_id_type=pl.DeviceIdType.MESH,
    )


def whole_tables(half_ref, whole_ref, sign):
    quarter = half_ref.shape[1]
    for k in range(RADIX):
        cosine, sine = half_ref[k, :, :quarter], half_ref[k, :, quarter:]
        upper, lower = (-sine, sine) if sign > 0 else (sine, -sine)
        whole_ref[k, :quarter, :quarter] = cosine
        whole_ref[k, :quarter, quarter:] = upper
        whole_ref[k, quarter:, :quarter] = lower
        whole_ref[k, quarter:, quarter:] = cosine


def plan_kernel(slots, count_ref, cell_ref, band_ref, cells_out, inverse_out, wave_out, route_out):
    chips = count_ref.shape[0] // 2
    over_x, over_y = OVER_X, OVER_Y
    share = STARS_CHIP
    first = [count_ref[2 * c] for c in range(chips)]
    held = [first[c] + count_ref[2 * c + 1] for c in range(chips)]
    level = []
    for y in range(chips // 2):
        both = held[2 * y] + held[2 * y + 1]
        if y == 0:
            level += [both // 2, both - both // 2]
        else:
            level += [2 * share - level[0], 2 * share - level[1]]
    keep_x = [jnp.minimum(held[c], level[c]) for c in range(chips)]
    keep_y = [jnp.minimum(level[c], share) for c in range(chips)]

    def choose(values, index):
        out = values[0]
        for c in range(1, chips):
            out = jnp.where(index == c, values[c], out)
        return out

    def slot_of(chip, place):
        place = jnp.minimum(place, choose(held, chip) - 1)
        start = choose(first, chip)
        return jnp.where(place < start, place, slots + place - start)

    def after_x(chip, place):
        place = jnp.minimum(place, choose(level, chip) - 1)
        kept = choose(keep_x, chip)
        return jnp.where(place < kept, slot_of(chip, place), 2 * slots + place - kept)

    def star_x(chip, place):
        kept = choose(keep_x, chip)
        other = chip + 1 - 2 * (chip % 2)
        own = chip * 2 * slots + slot_of(chip, place)
        far = other * 2 * slots + slot_of(other, choose(keep_x, other) + place - kept)
        return jnp.where(place < kept, own, far)

    per_chip = over_x + over_y + share

    def fill(chip, carry):
        base = chip * per_chip
        kept_x, kept_y = choose(keep_x, chip), choose(keep_y, chip)
        for i in range(over_x):
            route_out[base + i] = slot_of(chip, kept_x + i)
        for i in range(over_y):
            route_out[base + over_x + i] = after_x(chip, kept_y + i)
        other = chip + 2 - 4 * (chip // 2)
        for i in range(share):
            from_y = 2 * slots + over_x + i - kept_y
            route_out[base + over_x + over_y + i] = jnp.where(
                i < kept_y, after_x(chip, i), from_y
            )
            star = jnp.where(
                i < kept_y, star_x(chip, i), star_x(other, choose(keep_y, other) + i - kept_y)
            )
            group = star // slots
            band = band_ref[group, star - group * slots]
            at = chip * share + i
            cells_out[at] = cell_ref[group, star - group * slots]
            inverse, wave = jnp.float32(0), jnp.float32(0)
            for b in range(BANDS):
                length = 0.55 + 0.35 * b / (BANDS - 1)
                inverse = jnp.where(band == b, np.float32(1.0 / length), inverse)
                wave = jnp.where(band == b, np.float32(2.0 * np.pi / length), wave)
            inverse_out[at] = inverse
            wave_out[at] = wave
        return carry

    lax.fori_loop(0, chips, fill, 0)


def plan(star_counts, star_cells, star_bands):
    smem = pl.BlockSpec(memory_space=pltpu.SMEM)
    groups, slots = star_cells.shape
    chips = groups // 2
    total = chips * STARS_CHIP
    return pl.pallas_call(
        functools.partial(plan_kernel, slots),
        out_shape=(
            jax.ShapeDtypeStruct((total,), jnp.int32),
            jax.ShapeDtypeStruct((total,), F32),
            jax.ShapeDtypeStruct((total,), F32),
            jax.ShapeDtypeStruct((chips * (OVER_X + OVER_Y + STARS_CHIP),), jnp.int32),
        ),
        in_specs=[smem] * 3,
        out_specs=(smem,) * 4,
        name="plan",
    )(star_counts, star_cells, star_bands)


def group_rows(step, depth, row_count, lanes):
    return [
        pl.ds(pl.multiple_of(lane * row_count + step * depth, depth), depth)
        for lane in range(lanes)
    ]


def focal_kernel(
    groups, lanes, cell_ref, inverse_ref, route_ref, coef_ref, maps_ref, cot_ref, right_half, left_half,
    turns_out, xr, xi, right_ref, left_ref, maps_buf, stage, raw, pool, x_stage, y_stage, z_stage, ct, ct_turned,
    order, spread, yr, yi, *scratch,
):
    steps = TURN_STEPS
    chunks = pool.shape[0]
    x_got, y_got = scratch[:chunks], scratch[chunks : 2 * chunks]
    (
        m_sem, t_local, t_send, t_recv, r_local, r_send, r_recv, x_send, x_recv,
        y_send, y_recv, z_local, z_send, z_recv,
    ) = scratch[2 * chunks :]
    row = lax.axis_index("row")
    me = lax.axis_index("star")
    core = me % 2
    chip = me // 2
    twin = me + 1 - 2 * core
    over_x = me + 2 - 4 * (chip % 2)
    over_y = me + 4 - 8 * (me // 4)
    map_count, depth, size = maps_buf.shape[1:]
    row_count = depth * steps
    half = size // 2
    quarter = size // RADIX
    slots = raw.shape[0] // 2
    places = [(d, e) for e in range(2) for d in range(lanes)][1:]
    peers = [{"row": (row + d) % lanes, "star": twin if e else me} for d, e in places]
    greet(peers + [{"star": over_x}, {"star": over_y}])

    slot_range = pl.ds(core * slots, slots)
    other = 1 - core
    raw_own = pltpu.make_async_copy(
        cot_ref.at[:, :, pl.ds(pl.multiple_of(core * half, half), half)], raw.at[slot_range], r_local
    )
    raw_twin = send(
        cot_ref.at[:, :, pl.ds(pl.multiple_of(other * half, half), half)],
        raw.at[slot_range],
        r_send,
        r_recv,
        {"star": twin},
    )
    raw_own.start()
    raw_twin.start()

    def fetch(step):
        slot = step % 2
        rows = pl.ds(pl.multiple_of(step * depth, depth), depth)
        return pltpu.make_async_copy(maps_ref.at[:, rows], maps_buf.at[slot], m_sem.at[slot])

    fetch(0).start()
    fetch(1).start()
    whole_tables(right_half, right_ref, -1)
    whole_tables(left_half, left_ref, 1)

    lines = lanes * ROWS_STEP
    wide = map_count * ROWS_STEP
    cells = lax.broadcasted_iota(jnp.int32, (ROWS_STEP, coef_ref.shape[0]), 1)
    hot = jnp.concatenate(
        [
            jnp.where(cells == cell_ref[me * lanes + s], 1.0, 0.0).astype(BF16)
            for s in range(lanes)
        ],
        0,
    )
    coefs = jnp.dot(hot, coef_ref[...], preferred_element_type=F32).astype(BF16)
    at = lax.broadcasted_iota(jnp.int32, (map_count, wide), 0)
    to = lax.broadcasted_iota(jnp.int32, (map_count, wide), 1)
    repeat = jnp.where(to // ROWS_STEP == at, 1.0, 0.0).astype(BF16)
    repeated = jnp.dot(coefs, repeat, preferred_element_type=F32)
    at = lax.broadcasted_iota(jnp.int32, (lines, wide), 0)
    to = lax.broadcasted_iota(jnp.int32, (lines, wide), 1)
    spread[...] = jnp.where(at % ROWS_STEP == to % ROWS_STEP, repeated, 0.0).astype(BF16)

    def turn_copies(step):
        rows = pl.ds(pl.multiple_of(step * depth, depth), depth)
        place = pl.ds(pl.multiple_of(row * row_count + step * depth, depth), depth)
        return [
            pltpu.make_async_copy(stage.at[row, rows], turns_out.at[place], t_local.at[step])
        ] + [
            send(
                stage.at[(row + d) % lanes, rows],
                turns_out.at[place],
                t_send.at[step, d - 1],
                t_recv.at[step, d - 1],
                {"row": (row + d) % lanes},
            )
            for d in range(1, lanes)
        ]

    def phase_step(step, carry):
        slot = step % 2
        fetch(step).wait()
        for part in range(depth // ROWS_STEP):
            lined = pl.ds(part * ROWS_STEP, ROWS_STEP)
            maps = maps_buf[slot, :, lined].reshape(wide, size)
            path = jnp.dot(spread[...], maps, preferred_element_type=F32)
            rows = pl.ds(pl.multiple_of(step * depth + part * ROWS_STEP, ROWS_STEP), ROWS_STEP)
            for s in range(lanes):
                turned = path[s * ROWS_STEP : (s + 1) * ROWS_STEP] * inverse_ref[me * lanes + s]
                stage[s, rows] = (turned - jnp.floor(turned + 0.5)).astype(BF16)
        for copy in turn_copies(step):
            copy.start()

        @pl.when(step + 2 < steps)
        def _():
            fetch(step + 2).start()

        return carry

    lax.fori_loop(0, EARLY_STEPS, phase_step, 0)

    def x_copy(c):
        return send(x_stage.at[c], x_got[c], x_send.at[c], x_recv.at[c], {"star": over_x})

    def y_copy(c):
        return send(y_stage.at[c], y_got[c], y_send.at[c], y_recv.at[c], {"star": over_y})

    tall = quarter // lanes
    piece = tall * RADIX // chunks
    parts = chunks // RADIX
    per_chip = OVER_X + OVER_Y + STARS_CHIP
    base = chip * per_chip

    def z_copies(c):
        kind, part = c // parts, c % parts
        target = ct.at[
            kind,
            pl.ds(pl.multiple_of(row * tall + part * piece, piece), piece),
            pl.ds(pl.multiple_of(core * half, half), half),
        ]
        own = z_stage.at[c, core * lanes + row]
        return [pltpu.make_async_copy(own, target, z_local.at[c])] + [
            send(
                z_stage.at[c, (core + e) % 2 * lanes + (row + d) % lanes],
                target,
                z_send.at[c, n],
                z_recv.at[c, n],
                peers[n],
            )
            for n, (d, e) in enumerate(places)
        ]

    raw_own.wait()
    raw_twin.wait()
    at = lax.broadcasted_iota(jnp.int32, (row_count, row_count), 0)
    to = lax.broadcasted_iota(jnp.int32, (row_count, row_count), 1)
    sort = jnp.where(at % tall * RADIX + at // tall == to, 1.0, 0.0).astype(BF16)

    def sort_slot(slot, carry):
        sorted_rows = jnp.dot(sort, raw[slot], preferred_element_type=F32).astype(BF16)
        for c in range(chunks):
            pool[c, slot] = sorted_rows[c * piece : (c + 1) * piece]
        return carry

    lax.fori_loop(0, 2 * slots, sort_slot, 0)
    for c in range(chunks):
        for i in range(OVER_X):
            x_stage[c, i] = pool[c, route_ref[base + i]]
        x_copy(c).start()

    lax.fori_loop(EARLY_STEPS, steps, phase_step, 0)
    at = lax.broadcasted_iota(jnp.int32, (size, size), 0)
    to = lax.broadcasted_iota(jnp.int32, (size, size), 1)
    order[...] = jnp.where(at % quarter * RADIX + at // quarter == to, 1.0, 0.0).astype(BF16)

    def pick_x(c, index):
        mine = pool[c, jnp.minimum(index, 2 * slots - 1)]
        far = x_got[c][jnp.clip(index - 2 * slots, 0, OVER_X - 1)]
        return jnp.where(index < 2 * slots, mine, far)

    def route(c):
        x_copy(c).wait()
        for i in range(OVER_Y):
            y_stage[c, i] = pick_x(c, route_ref[base + OVER_X + i])
        y_copy(c).start()
        y_copy(c).wait()
        for i in range(STARS_CHIP):
            index = route_ref[base + OVER_X + OVER_Y + i]
            far = y_got[c][jnp.clip(index - 2 * slots - OVER_X, 0, OVER_Y - 1)]
            near = pick_x(c, jnp.minimum(index, 2 * slots + OVER_X - 1))
            z_stage[c, i] = jnp.where(index < 2 * slots + OVER_X, near, far)
        for copy in z_copies(c):
            copy.start()

    for c in range(chunks // 2):
        route(c)

    blocks = [slice(m * quarter, (m + 1) * quarter) for m in range(RADIX)]
    centre = 0.5 * (size - 1)
    scale = 1.0 / size
    tile = lanes * depth

    def forward_columns(step, carry):
        for copy in turn_copies(step):
            copy.wait()
        rows = group_rows(step, depth, row_count, lanes)
        turns = jnp.concatenate([turns_out[r, :] for r in rows], 0)
        cosine, sine = turn_cos_sin(turns.astype(F32))
        line = lax.broadcasted_iota(jnp.int32, (tile, size), 0)
        place = line // depth * row_count + line % depth + step * depth
        row_pos = place.astype(F32) - centre
        col_pos = lax.broadcasted_iota(jnp.int32, (tile, size), 1).astype(F32) - centre
        inside = row_pos * row_pos + col_pos * col_pos <= 0.25 * size * size
        real = jnp.where(inside, cosine, 0.0)
        imag = jnp.where(inside, sine, 0.0)
        mixed_real, mixed_imag = butterfly(
            [real[:, b] for b in blocks], [imag[:, b] for b in blocks], -1
        )
        for k in range(RADIX):
            both = jnp.concatenate([mixed_real[k].astype(BF16), mixed_imag[k].astype(BF16)], 1)
            made = jnp.dot(both, right_ref[k], preferred_element_type=F32).astype(BF16)
            for lane in range(lanes):
                lined = slice(lane * depth, (lane + 1) * depth)
                yr[rows[lane], blocks[k]] = made[lined, :quarter]
                yi[rows[lane], blocks[k]] = made[lined, quarter:]
        return carry

    lax.fori_loop(0, steps, forward_columns, 0)
    for c in range(chunks // 2, chunks):
        route(c)

    def focal(kind, carry):
        for part in range(parts):
            for copy in z_copies(kind * parts + part):
                copy.wait()
        ct_turned[...] = lax.dot_general(
            order[...], ct[kind], (((1,), (1,)), ((), ())), preferred_element_type=F32
        )
        cols = pl.ds(pl.multiple_of(kind * quarter, quarter), quarter)
        mixed_real, mixed_imag = butterfly(
            [yr[b, cols].astype(F32) for b in blocks],
            [yi[b, cols].astype(F32) for b in blocks],
            -1,
        )
        back_real, back_imag = [], []
        for k in range(RADIX):
            both = jnp.concatenate([mixed_real[k].astype(BF16), mixed_imag[k].astype(BF16)], 0)
            field = jnp.dot(left_ref[k], both, preferred_element_type=F32)
            weight = ct_turned[blocks[k], :] * (2.0 * scale)
            grad = (field * jnp.concatenate([weight, weight], 0)).astype(BF16)
            back = jnp.dot(right_ref[k], grad, preferred_element_type=F32)
            back_real.append(back[:quarter])
            back_imag.append(back[quarter:])
        spec_real, spec_imag = butterfly(back_real, back_imag, 1)
        for m in range(RADIX):
            xr[blocks[m], cols] = (spec_real[m] * scale).astype(BF16)
            xi[blocks[m], cols] = (spec_imag[m] * scale).astype(BF16)
        return carry

    lax.fori_loop(0, RADIX, focal, 0)


def focal_fields(cells, inverse, route, coef_table, feature_maps, cotangent, right, left, groups, lanes):
    map_count, row_count, size = feature_maps.shape
    slots = cotangent.shape[0]
    depth = row_count // TURN_STEPS
    half, quarter = size // 2, size // RADIX
    chunks = ROUTE_CHUNKS
    piece = row_count // chunks
    dma = pltpu.SemaphoreType.DMA
    smem = pl.BlockSpec(memory_space=pltpu.SMEM)
    vmem = pl.BlockSpec(memory_space=pltpu.VMEM)
    hbm = pl.BlockSpec(memory_space=pl.ANY)
    square = jax.ShapeDtypeStruct((size, size), BF16)
    others = 2 * lanes - 1
    return pl.pallas_call(
        functools.partial(focal_kernel, groups, lanes),
        out_shape=(square,) * 3,
        in_specs=[smem, smem, smem, vmem, hbm, hbm, vmem, vmem],
        out_specs=(vmem,) * 3,
        scratch_shapes=[
            pltpu.VMEM((RADIX, half, half), BF16),
            pltpu.VMEM((RADIX, half, half), BF16),
            pltpu.VMEM((2, map_count, depth, size), BF16),
            pltpu.VMEM((lanes, row_count, size), BF16),
            pltpu.VMEM((2 * slots, row_count, half), BF16),
            pltpu.VMEM((chunks, 2 * slots, piece, half), BF16),
            pltpu.VMEM((chunks, OVER_X, piece, half), BF16),
            pltpu.VMEM((chunks, OVER_Y, piece, half), BF16),
            pltpu.VMEM((chunks, STARS_CHIP, piece, half), BF16),
            pltpu.VMEM((RADIX, quarter, size), BF16),
            pltpu.VMEM((size, quarter), F32),
            pltpu.VMEM((size, size), BF16),
            pltpu.VMEM((lanes * ROWS_STEP, map_count * ROWS_STEP), BF16),
            pltpu.VMEM((size, size), BF16),
            pltpu.VMEM((size, size), BF16),
        ]
        + [pltpu.VMEM((OVER_X, piece, half), BF16)] * chunks
        + [pltpu.VMEM((OVER_Y, piece, half), BF16)] * chunks
        + [
            dma((2,)),
            dma((TURN_STEPS,)),
            dma((TURN_STEPS, lanes - 1)),
            dma((TURN_STEPS, lanes - 1)),
            dma,
            dma,
            dma,
            dma((chunks,)),
            dma((chunks,)),
            dma((chunks,)),
            dma((chunks,)),
            dma((chunks,)),
            dma((chunks, others)),
            dma((chunks, others)),
        ],
        compiler_params=pltpu.CompilerParams(
            collective_id=0, has_side_effects=True, vmem_limit_bytes=60 << 20
        ),
        name="focal_fields",
    )(cells, inverse, route, coef_table, feature_maps, cotangent, right, left)


def gradient_kernel(
    groups, lanes, cell_ref, wave_ref, coef_ref, turns_ref, xr, xi, half_ref, maps_ref, grad_out, coef_out,
    left, gathered, away, maps_buf, sums_buf, score, weights, row_part, star_part,
    m_sem, o_sem, z_send, z_recv, p_send, p_recv, c_send, c_recv, sr_send, sr_recv, ss_send, ss_recv,
):
    row = lax.axis_index("row")
    me = lax.axis_index("star")
    steps = GATHER_STEPS
    share = sums_buf.shape[1]
    map_count, row_count, size = maps_ref.shape
    depth = row_count // steps
    parts = depth // ROWS_STEP
    quarter = size // RADIX
    total = groups * lanes
    core = me + 1 - 2 * (me % 2)
    across = me + 2 - 4 * ((me // 2) % 2)
    along = me + 4 - 8 * ((me // 4) % 2)
    corner = across + 4 - 8 * ((me // 4) % 2)
    row_peers = [{"row": (row + d) % lanes} for d in range(1, lanes)]
    star_peers = [{"star": (me + d) % groups} for d in range(1, groups)]
    to_core, to_across, to_along = {"star": core}, {"star": across}, {"star": along}
    greet(row_peers + star_peers)
    half_lanes = lanes // 2

    def fetch(step, part):
        rows = pl.ds(pl.multiple_of(step * depth + part * ROWS_STEP, ROWS_STEP), ROWS_STEP)
        return pltpu.make_async_copy(maps_ref.at[:, rows], maps_buf.at[part], m_sem.at[part])

    for part in range(parts):
        fetch(0, part).start()
    whole_tables(half_ref, left, 1)

    def cell_of(group, d):
        return cell_ref[group * lanes + (row + lanes - d) % lanes]

    at = lax.broadcasted_iota(jnp.int32, (total, coef_ref.shape[0]), 0)
    to = lax.broadcasted_iota(jnp.int32, (total, coef_ref.shape[0]), 1)
    wanted = jnp.zeros_like(at)
    for group in range(groups):
        for d in range(lanes):
            wanted = jnp.where(at == group * lanes + d, cell_of(group, d), wanted)
    hot = jnp.where(to == wanted, 1.0, 0.0).astype(BF16)
    rows_of = jnp.dot(hot, coef_ref[...], preferred_element_type=F32).astype(BF16)
    lines = share * ROWS_STEP
    wide = total * ROWS_STEP
    at = lax.broadcasted_iota(jnp.int32, (lines, map_count), 0)
    to = lax.broadcasted_iota(jnp.int32, (lines, map_count), 1)
    mine = jnp.where(to == me * share + at // ROWS_STEP, 1.0, 0.0).astype(BF16)
    columns = lax.dot_general(
        mine, rows_of, (((1,), (1,)), ((), ())), preferred_element_type=F32
    ).astype(BF16)
    at = lax.broadcasted_iota(jnp.int32, (total, wide), 0)
    to = lax.broadcasted_iota(jnp.int32, (total, wide), 1)
    repeat = jnp.where(to // ROWS_STEP == at, 1.0, 0.0).astype(BF16)
    repeated = jnp.dot(columns, repeat, preferred_element_type=F32)
    at = lax.broadcasted_iota(jnp.int32, (lines, wide), 0)
    to = lax.broadcasted_iota(jnp.int32, (lines, wide), 1)
    weights[...] = jnp.where(at % ROWS_STEP == to % ROWS_STEP, repeated, 0.0).astype(BF16)
    score[...] = jnp.zeros_like(score)

    blocks = [slice(m * quarter, (m + 1) * quarter) for m in range(RADIX)]
    centre = 0.5 * (size - 1)
    tile = lanes * depth

    def rows_at(step):
        return pl.ds(pl.multiple_of(step * depth, depth), depth)

    def block(group, step, first=0, count=lanes):
        return gathered.at[group, pl.ds(first, count), rows_at(step)]

    def z_copies(step):
        return [
            send(
                away.at[d - 1, rows_at(step)],
                gathered.at[me, d, rows_at(step)],
                z_send.at[step, d - 1],
                z_recv.at[step, d - 1],
                row_peers[d - 1],
            )
            for d in range(1, lanes)
        ]

    def plane(step, way, part, peer):
        return send(part, part, p_send.at[step, way], p_recv.at[step, way], peer)

    def twin(step, way, part):
        return send(part, part, c_send.at[step, way], c_recv.at[step, way], to_core)

    def sides_own(step):
        part = block(me, step, 0, 1)
        return [plane(step, 0, part, to_across), plane(step, 1, part, to_along)]

    def sides_rest(step):
        part = block(me, step, 1, lanes - 1)
        return [plane(step, 2, part, to_across), plane(step, 3, part, to_along)]

    def corners(step):
        return [
            plane(step, 4, block(across, step, 0, half_lanes), to_along),
            plane(step, 5, block(along, step, half_lanes, lanes - half_lanes), to_across),
        ]

    def twins(step, first=0, last=5):
        parts = [
            lambda: block(me, step, 0, 1),
            lambda: block(me, step, 1, lanes - 1),
            lambda: block(across, step),
            lambda: block(along, step),
            lambda: block(corner, step),
        ]
        return [twin(step, way, parts[way]()) for way in range(first, last)]

    def columns_step(step):
        firsts = [(row + d) % lanes * row_count + step * depth for d in range(lanes)]
        rows = [pl.ds(pl.multiple_of(first, depth), depth) for first in firsts]
        turns = jnp.concatenate([turns_ref[r, :] for r in rows], 0)
        cosine, sine = turn_cos_sin(turns.astype(F32))
        line = lax.broadcasted_iota(jnp.int32, (tile, size), 0)
        place = (line // depth + row) % lanes * row_count + line % depth + step * depth
        row_pos = place.astype(F32) - centre
        col_pos = lax.broadcasted_iota(jnp.int32, (tile, size), 1).astype(F32) - centre
        inside = row_pos * row_pos + col_pos * col_pos <= 0.25 * size * size
        real = jnp.where(inside, cosine, 0.0)
        imag = jnp.where(inside, sine, 0.0)
        part_real, part_imag = [], []
        for k in range(RADIX):
            both = jnp.concatenate(
                [
                    jnp.concatenate([xr[r, blocks[k]] for r in rows], 0),
                    jnp.concatenate([xi[r, blocks[k]] for r in rows], 0),
                ],
                1,
            )
            made = jnp.dot(both, left[k], preferred_element_type=F32)
            part_real.append(made[:, :quarter])
            part_imag.append(made[:, quarter:])
        grad_real, grad_imag = butterfly(part_real, part_imag, 1)
        wave = wave_ref[me * lanes + row]
        for m in range(RADIX):
            grad = real[:, blocks[m]] * grad_imag[m] - imag[:, blocks[m]] * grad_real[m]
            grad = (wave * grad).astype(BF16)
            gathered[me, 0, rows_at(step), blocks[m]] = grad[:depth]
            for d in range(1, lanes):
                away[d - 1, rows_at(step), blocks[m]] = grad[d * depth : (d + 1) * depth]

    def score_step(step):
        for part in range(parts):
            fetch(step, part).wait()
            rows = pl.ds(pl.multiple_of(step * depth + part * ROWS_STEP, ROWS_STEP), ROWS_STEP)
            grads = gathered[me, :, rows].reshape(lanes * ROWS_STEP, size)
            maps = maps_buf[part].reshape(map_count * ROWS_STEP, size)
            score[...] += lax.dot_general(
                maps, grads, (((1,), (1,)), ((), ())), preferred_element_type=F32
            )

            @pl.when(step + 1 < steps)
            def _():
                fetch(step + 1, part).start()

    def sums_out(step):
        return pltpu.make_async_copy(
            sums_buf.at[step % 2], grad_out.at[:, rows_at(step)], o_sem.at[step % 2]
        )

    def sums_step(step):
        @pl.when(step >= 2)
        def _():
            sums_out(step - 2).wait()

        for part in range(parts):
            rows = pl.ds(pl.multiple_of(step * depth + part * ROWS_STEP, ROWS_STEP), ROWS_STEP)
            grads = gathered[:, :, rows].reshape(wide, size)
            made = jnp.dot(weights[...], grads, preferred_element_type=F32)
            sums_buf[step % 2, :, pl.ds(part * ROWS_STEP, ROWS_STEP)] = made.reshape(
                share, ROWS_STEP, size
            )
        sums_out(step).start()

    def row_copies():
        return [
            send(row_part.at[row], row_part.at[row], sr_send.at[d], sr_recv.at[d], row_peers[d])
            for d in range(lanes - 1)
        ]

    def star_copies():
        return [
            send(star_part.at[me], star_part.at[me], ss_send.at[d], ss_recv.at[d], star_peers[d])
            for d in range(groups - 1)
        ]

    def scores_rows():
        lined = score[...]
        at = lax.broadcasted_iota(jnp.int32, lined.shape, 0)
        to = lax.broadcasted_iota(jnp.int32, lined.shape, 1)
        kept = jnp.where(at % ROWS_STEP == to % ROWS_STEP, lined, 0.0)
        kept = jnp.sum(kept.reshape(map_count, ROWS_STEP, lined.shape[1]), axis=1)
        to = lax.broadcasted_iota(jnp.int32, kept.shape, 1)
        cell = lax.broadcasted_iota(jnp.int32, row_part.shape[1:], 1)
        part = jnp.zeros(row_part.shape[1:], F32)
        for d in range(lanes):
            value = jnp.sum(jnp.where(to // ROWS_STEP == d, kept, 0.0), axis=1, keepdims=True)
            part += jnp.where(cell == cell_of(me, d), value, 0.0)
        row_part[row] = part
        for copy in row_copies():
            copy.start()

    def scores_stars():
        for copy in row_copies():
            copy.wait()
        star_part[me] = jnp.sum(row_part[...], axis=0)
        for copy in star_copies():
            copy.start()

    def scores_end():
        for copy in star_copies():
            copy.wait()
        summed = jnp.sum(star_part[...], axis=0) * (1.0 / (8 * size))
        coef_out[...] = summed.T[: coef_out.shape[0]]

    def between(tick, lag, body):
        @pl.when(jnp.logical_and(tick >= lag, tick < steps + lag))
        def _():
            body(tick - lag)

    def compute(step):
        columns_step(step)
        for copy in z_copies(step) + sides_own(step) + twins(step, 0, 1):
            copy.start()

    def own_arrived(step):
        for copy in z_copies(step):
            copy.wait_recv()
        for copy in sides_rest(step) + twins(step, 1, 2):
            copy.start()

    def sides_arrived(step):
        for copy in sides_own(step) + sides_rest(step):
            copy.wait_recv()
        for copy in corners(step) + twins(step, 2, 4):
            copy.start()

    def corners_arrived(step):
        for copy in corners(step):
            copy.wait_recv()
        for copy in twins(step, 4):
            copy.start()

    def all_arrived(step):
        for copy in twins(step):
            copy.wait_recv()
        sums_step(step)

    def tick_body(tick, carry):
        between(tick, 0, compute)
        between(tick, 1, own_arrived)
        between(tick, 2, sides_arrived)
        between(tick, 3, corners_arrived)
        between(tick, 1, score_step)

        @pl.when(tick == steps)
        def _():
            scores_rows()

        @pl.when(tick == steps + 1)
        def _():
            scores_stars()

        @pl.when(tick == steps + 2)
        def _():
            scores_end()

        between(tick, 4, all_arrived)
        return carry

    lax.fori_loop(0, steps + 4, tick_body, 0)

    def drain(step, carry):
        for copy in (
            z_copies(step) + sides_own(step) + sides_rest(step) + corners(step) + twins(step)
        ):
            copy.wait_send()
        return carry

    lax.fori_loop(0, steps, drain, 0)
    for step in range(steps - 2, steps):
        sums_out(step).wait()


def gradient_sums(cells, wave, coef_table, turns, spec_real, spec_imag, halves, feature_maps, groups, lanes):
    map_count, row_count, size = feature_maps.shape
    cell_count = coef_table.shape[0]
    share = map_count // groups
    depth = row_count // GATHER_STEPS
    dma = pltpu.SemaphoreType.DMA
    smem = pl.BlockSpec(memory_space=pltpu.SMEM)
    vmem = pl.BlockSpec(memory_space=pltpu.VMEM)
    hbm = pl.BlockSpec(memory_space=pl.ANY)
    half = size // 2
    padded = -(-cell_count // 128) * 128
    return pl.pallas_call(
        functools.partial(gradient_kernel, groups, lanes),
        out_shape=(
            jax.ShapeDtypeStruct((share, row_count, size), F32),
            jax.ShapeDtypeStruct((cell_count, map_count), F32),
        ),
        in_specs=[smem, smem, vmem, vmem, vmem, vmem, vmem, hbm],
        out_specs=(hbm, vmem),
        scratch_shapes=[
            pltpu.VMEM((RADIX, half, half), BF16),
            pltpu.VMEM((groups, lanes, row_count, size), BF16),
            pltpu.VMEM((lanes - 1, row_count, size), BF16),
            pltpu.VMEM((depth // ROWS_STEP, map_count, ROWS_STEP, size), BF16),
            pltpu.VMEM((2, share, depth, size), F32),
            pltpu.VMEM((map_count * ROWS_STEP, lanes * ROWS_STEP), F32),
            pltpu.VMEM((share * ROWS_STEP, groups * lanes * ROWS_STEP), BF16),
            pltpu.VMEM((lanes, map_count, padded), F32),
            pltpu.VMEM((groups, map_count, padded), F32),
            dma((depth // ROWS_STEP,)),
            dma((2,)),
            dma((GATHER_STEPS, lanes - 1)),
            dma((GATHER_STEPS, lanes - 1)),
            dma((GATHER_STEPS, 6)),
            dma((GATHER_STEPS, 6)),
            dma((GATHER_STEPS, 5)),
            dma((GATHER_STEPS, 5)),
            dma((lanes - 1,)),
            dma((lanes - 1,)),
            dma((groups - 1,)),
            dma((groups - 1,)),
        ],
        compiler_params=pltpu.CompilerParams(
            collective_id=1, has_side_effects=True, vmem_limit_bytes=60 << 20
        ),
        name="gradient_sums",
    )(cells, wave, coef_table, turns, spec_real, spec_imag, halves, feature_maps)


def star_devices(feature_maps, coef_table, star_counts, star_cells, star_bands, psf_cotangent):
    groups = lax.axis_size("star")
    lanes = lax.axis_size("row")
    size = feature_maps.shape[2]
    cells, inverse, wave, route = plan(star_counts, star_cells, star_bands)
    right, left = half_tables(size)
    turns, spec_real, spec_imag = focal_fields(
        cells, inverse, route, coef_table, feature_maps, psf_cotangent, right, left, groups, lanes
    )
    return gradient_sums(
        cells, wave, coef_table, turns, spec_real, spec_imag, left, feature_maps, groups, lanes
    )


def solution(mesh):
    placed = (P(None, "row", None), P(), P(), P(), P(), P("star", "row", None))
    fits = mesh.shape["row"] == LIVE_DEV and mesh.shape["star"] == PLANE_DEV
    device = star_devices if fits else per_device
    return jax.shard_map(
        device,
        mesh=mesh,
        in_specs=placed,
        out_specs=(P("star", "row", None), P()),
        check_vma=False,
    )
```

```python
import functools

import jax
import jax.numpy as jnp
import numpy as np
from jax import lax
from jax.experimental import pallas as pl
from jax.experimental.pallas import tpu as pltpu
from jax.sharding import PartitionSpec as P

BANDS = 8
LIVE_DEV = 4
PLANE_DEV = 8
RADIX = 4
ROWS_STEP = 16
TURN_STEPS = 8
EARLY_STEPS = 2
ROUTE_CHUNKS = 8
GATHER_STEPS = 8
Z_AHEAD = 2
SIDES_LAG = 2
CORNERS_LAG = 2
OVER_X = 11
OVER_Y = 6
STARS_CHIP = 8
K1_LIMIT = 47
K2_LIMIT = 34
F32 = jnp.float32
BF16 = jnp.bfloat16


def fourier_tables(pupil_size):
    index_row = jnp.arange(pupil_size, dtype=jnp.int32)
    products = index_row[:, None] * index_row[None, :] % pupil_size
    angles = 2.0 * jnp.pi / pupil_size * products.astype(jnp.float32)
    return (jnp.cos(angles).astype(jnp.bfloat16), (-jnp.sin(angles)).astype(jnp.bfloat16))


def aperture_rows(first_row, row_count, pupil_size):
    centre = 0.5 * (pupil_size - 1)
    row_pos = (first_row + jnp.arange(row_count, dtype=jnp.int32)).astype(jnp.float32) - centre
    col_pos = jnp.arange(pupil_size, dtype=jnp.int32).astype(jnp.float32) - centre
    radius = row_pos[:, None] * row_pos[:, None] + col_pos[None, :] * col_pos[None, :]
    return jnp.where(radius <= 0.25 * pupil_size * pupil_size, 1.0, 0.0).astype(jnp.float32)


def wave_numbers(band_ids):
    wavelength = 0.55 + 0.35 * band_ids.astype(jnp.float32) / (BANDS - 1)
    return 2.0 * jnp.pi / wavelength


def table_pick(values, indices):
    positions = jnp.arange(values.shape[0], dtype=jnp.int32)
    chosen = jnp.where(positions[None, :] == indices[:, None], values[None, :], 0)
    return jnp.sum(chosen, axis=1)


def per_device(feature_maps, coef_table, star_counts, star_cells, star_bands, psf_cotangent):
    groups = lax.axis_size("star")
    my_group = lax.axis_index("star")
    slot_count = psf_cotangent.shape[0]
    map_count, row_count, pupil_size = feature_maps.shape
    group_ends = jnp.cumsum(star_counts)
    group_starts = group_ends - star_counts
    flat_cells = star_cells.reshape(-1)
    flat_bands = star_bands.reshape(-1)
    cell_count = coef_table.shape[0]
    capacity = -(-slot_count // groups)
    targets = jnp.arange(groups, dtype=jnp.int32)
    lane_index = jnp.arange(capacity, dtype=jnp.int32)
    my_start = table_pick(group_starts, my_group[None])
    my_count = table_pick(star_counts, my_group[None])
    first_slot = (targets - my_start) % groups
    send_slot = (first_slot[:, None] + lane_index[None, :] * groups).reshape(-1)
    valid_mask = send_slot < my_count
    picked = jnp.take(psf_cotangent, jnp.minimum(send_slot, slot_count - 1), axis=0)
    outgoing = jnp.where(valid_mask[:, None, None], picked, jnp.zeros_like(picked))
    incoming = lax.all_to_all(outgoing, "star", split_axis=0, concat_axis=0, tiled=True)
    star_rank = my_group + jnp.arange(LIVE_DEV, dtype=jnp.int32) * groups
    owner_group = jnp.sum((group_ends[None, :] <= star_rank[:, None]).astype(jnp.int32), axis=1)
    within = star_rank - table_pick(group_starts, owner_group)
    live_mask = jnp.ones((LIVE_DEV,), dtype=bool)
    owner_group, within, live_mask = (owner_group, within, live_mask)
    cotangent = jnp.take(incoming, owner_group * capacity + within // groups, axis=0)
    slot_index = owner_group * slot_count + within
    cell_ids = table_pick(flat_cells, slot_index)
    band_ids = table_pick(flat_bands, slot_index)
    cell_hot = cell_ids[:, None] == jnp.arange(cell_count, dtype=jnp.int32)[None, :]
    coef_rows = jnp.dot(
        cell_hot.astype(jnp.bfloat16), coef_table, preferred_element_type=jnp.float32
    ).astype(jnp.bfloat16)
    flat_maps = feature_maps.reshape(map_count, row_count * pupil_size)
    path_error = jnp.dot(coef_rows, flat_maps, preferred_element_type=jnp.float32).reshape(
        -1, row_count, pupil_size
    )
    wave_number = wave_numbers(band_ids)
    phase_angle = wave_number[:, None, None] * path_error
    aperture = aperture_rows(lax.axis_index("row") * row_count, row_count, pupil_size)
    cos_phase = jnp.cos(phase_angle)
    sin_phase = jnp.sin(phase_angle)
    pupil_field = jnp.stack([aperture * cos_phase, aperture * sin_phase], 1).astype(jnp.bfloat16)
    cos_table, sin_table = fourier_tables(pupil_size)
    inverse = 1.0 / pupil_size
    along_cos = jnp.einsum(
        "sarc,cv->sarv", pupil_field, cos_table, preferred_element_type=jnp.float32
    )
    along_sin = jnp.einsum(
        "sarc,cv->sarv", pupil_field, sin_table, preferred_element_type=jnp.float32
    )
    column_field = jnp.stack(
        [along_cos[:, 0] - along_sin[:, 1], along_sin[:, 0] + along_cos[:, 1]], 1
    ).astype(jnp.bfloat16)
    pieces = lax.all_to_all(column_field, "row", split_axis=3, concat_axis=2, tiled=True)
    row_cos = jnp.einsum("sarv,ru->savu", pieces, cos_table, preferred_element_type=jnp.float32)
    row_sin = jnp.einsum("sarv,ru->savu", pieces, sin_table, preferred_element_type=jnp.float32)
    real_part = (row_cos[:, 0] - row_sin[:, 1]) * inverse
    imag_part = (row_sin[:, 0] + row_cos[:, 1]) * inverse
    focal_field = jnp.stack([real_part, imag_part], 1)
    weight = jnp.where(live_mask, 2.0, 0.0).astype(jnp.float32)[:, None, None, None]
    focal_grad = (weight * cotangent.astype(jnp.float32)[:, None] * focal_field).astype(
        jnp.bfloat16
    )
    back_cos = jnp.einsum(
        "savu,ur->savr", focal_grad, cos_table, preferred_element_type=jnp.float32
    )
    back_sin = jnp.einsum(
        "savu,ur->savr", focal_grad, sin_table, preferred_element_type=jnp.float32
    )
    spectrum_grad = jnp.stack(
        [(back_cos[:, 0] + back_sin[:, 1]) * inverse, (back_cos[:, 1] - back_sin[:, 0]) * inverse],
        1,
    ).astype(jnp.bfloat16)
    pieces = lax.all_to_all(spectrum_grad, "row", split_axis=3, concat_axis=2, tiled=True)
    col_cos = jnp.einsum("savr,vc->sarc", pieces, cos_table, preferred_element_type=jnp.float32)
    col_sin = jnp.einsum("savr,vc->sarc", pieces, sin_table, preferred_element_type=jnp.float32)
    pupil_grad = jnp.stack([col_cos[:, 0] + col_sin[:, 1], col_cos[:, 1] - col_sin[:, 0]], 1)
    phase_grad = aperture * (cos_phase * pupil_grad[:, 1] - sin_phase * pupil_grad[:, 0])
    path_grad = (
        (wave_number[:, None, None] * phase_grad)
        .astype(jnp.bfloat16)
        .reshape(-1, row_count * pupil_size)
    )
    map_scores = lax.dot_general(
        path_grad, flat_maps, (((1,), (1,)), ((), ())), preferred_element_type=jnp.float32
    )
    coef_part = lax.dot_general(
        cell_hot.astype(jnp.float32),
        map_scores * (1.0 / (8 * pupil_size)),
        (((0,), (0,)), ((), ())),
        precision=lax.Precision.HIGHEST,
    )
    coef_grad = lax.psum(coef_part, ("star", "row"))
    share = map_count // groups
    map_grad = lax.psum_scatter(
        lax.dot_general(
            coef_rows, path_grad, (((0,), (0,)), ((), ())), preferred_element_type=jnp.float32
        ),
        "star",
        scatter_dimension=0,
        tiled=True,
    )
    return (map_grad.reshape(share, row_count, pupil_size), coef_grad)


def half_tables(size):
    quarter = size // RADIX
    place = np.arange(quarter)[None, :, None]
    freq = RADIX * np.arange(quarter)[None, None, :] + np.arange(RADIX)[:, None, None]
    angle = 2.0 * np.pi / size * ((place * freq) % size)
    cosine, sine = np.cos(angle), -np.sin(angle)
    table = np.concatenate([cosine, sine], 2).astype(np.float32)
    return jnp.asarray(table.astype(jnp.bfloat16))


def turn_cos_sin(turns):
    half = turns * np.float32(np.pi)
    square = half * half
    sine = jnp.full_like(square, -1.0 / 39916800.0)
    for term in (1.0 / 362880.0, -1.0 / 5040.0, 1.0 / 120.0, -1.0 / 6.0, 1.0):
        sine = sine * square + np.float32(term)
    sine = sine * half
    cosine = jnp.full_like(square, 1.0 / 479001600.0)
    for term in (-1.0 / 3628800.0, 1.0 / 40320.0, -1.0 / 720.0, 1.0 / 24.0, -0.5, 1.0):
        cosine = cosine * square + np.float32(term)
    return 1.0 - 2.0 * sine * sine, 2.0 * sine * cosine


def butterfly(real, imag, sign):
    sr, dr = real[0] + real[2], real[0] - real[2]
    si, di = imag[0] + imag[2], imag[0] - imag[2]
    tr, er = real[1] + real[3], real[1] - real[3]
    ti, ei = imag[1] + imag[3], imag[1] - imag[3]
    if sign < 0:
        er, ei = -er, -ei
    return (
        [sr + tr, dr - ei, sr - tr, dr + ei],
        [si + ti, di + er, si - ti, di - er],
    )


def greet(peers):
    barrier = pltpu.get_barrier_semaphore()
    for peer in peers:
        pl.semaphore_signal(barrier, inc=1, device_id=peer, device_id_type=pl.DeviceIdType.MESH)


def greeted(peers):
    pl.semaphore_wait(pltpu.get_barrier_semaphore(), len(peers))


def send(source, target, send_sem, recv_sem, peer):
    return pltpu.make_async_remote_copy(
        src_ref=source,
        dst_ref=target,
        send_sem=send_sem,
        recv_sem=recv_sem,
        device_id=peer,
        device_id_type=pl.DeviceIdType.MESH,
    )


def right_tables(half_ref, whole_ref):
    quarter = half_ref.shape[1]
    for k in range(RADIX):
        cosine, sine = half_ref[k, :, :quarter], half_ref[k, :, quarter:]
        whole_ref[k, :quarter, :quarter] = cosine
        whole_ref[k, :quarter, quarter:] = sine
        whole_ref[k, quarter:, :quarter] = -sine
        whole_ref[k, quarter:, quarter:] = cosine


def left_tables(half_ref, whole_ref):
    quarter = half_ref.shape[1]
    at = lax.broadcasted_iota(jnp.int32, (quarter, quarter), 0)
    to = lax.broadcasted_iota(jnp.int32, (quarter, quarter), 1)
    same = jnp.where(at == to, 1.0, 0.0).astype(BF16)

    def turned(table):
        made = lax.dot_general(same, table, (((1,), (1,)), ((), ())), preferred_element_type=F32)
        return made.astype(BF16)

    def fill(k, carry):
        cosine, sine = turned(half_ref[k, :, :quarter]), turned(half_ref[k, :, quarter:])
        whole_ref[k, :quarter, :quarter] = cosine
        whole_ref[k, :quarter, quarter:] = -sine
        whole_ref[k, quarter:, :quarter] = sine
        whole_ref[k, quarter:, quarter:] = cosine
        return carry

    lax.fori_loop(0, RADIX, fill, 0)


def star_plan(slots, count_ref, cells_ref, bands_ref):
    chips = count_ref.shape[0] // 2
    first = [count_ref[2 * c] for c in range(chips)]
    held = [first[c] + count_ref[2 * c + 1] for c in range(chips)]
    level = []
    for y in range(chips // 2):
        both = held[2 * y] + held[2 * y + 1]
        if y == 0:
            level += [both // 2, both - both // 2]
        else:
            level += [2 * STARS_CHIP - level[0], 2 * STARS_CHIP - level[1]]
    keep_x = [jnp.minimum(held[c], level[c]) for c in range(chips)]
    keep_y = [jnp.minimum(level[c], STARS_CHIP) for c in range(chips)]

    def choose(values, index):
        out = values[0]
        for c in range(1, chips):
            out = jnp.where(index == c, values[c], out)
        return out

    def routes(chip):
        start, count, reached = choose(first, chip), choose(held, chip), choose(level, chip)
        kept_x, kept_y = choose(keep_x, chip), choose(keep_y, chip)

        def slot_of(place):
            place = jnp.minimum(place, count - 1)
            return jnp.where(place < start, place, slots + place - start)

        def after_x(place):
            place = jnp.minimum(place, reached - 1)
            return jnp.where(place < kept_x, slot_of(place), 2 * slots + place - kept_x)

        def after_y(place):
            return jnp.where(
                place < kept_y, after_x(place), 2 * slots + OVER_X + place - kept_y
            )

        return (
            [jnp.clip(slot_of(kept_x + i), 0, 2 * slots - 1) for i in range(OVER_X)]
            + [after_x(kept_y + i) for i in range(OVER_Y)]
            + [after_y(i) for i in range(STARS_CHIP)]
        )

    def star_at(chip, place):
        over_y = chip + 2 - 4 * (chip // 2)
        kept_y = choose(keep_y, chip)
        here = jnp.where(place < kept_y, chip, over_y)
        place = jnp.where(place < kept_y, place, choose(keep_y, over_y) + place - kept_y)
        over_x = here + 1 - 2 * (here % 2)
        kept_x = choose(keep_x, here)
        origin = jnp.where(place < kept_x, here, over_x)
        place = jnp.where(place < kept_x, place, choose(keep_x, over_x) + place - kept_x)
        inner = place < choose(first, origin)
        group = 2 * origin + jnp.where(inner, 0, 1)
        slot = jnp.where(inner, place, place - choose(first, origin))
        return jnp.clip(group, 0, 2 * chips - 1), jnp.clip(slot, 0, slots - 1)

    def cell_at(chip, place):
        group, slot = star_at(chip, place)
        return cells_ref[group, slot]

    def wave_at(chip, place, scale):
        group, slot = star_at(chip, place)
        band = bands_ref[group, slot]
        value = jnp.float32(0)
        for b in range(BANDS):
            length = 0.55 + 0.35 * b / (BANDS - 1)
            value = jnp.where(band == b, np.float32(scale / length), value)
        return value

    return routes, cell_at, wave_at


def aperture_widths(size, row_count, depth):
    widths = []
    for step in range(row_count // depth):
        lowest = abs(step * depth + depth - 1 - 0.5 * (size - 1))
        reach = 2 * (np.sqrt(0.25 * size * size - lowest * lowest) + 1)
        widths.append(min(size, int(-(-reach // 256) * 256)))
    return widths


def group_rows(step, depth, row_count, lanes):
    return [
        pl.ds(pl.multiple_of(lane * row_count + step * depth, depth), depth)
        for lane in range(lanes)
    ]


def focal_kernel(
    groups, lanes, count_hbm, cells_hbm, bands_hbm, coef_hbm, maps_ref, cot_ref, half_ref,
    turns_out, xr, xi, left_ref, right_ref, maps_buf, stage, raw, pool, x_stage, y_stage, ct, ct_turned,
    spread, yr, yi, route_ref, count_ref, cells_ref, bands_ref, coef_ref,
    small_sem, *scratch,
):
    steps = TURN_STEPS
    small = [
        pltpu.make_async_copy(count_hbm, count_ref, small_sem.at[0]),
        pltpu.make_async_copy(cells_hbm, cells_ref, small_sem.at[1]),
        pltpu.make_async_copy(bands_hbm, bands_ref, small_sem.at[2]),
        pltpu.make_async_copy(coef_hbm, coef_ref, small_sem.at[3]),
    ]
    for copy in small:
        copy.start()
    chunks = pool.shape[0]
    x_got, y_got = scratch[:chunks], scratch[chunks : 2 * chunks]
    (
        m_sem, t_local, t_send, t_recv, r_local, r_send, r_recv, x_send, x_recv,
        y_send, y_recv, z_local, z_send, z_recv,
    ) = scratch[2 * chunks :]
    row = lax.axis_index("row")
    me = lax.axis_index("star")
    core = me % 2
    chip = me // 2
    twin = me + 1 - 2 * core
    over_x = me + 2 - 4 * (chip % 2)
    over_y = me + 4 - 8 * (me // 4)
    map_count, row_count, size = maps_ref.shape
    depth = row_count // steps
    half = size // 2
    quarter = size // RADIX
    slots = raw.shape[0] // 2
    places = [(d, e) for e in range(2) for d in range(lanes)][1:]
    peers = [{"row": (row + d) % lanes, "star": twin if e else me} for d, e in places]
    peers_all = peers + [{"star": over_x}, {"star": over_y}]
    greet(peers_all)

    slot_range = pl.ds(core * slots, slots)
    other = 1 - core
    raw_own = pltpu.make_async_copy(
        cot_ref.at[:, :, pl.ds(pl.multiple_of(core * half, half), half)], raw.at[slot_range], r_local
    )
    raw_twin = send(
        cot_ref.at[:, :, pl.ds(pl.multiple_of(other * half, half), half)],
        raw.at[slot_range],
        r_send,
        r_recv,
        {"star": twin},
    )
    raw_own.start()

    def fetch(step, part):
        rows = pl.ds(pl.multiple_of(step * depth + part * ROWS_STEP, ROWS_STEP), ROWS_STEP)
        return pltpu.make_async_copy(maps_ref.at[:, rows], maps_buf.at[part], m_sem.at[part])

    for part in range(depth // ROWS_STEP):
        fetch(0, part).start()
    for copy in small:
        copy.wait()
    routes, cell_at, wave_at = star_plan(slots, count_ref, cells_ref, bands_ref)
    places_here = [core * lanes + s for s in range(lanes)]
    cell_here = [cell_at(chip, place) for place in places_here]
    turn_here = [wave_at(chip, place, 1.0) for place in places_here]

    lines = lanes * ROWS_STEP
    wide = map_count * ROWS_STEP
    cells = lax.broadcasted_iota(jnp.int32, (ROWS_STEP, coef_ref.shape[0]), 1)
    hot = jnp.concatenate(
        [
            jnp.where(cells == cell_here[s], 1.0, 0.0).astype(BF16)
            for s in range(lanes)
        ],
        0,
    )
    coefs = jnp.dot(hot, coef_ref[...], preferred_element_type=F32).astype(BF16)
    at = lax.broadcasted_iota(jnp.int32, (map_count, wide), 0)
    to = lax.broadcasted_iota(jnp.int32, (map_count, wide), 1)
    repeat = jnp.where(to // ROWS_STEP == at, 1.0, 0.0).astype(BF16)
    repeated = jnp.dot(coefs, repeat, preferred_element_type=F32)
    at = lax.broadcasted_iota(jnp.int32, (lines, wide), 0)
    to = lax.broadcasted_iota(jnp.int32, (lines, wide), 1)
    spread[...] = jnp.where(at % ROWS_STEP == to % ROWS_STEP, repeated, 0.0).astype(BF16)

    widths = aperture_widths(size, row_count, depth)

    def turn_local(step):
        rows = pl.ds(pl.multiple_of(step * depth, depth), depth)
        place = pl.ds(pl.multiple_of(row * row_count + step * depth, depth), depth)
        return pltpu.make_async_copy(stage.at[row, rows], turns_out.at[place], t_local.at[step])

    def turn_copy(step, d, source, width):
        rows = pl.ds(pl.multiple_of(step * depth, depth), depth)
        place = pl.ds(pl.multiple_of(source * row_count + step * depth, depth), depth)
        cols = pl.ds((size - width) // 2, width)
        return send(
            stage.at[(row + d) % lanes, rows, cols],
            turns_out.at[place, cols],
            t_send.at[step],
            t_recv.at[step, d - 1],
            {"row": (row + d) % lanes},
        )

    def each_width(step, source, body):
        outer = jnp.where(source == 0, step, jnp.where(source == lanes - 1, steps - 1 - step, steps))
        first = 0
        for width in sorted(set(widths) | {size}):
            last = first + widths.count(width) if width < size else steps + 1

            @pl.when(jnp.logical_and(outer >= first, outer < last))
            def _():
                body(width)

            first = last

    def turns_start(step):
        turn_local(step).start()

        def start(width):
            for d in range(1, lanes):
                turn_copy(step, d, row, width).start()

        each_width(step, row, start)

    def turns_wait(step):
        turn_local(step).wait()
        rows = pl.ds(pl.multiple_of(step * depth, depth), depth)

        def sent(width):
            part = stage.at[pl.ds(0, lanes - 1), rows, pl.ds((size - width) // 2, width)]
            send(part, part, t_send.at[step], t_recv.at[step, 0], peers[0]).wait_send()

        each_width(step, row, sent)
        for d in range(1, lanes):
            source = (row + lanes - d) % lanes
            each_width(
                step, source, lambda width: turn_copy(step, d, source, width).wait_recv()
            )

    def phase_turns(step, carry):
        for part in range(depth // ROWS_STEP):
            fetch(step, part).wait()
            maps = maps_buf[part].reshape(wide, size)
            path = jnp.dot(spread[...], maps, preferred_element_type=F32)
            rows = pl.ds(pl.multiple_of(step * depth + part * ROWS_STEP, ROWS_STEP), ROWS_STEP)
            for s in range(lanes):
                turned = path[s * ROWS_STEP : (s + 1) * ROWS_STEP] * turn_here[s]
                stage[s, rows] = (turned - jnp.floor(turned + 0.5)).astype(BF16)

            @pl.when(step + 1 < steps)
            def _():
                fetch(step + 1, part).start()

        return carry

    def phase_step(step, carry):
        phase_turns(step, carry)
        turns_start(step)
        return carry

    def x_copy(c):
        return send(x_stage.at[c], x_got[c], x_send, x_recv.at[c], {"star": over_x})

    def y_copy(c):
        return send(y_stage.at[c], y_got[c], y_send, y_recv.at[c], {"star": over_y})

    tall = quarter // lanes
    piece = tall * RADIX // chunks
    parts = chunks // RADIX

    def star_piece(c, star):
        lined = pl.ds(pl.multiple_of(c * piece, piece), piece)
        return raw.at[2 * RADIX + star, lined]

    def z_target(c):
        kind, part = c // parts, c % parts
        return ct.at[
            kind,
            pl.ds(pl.multiple_of(row * tall + part * piece, piece), piece),
            pl.ds(pl.multiple_of(core * half, half), half),
        ]

    def z_local_copy(c):
        return pltpu.make_async_copy(star_piece(c, core * lanes + row), z_target(c), z_local.at[c])

    def z_start(c):
        z_local_copy(c).start()
        for d, e in places:
            star = (core + e) % 2 * lanes + (row + d) % lanes
            peer = {"row": (row + d) % lanes, "star": twin if e else me}
            send(star_piece(c, star), z_target(c), z_send, z_recv.at[c], peer).start()

    def z_arrival(c):
        sized = raw.at[pl.ds(0, len(places)), pl.ds(0, piece)]
        return send(sized, sized, z_send, z_recv.at[c], peers[0])

    def sort_slot(slot, carry):
        sorted_rows = jnp.dot(sort, raw[slot], preferred_element_type=F32).astype(BF16)
        for c in range(chunks):
            pool[c, slot] = sorted_rows[c * piece : (c + 1) * piece]
        return carry

    phase_turns(0, 0)
    for i, entry in enumerate(routes(chip)):
        route_ref[i] = entry
    at = lax.broadcasted_iota(jnp.int32, (row_count, row_count), 0)
    to = lax.broadcasted_iota(jnp.int32, (row_count, row_count), 1)
    sort = jnp.where(at % tall * RADIX + at // tall == to, 1.0, 0.0).astype(BF16)
    greeted(peers_all)
    raw_twin.start()
    turns_start(0)
    raw_own.wait()
    lax.fori_loop(core * slots, core * slots + slots, sort_slot, 0)
    lax.fori_loop(1, EARLY_STEPS, phase_step, 0)
    raw_twin.wait()
    lax.fori_loop(other * slots, other * slots + slots, sort_slot, 0)
    for c in range(chunks):
        for i in range(OVER_X):
            x_stage[c, i] = pool[c, route_ref[i]]
        x_copy(c).start()

    lax.fori_loop(EARLY_STEPS, steps, phase_step, 0)
    right_tables(half_ref, right_ref)
    left_tables(half_ref, left_ref)
    at = lax.broadcasted_iota(jnp.int32, (quarter, half), 0)
    to = lax.broadcasted_iota(jnp.int32, (quarter, half), 1)
    for k in range(RADIX):
        for side in range(2):
            raw[2 * k + side] = jnp.where(at * RADIX + k == to + side * half, 1.0, 0.0).astype(BF16)

    def pick_x(c, index):
        mine = pool[c, jnp.clip(index, 0, 2 * slots - 1)]
        far = x_got[c][jnp.clip(index - 2 * slots, 0, OVER_X - 1)]
        return jnp.where(index < 2 * slots, mine, far)

    def route_y(c):
        x_copy(c).wait_recv()
        for i in range(OVER_Y):
            y_stage[c, i] = pick_x(c, route_ref[OVER_X + i])
        y_copy(c).start()

    def route_z(c):
        y_copy(c).wait_recv()
        for i in range(STARS_CHIP):
            index = route_ref[OVER_X + OVER_Y + i]
            far = y_got[c][jnp.clip(index - 2 * slots - OVER_X, 0, OVER_Y - 1)]
            near = pick_x(c, jnp.minimum(index, 2 * slots + OVER_X - 1))
            raw[2 * RADIX + i, c * piece : (c + 1) * piece] = jnp.where(
                index < 2 * slots + OVER_X, near, far
            )
        z_start(c)

    blocks = [slice(m * quarter, (m + 1) * quarter) for m in range(RADIX)]
    centre = 0.5 * (size - 1)
    scale = 1.0 / size
    tile = lanes * depth

    def forward_columns(step, carry):
        turns_wait(step)
        rows = group_rows(step, depth, row_count, lanes)
        turns = jnp.concatenate([turns_out[r, :] for r in rows], 0)
        cosine, sine = turn_cos_sin(turns.astype(F32))
        line = lax.broadcasted_iota(jnp.int32, (tile, size), 0)
        place = line // depth * row_count + line % depth + step * depth
        row_pos = place.astype(F32) - centre
        col_pos = lax.broadcasted_iota(jnp.int32, (tile, size), 1).astype(F32) - centre
        inside = row_pos * row_pos + col_pos * col_pos <= 0.25 * size * size
        real = jnp.where(inside, cosine, 0.0)
        imag = jnp.where(inside, sine, 0.0)
        mixed_real, mixed_imag = butterfly(
            [real[:, b] for b in blocks], [imag[:, b] for b in blocks], -1
        )
        for k in range(RADIX):
            both = jnp.concatenate([mixed_real[k].astype(BF16), mixed_imag[k].astype(BF16)], 1)
            made = jnp.dot(both, right_ref[k], preferred_element_type=F32).astype(BF16)
            for lane in range(lanes):
                lined = slice(lane * depth, (lane + 1) * depth)
                yr[rows[lane], blocks[k]] = made[lined, :quarter]
                yi[rows[lane], blocks[k]] = made[lined, quarter:]
        return carry

    def focal(kind, carry):
        for part in range(parts):
            z_local_copy(kind * parts + part).wait()
            z_arrival(kind * parts + part).wait_recv()
        for side in range(2):
            cols = slice(side * half, (side + 1) * half)
            order = jnp.concatenate([raw[2 * k + side] for k in range(RADIX)], 0)
            turned = lax.dot_general(
                order, ct[kind, :, cols], (((1,), (1,)), ((), ())), preferred_element_type=F32
            )
            ct_turned[...] = turned if side == 0 else ct_turned[...] + turned
        cols = pl.ds(pl.multiple_of(kind * quarter, quarter), quarter)
        mixed_real, mixed_imag = butterfly(
            [yr[b, cols].astype(F32) for b in blocks],
            [yi[b, cols].astype(F32) for b in blocks],
            -1,
        )
        back_real, back_imag = [], []
        for k in range(RADIX):
            both = jnp.concatenate([mixed_real[k].astype(BF16), mixed_imag[k].astype(BF16)], 0)
            field = jnp.dot(left_ref[k], both, preferred_element_type=F32)
            weight = ct_turned[blocks[k], :] * (2.0 * scale)
            grad = (field * jnp.concatenate([weight, weight], 0)).astype(BF16)
            back = jnp.dot(right_ref[k], grad, preferred_element_type=F32)
            back_real.append(back[:quarter])
            back_imag.append(back[quarter:])
        spec_real, spec_imag = butterfly(back_real, back_imag, 1)
        for m in range(RADIX):
            xr[blocks[m], cols] = (spec_real[m] * scale).astype(BF16)
            xi[blocks[m], cols] = (spec_imag[m] * scale).astype(BF16)
        return carry

    column_plan = {chunks // 4: (0, 3), 3 * chunks // 8: (3, 6), 5 * chunks // 8: (6, 8)}
    focal_plan = {chunks - 2: 0, chunks - 1: 1}
    for c in range(chunks):
        route_y(c)
        if c in column_plan:
            first, last = column_plan[c]
            lax.fori_loop(first * steps // 8, last * steps // 8, forward_columns, 0)
        if c in focal_plan:
            focal(focal_plan[c], 0)
        route_z(c)
    lax.fori_loop(len(focal_plan), RADIX, focal, 0)
    sized = raw.at[pl.ds(0, len(places))]
    send(sized, sized, z_send, z_recv.at[0], peers[0]).wait_send()
    send(x_stage, x_stage, x_send, x_recv.at[0], {"star": over_x}).wait_send()
    send(y_stage, y_stage, y_send, y_recv.at[0], {"star": over_y}).wait_send()


def focal_fields(counts, cells, bands, coef_table, feature_maps, cotangent, halves, groups, lanes):
    map_count, row_count, size = feature_maps.shape
    slots = cotangent.shape[0]
    depth = row_count // TURN_STEPS
    half, quarter = size // 2, size // RADIX
    chunks = ROUTE_CHUNKS
    piece = row_count // chunks
    dma = pltpu.SemaphoreType.DMA
    smem = pl.BlockSpec(memory_space=pltpu.SMEM)
    vmem = pl.BlockSpec(memory_space=pltpu.VMEM)
    hbm = pl.BlockSpec(memory_space=pl.ANY)
    square = pltpu.VMEM((size, size), BF16)
    return pl.pallas_call(
        functools.partial(focal_kernel, groups, lanes),
        out_shape=(square,) * 3 + (pltpu.VMEM((RADIX, half, half), BF16),),
        in_specs=[pl.BlockSpec(memory_space=pltpu.HBM)] * 4 + [hbm, hbm, vmem],
        out_specs=(vmem,) * 4,
        scratch_shapes=[
            pltpu.VMEM((RADIX, half, half), BF16),
            pltpu.VMEM((depth // ROWS_STEP, map_count, ROWS_STEP, size), BF16),
            pltpu.VMEM((lanes, row_count, size), BF16),
            pltpu.VMEM((2 * slots, row_count, half), BF16),
            pltpu.VMEM((chunks, 2 * slots, piece, half), BF16),
            pltpu.VMEM((chunks, OVER_X, piece, half), BF16),
            pltpu.VMEM((chunks, OVER_Y, piece, half), BF16),
            pltpu.VMEM((RADIX, quarter, size), BF16),
            pltpu.VMEM((size, quarter), F32),
            pltpu.VMEM((lanes * ROWS_STEP, map_count * ROWS_STEP), BF16),
            pltpu.VMEM((size, size), BF16),
            pltpu.VMEM((size, size), BF16),
        ]
        + [
            pltpu.SMEM((OVER_X + OVER_Y + STARS_CHIP,), jnp.int32),
            pltpu.SMEM(counts.shape, jnp.int32),
            pltpu.SMEM(cells.shape, jnp.int32),
            pltpu.SMEM(bands.shape, jnp.int32),
            pltpu.VMEM(coef_table.shape, BF16),
            dma((4,)),
        ]
        + [pltpu.VMEM((OVER_X, piece, half), BF16)] * chunks
        + [pltpu.VMEM((OVER_Y, piece, half), BF16)] * chunks
        + [
            dma((depth // ROWS_STEP,)),
            dma((TURN_STEPS,)),
            dma((TURN_STEPS,)),
            dma((TURN_STEPS, lanes - 1)),
            dma,
            dma,
            dma,
            dma,
            dma((chunks,)),
            dma,
            dma((chunks,)),
            dma((chunks,)),
            dma,
            dma((chunks,)),
        ],
        compiler_params=pltpu.CompilerParams(
            collective_id=0, has_side_effects=True, vmem_limit_bytes=K1_LIMIT << 20
        ),
        name="focal_fields",
    )(counts, cells, bands, coef_table, feature_maps, cotangent, halves)


def gradient_kernel(
    groups, lanes, count_ref, cells_ref, bands_ref, coef_ref, turns_ref, xr, xi, left, maps_ref,
    grad_out, coef_out, cell_ref, gathered, away, maps_buf, score, weights, row_part, star_part,
    m_sem, z_send, z_recv, p_send, p_recv, c_send, c_recv, sr_send, sr_recv, ss_send, ss_recv,
):
    row = lax.axis_index("row")
    me = lax.axis_index("star")
    steps = GATHER_STEPS
    share = grad_out.shape[0]
    map_count, row_count, size = maps_ref.shape
    depth = row_count // steps
    parts = depth // ROWS_STEP
    quarter = size // RADIX
    total = groups * lanes
    core = me + 1 - 2 * (me % 2)
    across = me + 2 - 4 * ((me // 2) % 2)
    along = me + 4 - 8 * ((me // 4) % 2)
    corner = across + 4 - 8 * ((me // 4) % 2)
    row_peers = [{"row": (row + d) % lanes} for d in range(1, lanes)]
    star_peers = [{"star": (me + d) % groups} for d in range(1, groups)]
    to_core, to_across, to_along = {"star": core}, {"star": across}, {"star": along}
    greet(row_peers + star_peers)
    half_lanes = lanes // 2

    def fetch(step, part):
        rows = pl.ds(pl.multiple_of(step * depth + part * ROWS_STEP, ROWS_STEP), ROWS_STEP)
        return pltpu.make_async_copy(maps_ref.at[:, rows], maps_buf.at[part], m_sem.at[part])

    for part in range(parts):
        fetch(0, part).start()

    slots = cells_ref.shape[1]
    routes, cell_at, wave_at = star_plan(slots, count_ref, cells_ref, bands_ref)
    wave = wave_at(me // 2, me % 2 * lanes + row, 2.0 * np.pi)

    def cell_of(group, d):
        return cell_ref[group * lanes + (row + lanes - d) % lanes]

    blocks = [slice(m * quarter, (m + 1) * quarter) for m in range(RADIX)]
    centre = 0.5 * (size - 1)
    tile = lanes * depth

    def rows_at(step):
        return pl.ds(pl.multiple_of(step * depth, depth), depth)

    def block(group, step, first=0, count=lanes):
        return gathered.at[group, pl.ds(first, count), rows_at(step)]

    def z_start(step):
        for d in range(1, lanes):
            send(
                away.at[d - 1, rows_at(step)],
                gathered.at[me, d, rows_at(step)],
                z_send,
                z_recv.at[step],
                row_peers[d - 1],
            ).start()

    def plane(step, way, part, peer):
        send(part, part, p_send, p_recv.at[step, way], peer).start()

    def twin(step, part):
        send(part, part, c_send, c_recv.at[step], to_core).start()

    def sides(step, first, count):
        part = block(me, step, first, count)
        plane(step, 0, part, to_across)
        plane(step, 0, part, to_along)
        twin(step, part)

    def arrived(part, sem):
        send(part, part, p_send, sem, to_core).wait_recv()

    def columns_step(step):
        firsts = [(row + d) % lanes * row_count + step * depth for d in range(lanes)]
        rows = [pl.ds(pl.multiple_of(first, depth), depth) for first in firsts]
        turns = jnp.concatenate([turns_ref[r, :] for r in rows], 0)
        cosine, sine = turn_cos_sin(turns.astype(F32))
        line = lax.broadcasted_iota(jnp.int32, (tile, size), 0)
        place = (line // depth + row) % lanes * row_count + line % depth + step * depth
        row_pos = place.astype(F32) - centre
        col_pos = lax.broadcasted_iota(jnp.int32, (tile, size), 1).astype(F32) - centre
        inside = row_pos * row_pos + col_pos * col_pos <= 0.25 * size * size
        real = jnp.where(inside, cosine, 0.0)
        imag = jnp.where(inside, sine, 0.0)
        part_real, part_imag = [], []
        for k in range(RADIX):
            both = jnp.concatenate(
                [
                    jnp.concatenate([xr[r, blocks[k]] for r in rows], 0),
                    jnp.concatenate([xi[r, blocks[k]] for r in rows], 0),
                ],
                1,
            )
            made = jnp.dot(both, left[k], preferred_element_type=F32)
            part_real.append(made[:, :quarter])
            part_imag.append(made[:, quarter:])
        grad_real, grad_imag = butterfly(part_real, part_imag, 1)
        for m in range(RADIX):
            grad = real[:, blocks[m]] * grad_imag[m] - imag[:, blocks[m]] * grad_real[m]
            grad = (wave * grad).astype(BF16)
            gathered[me, 0, rows_at(step), blocks[m]] = grad[:depth]
            for d in range(1, lanes):
                away[d - 1, rows_at(step), blocks[m]] = grad[d * depth : (d + 1) * depth]

    def score_step(step):
        for part in range(parts):
            fetch(step, part).wait()
            rows = pl.ds(pl.multiple_of(step * depth + part * ROWS_STEP, ROWS_STEP), ROWS_STEP)
            grads = gathered[me, :, rows].reshape(lanes * ROWS_STEP, size)
            maps = maps_buf[part].reshape(map_count * ROWS_STEP, size)
            score[...] += lax.dot_general(
                maps, grads, (((1,), (1,)), ((), ())), preferred_element_type=F32
            )

            @pl.when(step + 1 < steps)
            def _():
                fetch(step + 1, part).start()

    def sums_step(step):
        for part in range(parts):
            rows = pl.ds(pl.multiple_of(step * depth + part * ROWS_STEP, ROWS_STEP), ROWS_STEP)
            grads = gathered[:, :, rows].reshape(wide, size)
            made = jnp.dot(weights[...], grads, preferred_element_type=F32)
            grad_out[:, rows] = made.reshape(share, ROWS_STEP, size)

    def row_copies():
        return [
            send(row_part.at[row], row_part.at[row], sr_send.at[d], sr_recv.at[d], row_peers[d])
            for d in range(lanes - 1)
        ]

    def star_copies():
        return [
            send(star_part.at[me], star_part.at[me], ss_send.at[d], ss_recv.at[d], star_peers[d])
            for d in range(groups - 1)
        ]

    def scores_rows():
        lined = score[...]
        at = lax.broadcasted_iota(jnp.int32, lined.shape, 0)
        to = lax.broadcasted_iota(jnp.int32, lined.shape, 1)
        kept = jnp.where(at % ROWS_STEP == to % ROWS_STEP, lined, 0.0)
        kept = jnp.sum(kept.reshape(map_count, ROWS_STEP, lined.shape[1]), axis=1)
        to = lax.broadcasted_iota(jnp.int32, kept.shape, 1)
        cell = lax.broadcasted_iota(jnp.int32, row_part.shape[1:], 1)
        part = jnp.zeros(row_part.shape[1:], F32)
        for d in range(lanes):
            value = jnp.sum(jnp.where(to // ROWS_STEP == d, kept, 0.0), axis=1, keepdims=True)
            part += jnp.where(cell == cell_of(me, d), value, 0.0)
        row_part[row] = part
        for copy in row_copies():
            copy.start()

    def scores_stars():
        for copy in row_copies():
            copy.wait()
        star_part[me] = jnp.sum(row_part[...], axis=0)
        for copy in star_copies():
            copy.start()

    def scores_end():
        for copy in star_copies():
            copy.wait()
        summed = jnp.sum(star_part[...], axis=0) * (1.0 / (8 * size))
        coef_out[...] = summed.T[: coef_out.shape[0]]

    def between(tick, lag, body):
        @pl.when(jnp.logical_and(tick >= lag, tick < steps + lag))
        def _():
            body(tick - lag)

    def compute(step, carry):
        columns_step(step)
        sides(step, 0, 1)
        return carry

    def own_arrived(step):
        sized = away.at[:, rows_at(step)]
        arrived(sized, z_recv.at[step])

        @pl.when(step + Z_AHEAD < steps)
        def _():
            z_start(step + Z_AHEAD)

        sides(step, 1, lanes - 1)

    def sides_arrived(step):
        arrived(gathered.at[pl.ds(0, 2), :, rows_at(step)], p_recv.at[step, 0])
        plane(step, 1, block(across, step, 0, half_lanes), to_along)
        plane(step, 1, block(along, step, half_lanes, lanes - half_lanes), to_across)
        twin(step, block(across, step))
        twin(step, block(along, step))

    def corners_arrived(step):
        arrived(gathered.at[pl.ds(0, 1), :, rows_at(step)], p_recv.at[step, 1])
        twin(step, block(corner, step))

    def all_arrived(step):
        arrived(gathered.at[pl.ds(0, groups // 2), :, rows_at(step)], c_recv.at[step])
        sums_step(step)

    def tick_body(tick, carry):
        between(tick, 0, own_arrived)
        between(tick, SIDES_LAG, sides_arrived)
        between(tick, SIDES_LAG + CORNERS_LAG, corners_arrived)
        between(tick, 0, score_step)

        @pl.when(tick == steps)
        def _():
            scores_rows()

        @pl.when(tick == steps + 1)
        def _():
            scores_stars()

        between(tick, SIDES_LAG + CORNERS_LAG + 1, all_arrived)
        return carry

    columns_step(0)
    greeted(row_peers + star_peers)
    z_start(0)
    sides(0, 0, 1)
    for step in range(1, Z_AHEAD):
        compute(step, 0)
        z_start(step)
    lax.fori_loop(Z_AHEAD, steps, compute, 0)
    def cell_fill(chip, carry):
        for place in range(STARS_CHIP):
            cell_ref[chip * STARS_CHIP + place] = cell_at(chip, place)
        return carry

    lax.fori_loop(0, total // STARS_CHIP, cell_fill, 0)
    at = lax.broadcasted_iota(jnp.int32, (total, coef_ref.shape[0]), 0)
    to = lax.broadcasted_iota(jnp.int32, (total, coef_ref.shape[0]), 1)
    wanted = jnp.zeros_like(at)
    for group in range(groups):
        for d in range(lanes):
            wanted = jnp.where(at == group * lanes + d, cell_of(group, d), wanted)
    hot = jnp.where(to == wanted, 1.0, 0.0).astype(BF16)
    rows_of = jnp.dot(hot, coef_ref[...], preferred_element_type=F32).astype(BF16)
    lines = share * ROWS_STEP
    wide = total * ROWS_STEP
    at = lax.broadcasted_iota(jnp.int32, (lines, map_count), 0)
    to = lax.broadcasted_iota(jnp.int32, (lines, map_count), 1)
    mine = jnp.where(to == me * share + at // ROWS_STEP, 1.0, 0.0).astype(BF16)
    columns = lax.dot_general(
        mine, rows_of, (((1,), (1,)), ((), ())), preferred_element_type=F32
    ).astype(BF16)
    at = lax.broadcasted_iota(jnp.int32, (total, wide), 0)
    to = lax.broadcasted_iota(jnp.int32, (total, wide), 1)
    repeat = jnp.where(to // ROWS_STEP == at, 1.0, 0.0).astype(BF16)
    repeated = jnp.dot(columns, repeat, preferred_element_type=F32)
    at = lax.broadcasted_iota(jnp.int32, (lines, wide), 0)
    to = lax.broadcasted_iota(jnp.int32, (lines, wide), 1)
    weights[...] = jnp.where(at % ROWS_STEP == to % ROWS_STEP, repeated, 0.0).astype(BF16)
    score[...] = jnp.zeros_like(score)
    lax.fori_loop(0, steps + SIDES_LAG + CORNERS_LAG + 1, tick_body, 0)
    scores_end()
    send(away, away, z_send, z_recv.at[0], to_core).wait_send()
    three, four = gathered.at[pl.ds(0, 3)], gathered.at[pl.ds(0, groups // 2)]
    send(three, three, p_send, z_recv.at[0], to_core).wait_send()
    send(four, four, c_send, z_recv.at[0], to_core).wait_send()


def gradient_sums(counts, cells, bands, coef_table, turns, spec_real, spec_imag, left, feature_maps, groups, lanes):
    map_count, row_count, size = feature_maps.shape
    cell_count = coef_table.shape[0]
    share = map_count // groups
    depth = row_count // GATHER_STEPS
    dma = pltpu.SemaphoreType.DMA
    smem = pl.BlockSpec(memory_space=pltpu.SMEM)
    vmem = pl.BlockSpec(memory_space=pltpu.VMEM)
    hbm = pl.BlockSpec(memory_space=pl.ANY)
    padded = -(-cell_count // 128) * 128
    return pl.pallas_call(
        functools.partial(gradient_kernel, groups, lanes),
        out_shape=(
            pltpu.VMEM((share, row_count, size), F32),
            jax.ShapeDtypeStruct((cell_count, map_count), F32),
        ),
        in_specs=[smem, smem, smem, vmem, vmem, vmem, vmem, vmem, hbm],
        out_specs=(vmem, vmem),
        scratch_shapes=[
            pltpu.SMEM((groups * lanes,), jnp.int32),
            pltpu.VMEM((groups, lanes, row_count, size), BF16),
            pltpu.VMEM((lanes - 1, row_count, size), BF16),
            pltpu.VMEM((depth // ROWS_STEP, map_count, ROWS_STEP, size), BF16),
            pltpu.VMEM((map_count * ROWS_STEP, lanes * ROWS_STEP), F32),
            pltpu.VMEM((share * ROWS_STEP, groups * lanes * ROWS_STEP), BF16),
            pltpu.VMEM((lanes, map_count, padded), F32),
            pltpu.VMEM((groups, map_count, padded), F32),
            dma((depth // ROWS_STEP,)),
            dma,
            dma((GATHER_STEPS,)),
            dma,
            dma((GATHER_STEPS, 2)),
            dma,
            dma((GATHER_STEPS,)),
            dma((lanes - 1,)),
            dma((lanes - 1,)),
            dma((groups - 1,)),
            dma((groups - 1,)),
        ],
        compiler_params=pltpu.CompilerParams(
            collective_id=1, has_side_effects=True, vmem_limit_bytes=K2_LIMIT << 20
        ),
        name="gradient_sums",
    )(counts, cells, bands, coef_table, turns, spec_real, spec_imag, left, feature_maps)


def star_devices(feature_maps, coef_table, star_counts, star_cells, star_bands, psf_cotangent):
    groups = lax.axis_size("star")
    lanes = lax.axis_size("row")
    size = feature_maps.shape[2]
    halves = half_tables(size)
    turns, spec_real, spec_imag, left = focal_fields(
        star_counts, star_cells, star_bands, coef_table, feature_maps, psf_cotangent, halves, groups, lanes
    )
    return gradient_sums(
        star_counts, star_cells, star_bands, coef_table, turns, spec_real, spec_imag, left, feature_maps,
        groups, lanes,
    )


def solution(mesh):
    placed = (P(None, "row", None), P(), P(), P(), P(), P("star", "row", None))
    fits = mesh.shape["row"] == LIVE_DEV and mesh.shape["star"] == PLANE_DEV
    device = star_devices if fits else per_device
    return jax.shard_map(
        device,
        mesh=mesh,
        in_specs=placed,
        out_specs=(P("star", "row", None), P()),
        check_vma=False,
    )
```

```python
import functools

import jax
import jax.numpy as jnp
import numpy as np
from jax import lax
from jax.experimental import pallas as pl
from jax.experimental.pallas import tpu as pltpu
from jax.sharding import PartitionSpec as P

BANDS = 8
LIVE_DEV = 4
PLANE_DEV = 8
RADIX = 4
ROWS_STEP = 16
TURN_STEPS = 8
EARLY_STEPS = 2
ROUTE_CHUNKS = 8
GATHER_STEPS = 8
Z_AHEAD = 2
SIDES_LAG = 2
CORNERS_LAG = 2
OVER_X = 11
OVER_Y = 6
STARS_CHIP = 8
K1_LIMIT = 47
K2_LIMIT = 34
F32 = jnp.float32
BF16 = jnp.bfloat16


def fourier_tables(pupil_size):
    index_row = jnp.arange(pupil_size, dtype=jnp.int32)
    products = index_row[:, None] * index_row[None, :] % pupil_size
    angles = 2.0 * jnp.pi / pupil_size * products.astype(jnp.float32)
    return (jnp.cos(angles).astype(jnp.bfloat16), (-jnp.sin(angles)).astype(jnp.bfloat16))


def aperture_rows(first_row, row_count, pupil_size):
    centre = 0.5 * (pupil_size - 1)
    row_pos = (first_row + jnp.arange(row_count, dtype=jnp.int32)).astype(jnp.float32) - centre
    col_pos = jnp.arange(pupil_size, dtype=jnp.int32).astype(jnp.float32) - centre
    radius = row_pos[:, None] * row_pos[:, None] + col_pos[None, :] * col_pos[None, :]
    return jnp.where(radius <= 0.25 * pupil_size * pupil_size, 1.0, 0.0).astype(jnp.float32)


def wave_numbers(band_ids):
    wavelength = 0.55 + 0.35 * band_ids.astype(jnp.float32) / (BANDS - 1)
    return 2.0 * jnp.pi / wavelength


def table_pick(values, indices):
    positions = jnp.arange(values.shape[0], dtype=jnp.int32)
    chosen = jnp.where(positions[None, :] == indices[:, None], values[None, :], 0)
    return jnp.sum(chosen, axis=1)


def per_device(feature_maps, coef_table, star_counts, star_cells, star_bands, psf_cotangent):
    groups = lax.axis_size("star")
    my_group = lax.axis_index("star")
    slot_count = psf_cotangent.shape[0]
    map_count, row_count, pupil_size = feature_maps.shape
    group_ends = jnp.cumsum(star_counts)
    group_starts = group_ends - star_counts
    flat_cells = star_cells.reshape(-1)
    flat_bands = star_bands.reshape(-1)
    cell_count = coef_table.shape[0]
    capacity = -(-slot_count // groups)
    targets = jnp.arange(groups, dtype=jnp.int32)
    lane_index = jnp.arange(capacity, dtype=jnp.int32)
    my_start = table_pick(group_starts, my_group[None])
    my_count = table_pick(star_counts, my_group[None])
    first_slot = (targets - my_start) % groups
    send_slot = (first_slot[:, None] + lane_index[None, :] * groups).reshape(-1)
    valid_mask = send_slot < my_count
    picked = jnp.take(psf_cotangent, jnp.minimum(send_slot, slot_count - 1), axis=0)
    outgoing = jnp.where(valid_mask[:, None, None], picked, jnp.zeros_like(picked))
    incoming = lax.all_to_all(outgoing, "star", split_axis=0, concat_axis=0, tiled=True)
    star_rank = my_group + jnp.arange(LIVE_DEV, dtype=jnp.int32) * groups
    owner_group = jnp.sum((group_ends[None, :] <= star_rank[:, None]).astype(jnp.int32), axis=1)
    within = star_rank - table_pick(group_starts, owner_group)
    live_mask = jnp.ones((LIVE_DEV,), dtype=bool)
    owner_group, within, live_mask = (owner_group, within, live_mask)
    cotangent = jnp.take(incoming, owner_group * capacity + within // groups, axis=0)
    slot_index = owner_group * slot_count + within
    cell_ids = table_pick(flat_cells, slot_index)
    band_ids = table_pick(flat_bands, slot_index)
    cell_hot = cell_ids[:, None] == jnp.arange(cell_count, dtype=jnp.int32)[None, :]
    coef_rows = jnp.dot(
        cell_hot.astype(jnp.bfloat16), coef_table, preferred_element_type=jnp.float32
    ).astype(jnp.bfloat16)
    flat_maps = feature_maps.reshape(map_count, row_count * pupil_size)
    path_error = jnp.dot(coef_rows, flat_maps, preferred_element_type=jnp.float32).reshape(
        -1, row_count, pupil_size
    )
    wave_number = wave_numbers(band_ids)
    phase_angle = wave_number[:, None, None] * path_error
    aperture = aperture_rows(lax.axis_index("row") * row_count, row_count, pupil_size)
    cos_phase = jnp.cos(phase_angle)
    sin_phase = jnp.sin(phase_angle)
    pupil_field = jnp.stack([aperture * cos_phase, aperture * sin_phase], 1).astype(jnp.bfloat16)
    cos_table, sin_table = fourier_tables(pupil_size)
    inverse = 1.0 / pupil_size
    along_cos = jnp.einsum(
        "sarc,cv->sarv", pupil_field, cos_table, preferred_element_type=jnp.float32
    )
    along_sin = jnp.einsum(
        "sarc,cv->sarv", pupil_field, sin_table, preferred_element_type=jnp.float32
    )
    column_field = jnp.stack(
        [along_cos[:, 0] - along_sin[:, 1], along_sin[:, 0] + along_cos[:, 1]], 1
    ).astype(jnp.bfloat16)
    pieces = lax.all_to_all(column_field, "row", split_axis=3, concat_axis=2, tiled=True)
    row_cos = jnp.einsum("sarv,ru->savu", pieces, cos_table, preferred_element_type=jnp.float32)
    row_sin = jnp.einsum("sarv,ru->savu", pieces, sin_table, preferred_element_type=jnp.float32)
    real_part = (row_cos[:, 0] - row_sin[:, 1]) * inverse
    imag_part = (row_sin[:, 0] + row_cos[:, 1]) * inverse
    focal_field = jnp.stack([real_part, imag_part], 1)
    weight = jnp.where(live_mask, 2.0, 0.0).astype(jnp.float32)[:, None, None, None]
    focal_grad = (weight * cotangent.astype(jnp.float32)[:, None] * focal_field).astype(
        jnp.bfloat16
    )
    back_cos = jnp.einsum(
        "savu,ur->savr", focal_grad, cos_table, preferred_element_type=jnp.float32
    )
    back_sin = jnp.einsum(
        "savu,ur->savr", focal_grad, sin_table, preferred_element_type=jnp.float32
    )
    spectrum_grad = jnp.stack(
        [(back_cos[:, 0] + back_sin[:, 1]) * inverse, (back_cos[:, 1] - back_sin[:, 0]) * inverse],
        1,
    ).astype(jnp.bfloat16)
    pieces = lax.all_to_all(spectrum_grad, "row", split_axis=3, concat_axis=2, tiled=True)
    col_cos = jnp.einsum("savr,vc->sarc", pieces, cos_table, preferred_element_type=jnp.float32)
    col_sin = jnp.einsum("savr,vc->sarc", pieces, sin_table, preferred_element_type=jnp.float32)
    pupil_grad = jnp.stack([col_cos[:, 0] + col_sin[:, 1], col_cos[:, 1] - col_sin[:, 0]], 1)
    phase_grad = aperture * (cos_phase * pupil_grad[:, 1] - sin_phase * pupil_grad[:, 0])
    path_grad = (
        (wave_number[:, None, None] * phase_grad)
        .astype(jnp.bfloat16)
        .reshape(-1, row_count * pupil_size)
    )
    map_scores = lax.dot_general(
        path_grad, flat_maps, (((1,), (1,)), ((), ())), preferred_element_type=jnp.float32
    )
    coef_part = lax.dot_general(
        cell_hot.astype(jnp.float32),
        map_scores * (1.0 / (8 * pupil_size)),
        (((0,), (0,)), ((), ())),
        precision=lax.Precision.HIGHEST,
    )
    coef_grad = lax.psum(coef_part, ("star", "row"))
    share = map_count // groups
    map_grad = lax.psum_scatter(
        lax.dot_general(
            coef_rows, path_grad, (((0,), (0,)), ((), ())), preferred_element_type=jnp.float32
        ),
        "star",
        scatter_dimension=0,
        tiled=True,
    )
    return (map_grad.reshape(share, row_count, pupil_size), coef_grad)


def half_tables(size):
    quarter = size // RADIX
    place = np.arange(quarter)[None, :, None]
    freq = RADIX * np.arange(quarter)[None, None, :] + np.arange(RADIX)[:, None, None]
    angle = 2.0 * np.pi / size * ((place * freq) % size)
    cosine, sine = np.cos(angle), -np.sin(angle)
    table = np.concatenate([cosine, sine], 2).astype(np.float32)
    return jnp.asarray(table.astype(jnp.bfloat16))


def turn_cos_sin(turns):
    half = turns * np.float32(np.pi)
    square = half * half
    sine = jnp.full_like(square, -1.0 / 39916800.0)
    for term in (1.0 / 362880.0, -1.0 / 5040.0, 1.0 / 120.0, -1.0 / 6.0, 1.0):
        sine = sine * square + np.float32(term)
    sine = sine * half
    cosine = jnp.full_like(square, 1.0 / 479001600.0)
    for term in (-1.0 / 3628800.0, 1.0 / 40320.0, -1.0 / 720.0, 1.0 / 24.0, -0.5, 1.0):
        cosine = cosine * square + np.float32(term)
    return 1.0 - 2.0 * sine * sine, 2.0 * sine * cosine


def butterfly(real, imag, sign):
    sr, dr = real[0] + real[2], real[0] - real[2]
    si, di = imag[0] + imag[2], imag[0] - imag[2]
    tr, er = real[1] + real[3], real[1] - real[3]
    ti, ei = imag[1] + imag[3], imag[1] - imag[3]
    if sign < 0:
        er, ei = -er, -ei
    return (
        [sr + tr, dr - ei, sr - tr, dr + ei],
        [si + ti, di + er, si - ti, di - er],
    )


def greet(peers):
    barrier = pltpu.get_barrier_semaphore()
    for peer in peers:
        pl.semaphore_signal(barrier, inc=1, device_id=peer, device_id_type=pl.DeviceIdType.MESH)


def greeted(peers):
    pl.semaphore_wait(pltpu.get_barrier_semaphore(), len(peers))


def send(source, target, send_sem, recv_sem, peer):
    return pltpu.make_async_remote_copy(
        src_ref=source,
        dst_ref=target,
        send_sem=send_sem,
        recv_sem=recv_sem,
        device_id=peer,
        device_id_type=pl.DeviceIdType.MESH,
    )


def right_tables(half_ref, whole_ref):
    quarter = half_ref.shape[1]
    for k in range(RADIX):
        cosine, sine = half_ref[k, :, :quarter], half_ref[k, :, quarter:]
        whole_ref[k, :quarter, :quarter] = cosine
        whole_ref[k, :quarter, quarter:] = sine
        whole_ref[k, quarter:, :quarter] = -sine
        whole_ref[k, quarter:, quarter:] = cosine


def left_tables(half_ref, whole_ref):
    quarter = half_ref.shape[1]
    at = lax.broadcasted_iota(jnp.int32, (quarter, quarter), 0)
    to = lax.broadcasted_iota(jnp.int32, (quarter, quarter), 1)
    same = jnp.where(at == to, 1.0, 0.0).astype(BF16)

    def turned(table):
        made = lax.dot_general(same, table, (((1,), (1,)), ((), ())), preferred_element_type=F32)
        return made.astype(BF16)

    def fill(k, carry):
        cosine, sine = turned(half_ref[k, :, :quarter]), turned(half_ref[k, :, quarter:])
        whole_ref[k, :quarter, :quarter] = cosine
        whole_ref[k, :quarter, quarter:] = -sine
        whole_ref[k, quarter:, :quarter] = sine
        whole_ref[k, quarter:, quarter:] = cosine
        return carry

    lax.fori_loop(0, RADIX, fill, 0)


def star_plan(slots, count_ref, cells_ref, bands_ref):
    chips = count_ref.shape[0] // 2
    first = [count_ref[2 * c] for c in range(chips)]
    held = [first[c] + count_ref[2 * c + 1] for c in range(chips)]
    level = []
    for y in range(chips // 2):
        both = held[2 * y] + held[2 * y + 1]
        if y == 0:
            level += [both // 2, both - both // 2]
        else:
            level += [2 * STARS_CHIP - level[0], 2 * STARS_CHIP - level[1]]
    keep_x = [jnp.minimum(held[c], level[c]) for c in range(chips)]
    keep_y = [jnp.minimum(level[c], STARS_CHIP) for c in range(chips)]

    def choose(values, index):
        out = values[0]
        for c in range(1, chips):
            out = jnp.where(index == c, values[c], out)
        return out

    def routes(chip):
        start, count, reached = choose(first, chip), choose(held, chip), choose(level, chip)
        kept_x, kept_y = choose(keep_x, chip), choose(keep_y, chip)

        def slot_of(place):
            place = jnp.minimum(place, count - 1)
            return jnp.where(place < start, place, slots + place - start)

        def after_x(place):
            place = jnp.minimum(place, reached - 1)
            return jnp.where(place < kept_x, slot_of(place), 2 * slots + place - kept_x)

        def after_y(place):
            return jnp.where(
                place < kept_y, after_x(place), 2 * slots + OVER_X + place - kept_y
            )

        return (
            [jnp.clip(slot_of(kept_x + i), 0, 2 * slots - 1) for i in range(OVER_X)]
            + [after_x(kept_y + i) for i in range(OVER_Y)]
            + [after_y(i) for i in range(STARS_CHIP)]
        )

    def star_at(chip, place):
        over_y = chip + 2 - 4 * (chip // 2)
        kept_y = choose(keep_y, chip)
        here = jnp.where(place < kept_y, chip, over_y)
        place = jnp.where(place < kept_y, place, choose(keep_y, over_y) + place - kept_y)
        over_x = here + 1 - 2 * (here % 2)
        kept_x = choose(keep_x, here)
        origin = jnp.where(place < kept_x, here, over_x)
        place = jnp.where(place < kept_x, place, choose(keep_x, over_x) + place - kept_x)
        inner = place < choose(first, origin)
        group = 2 * origin + jnp.where(inner, 0, 1)
        slot = jnp.where(inner, place, place - choose(first, origin))
        return jnp.clip(group, 0, 2 * chips - 1), jnp.clip(slot, 0, slots - 1)

    def cell_at(chip, place):
        group, slot = star_at(chip, place)
        return cells_ref[group, slot]

    def wave_at(chip, place, scale):
        group, slot = star_at(chip, place)
        band = bands_ref[group, slot]
        value = jnp.float32(0)
        for b in range(BANDS):
            length = 0.55 + 0.35 * b / (BANDS - 1)
            value = jnp.where(band == b, np.float32(scale / length), value)
        return value

    return routes, cell_at, wave_at


def aperture_widths(size, row_count, depth):
    widths = []
    for step in range(row_count // depth):
        lowest = abs(step * depth + depth - 1 - 0.5 * (size - 1))
        reach = 2 * (np.sqrt(0.25 * size * size - lowest * lowest) + 1)
        widths.append(min(size, int(-(-reach // 256) * 256)))
    return widths


def group_rows(step, depth, row_count, lanes):
    return [
        pl.ds(pl.multiple_of(lane * row_count + step * depth, depth), depth)
        for lane in range(lanes)
    ]


def focal_kernel(
    groups, lanes, count_hbm, cells_hbm, bands_hbm, coef_hbm, maps_ref, cot_ref, half_ref,
    turns_out, xr, xi, left_ref, right_ref, maps_buf, stage, raw, pool, x_stage, y_stage, ct, ct_turned,
    spread, yr, yi, route_ref, count_ref, cells_ref, bands_ref, coef_ref,
    small_sem, *scratch,
):
    steps = TURN_STEPS
    small = [
        pltpu.make_async_copy(count_hbm, count_ref, small_sem.at[0]),
        pltpu.make_async_copy(cells_hbm, cells_ref, small_sem.at[1]),
        pltpu.make_async_copy(bands_hbm, bands_ref, small_sem.at[2]),
        pltpu.make_async_copy(coef_hbm, coef_ref, small_sem.at[3]),
    ]
    for copy in small:
        copy.start()
    chunks = pool.shape[0]
    x_got, y_got = scratch[:chunks], scratch[chunks : 2 * chunks]
    (
        m_sem, t_local, t_send, t_recv, r_local, r_send, r_recv, x_send, x_recv,
        y_send, y_recv, z_local, z_send, z_recv,
    ) = scratch[2 * chunks :]
    row = lax.axis_index("row")
    me = lax.axis_index("star")
    core = me % 2
    chip = me // 2
    twin = me + 1 - 2 * core
    over_x = me + 2 - 4 * (chip % 2)
    over_y = me + 4 - 8 * (me // 4)
    map_count, row_count, size = maps_ref.shape
    depth = row_count // steps
    half = size // 2
    quarter = size // RADIX
    slots = raw.shape[0] // 2
    places = [(d, e) for e in range(2) for d in range(lanes)][1:]
    peers = [{"row": (row + d) % lanes, "star": twin if e else me} for d, e in places]
    peers_all = peers + [{"star": over_x}, {"star": over_y}]
    greet(peers_all)

    slot_range = pl.ds(core * slots, slots)
    some = slots // 2
    other = 1 - core
    raw_own = pltpu.make_async_copy(
        cot_ref.at[:, :, pl.ds(pl.multiple_of(core * half, half), half)], raw.at[slot_range], r_local
    )
    raw_twin = [
        send(
            cot_ref.at[
                pl.ds(part * some, some), :, pl.ds(pl.multiple_of(other * half, half), half)
            ],
            raw.at[pl.ds(core * slots + part * some, some)],
            r_send.at[part],
            r_recv.at[part],
            {"star": twin},
        )
        for part in range(2)
    ]
    raw_own.start()

    def fetch(step, part):
        rows = pl.ds(pl.multiple_of(step * depth + part * ROWS_STEP, ROWS_STEP), ROWS_STEP)
        return pltpu.make_async_copy(maps_ref.at[:, rows], maps_buf.at[part], m_sem.at[part])

    for part in range(depth // ROWS_STEP):
        fetch(0, part).start()
    greeted(peers_all)
    for copy in raw_twin:
        copy.start()
    for copy in small:
        copy.wait()
    routes, cell_at, wave_at = star_plan(slots, count_ref, cells_ref, bands_ref)
    places_here = [core * lanes + s for s in range(lanes)]
    cell_here = [cell_at(chip, place) for place in places_here]
    turn_here = [wave_at(chip, place, 1.0) for place in places_here]

    lines = lanes * ROWS_STEP
    wide = map_count * ROWS_STEP
    cells = lax.broadcasted_iota(jnp.int32, (ROWS_STEP, coef_ref.shape[0]), 1)
    hot = jnp.concatenate(
        [
            jnp.where(cells == cell_here[s], 1.0, 0.0).astype(BF16)
            for s in range(lanes)
        ],
        0,
    )
    coefs = jnp.dot(hot, coef_ref[...], preferred_element_type=F32).astype(BF16)
    at = lax.broadcasted_iota(jnp.int32, (map_count, wide), 0)
    to = lax.broadcasted_iota(jnp.int32, (map_count, wide), 1)
    repeat = jnp.where(to // ROWS_STEP == at, 1.0, 0.0).astype(BF16)
    repeated = jnp.dot(coefs, repeat, preferred_element_type=F32)
    at = lax.broadcasted_iota(jnp.int32, (lines, wide), 0)
    to = lax.broadcasted_iota(jnp.int32, (lines, wide), 1)
    spread[...] = jnp.where(at % ROWS_STEP == to % ROWS_STEP, repeated, 0.0).astype(BF16)

    widths = aperture_widths(size, row_count, depth)

    def turn_local(step):
        rows = pl.ds(pl.multiple_of(step * depth, depth), depth)
        place = pl.ds(pl.multiple_of(row * row_count + step * depth, depth), depth)
        return pltpu.make_async_copy(stage.at[row, rows], turns_out.at[place], t_local.at[step])

    def turn_copy(step, d, source, width):
        rows = pl.ds(pl.multiple_of(step * depth, depth), depth)
        place = pl.ds(pl.multiple_of(source * row_count + step * depth, depth), depth)
        cols = pl.ds((size - width) // 2, width)
        return send(
            stage.at[(row + d) % lanes, rows, cols],
            turns_out.at[place, cols],
            t_send.at[step],
            t_recv.at[step, d - 1],
            {"row": (row + d) % lanes},
        )

    def each_width(step, source, body):
        outer = jnp.where(source == 0, step, jnp.where(source == lanes - 1, steps - 1 - step, steps))
        first = 0
        for width in sorted(set(widths) | {size}):
            last = first + widths.count(width) if width < size else steps + 1

            @pl.when(jnp.logical_and(outer >= first, outer < last))
            def _():
                body(width)

            first = last

    def turns_start(step):
        turn_local(step).start()

        def start(width):
            for d in range(1, lanes):
                turn_copy(step, d, row, width).start()

        each_width(step, row, start)

    def turns_wait(step):
        turn_local(step).wait()
        rows = pl.ds(pl.multiple_of(step * depth, depth), depth)

        def sent(width):
            part = stage.at[pl.ds(0, lanes - 1), rows, pl.ds((size - width) // 2, width)]
            send(part, part, t_send.at[step], t_recv.at[step, 0], peers[0]).wait_send()

        each_width(step, row, sent)
        for d in range(1, lanes):
            source = (row + lanes - d) % lanes
            each_width(
                step, source, lambda width: turn_copy(step, d, source, width).wait_recv()
            )

    def phase_turns(step, carry):
        for part in range(depth // ROWS_STEP):
            fetch(step, part).wait()
            maps = maps_buf[part].reshape(wide, size)
            path = jnp.dot(spread[...], maps, preferred_element_type=F32)
            rows = pl.ds(pl.multiple_of(step * depth + part * ROWS_STEP, ROWS_STEP), ROWS_STEP)
            for s in range(lanes):
                turned = path[s * ROWS_STEP : (s + 1) * ROWS_STEP] * turn_here[s]
                stage[s, rows] = (turned - jnp.floor(turned + 0.5)).astype(BF16)

            @pl.when(step + 1 < steps)
            def _():
                fetch(step + 1, part).start()

        return carry

    def phase_step(step, carry):
        phase_turns(step, carry)
        turns_start(step)
        return carry

    def x_copy(c):
        return send(x_stage.at[c], x_got[c], x_send, x_recv.at[c], {"star": over_x})

    def y_copy(c):
        return send(y_stage.at[c], y_got[c], y_send, y_recv.at[c], {"star": over_y})

    tall = quarter // lanes
    piece = tall * RADIX // chunks
    parts = chunks // RADIX

    def star_piece(c, star):
        lined = pl.ds(pl.multiple_of(c * piece, piece), piece)
        return raw.at[2 * RADIX + star, lined]

    def z_target(c):
        kind, part = c // parts, c % parts
        return ct.at[
            kind,
            pl.ds(pl.multiple_of(row * tall + part * piece, piece), piece),
            pl.ds(pl.multiple_of(core * half, half), half),
        ]

    def z_local_copy(c):
        return pltpu.make_async_copy(star_piece(c, core * lanes + row), z_target(c), z_local.at[c])

    def z_start(c):
        z_local_copy(c).start()
        for d, e in places:
            star = (core + e) % 2 * lanes + (row + d) % lanes
            peer = {"row": (row + d) % lanes, "star": twin if e else me}
            send(star_piece(c, star), z_target(c), z_send, z_recv.at[c], peer).start()

    def z_arrival(c):
        sized = raw.at[pl.ds(0, len(places)), pl.ds(0, piece)]
        return send(sized, sized, z_send, z_recv.at[c], peers[0])

    def sort_slot(slot, carry):
        sorted_rows = jnp.dot(sort, raw[slot], preferred_element_type=F32).astype(BF16)
        for c in range(chunks):
            pool[c, slot] = sorted_rows[c * piece : (c + 1) * piece]
        return carry

    phase_turns(0, 0)
    for i, entry in enumerate(routes(chip)):
        route_ref[i] = entry
    at = lax.broadcasted_iota(jnp.int32, (row_count, row_count), 0)
    to = lax.broadcasted_iota(jnp.int32, (row_count, row_count), 1)
    sort = jnp.where(at % tall * RADIX + at // tall == to, 1.0, 0.0).astype(BF16)
    turns_start(0)
    raw_own.wait()
    lax.fori_loop(core * slots, core * slots + slots, sort_slot, 0)
    lax.fori_loop(1, EARLY_STEPS, phase_step, 0)
    for part in range(2):
        raw_twin[part].wait()
        begin = other * slots + part * some
        lax.fori_loop(begin, begin + some, sort_slot, 0)
    for c in range(chunks):
        for i in range(OVER_X):
            x_stage[c, i] = pool[c, route_ref[i]]
        x_copy(c).start()

    lax.fori_loop(EARLY_STEPS, steps, phase_step, 0)
    right_tables(half_ref, right_ref)
    left_tables(half_ref, left_ref)
    at = lax.broadcasted_iota(jnp.int32, (quarter, half), 0)
    to = lax.broadcasted_iota(jnp.int32, (quarter, half), 1)
    for k in range(RADIX):
        for side in range(2):
            raw[2 * k + side] = jnp.where(at * RADIX + k == to + side * half, 1.0, 0.0).astype(BF16)

    def pick_x(c, index):
        mine = pool[c, jnp.clip(index, 0, 2 * slots - 1)]
        far = x_got[c][jnp.clip(index - 2 * slots, 0, OVER_X - 1)]
        return jnp.where(index < 2 * slots, mine, far)

    def route_y(c):
        x_copy(c).wait_recv()
        for i in range(OVER_Y):
            y_stage[c, i] = pick_x(c, route_ref[OVER_X + i])
        y_copy(c).start()

    def route_z(c):
        y_copy(c).wait_recv()
        for i in range(STARS_CHIP):
            index = route_ref[OVER_X + OVER_Y + i]
            far = y_got[c][jnp.clip(index - 2 * slots - OVER_X, 0, OVER_Y - 1)]
            near = pick_x(c, jnp.minimum(index, 2 * slots + OVER_X - 1))
            raw[2 * RADIX + i, c * piece : (c + 1) * piece] = jnp.where(
                index < 2 * slots + OVER_X, near, far
            )
        z_start(c)

    blocks = [slice(m * quarter, (m + 1) * quarter) for m in range(RADIX)]
    centre = 0.5 * (size - 1)
    scale = 1.0 / size
    tile = lanes * depth

    def forward_columns(step, carry):
        turns_wait(step)
        rows = group_rows(step, depth, row_count, lanes)
        turns = jnp.concatenate([turns_out[r, :] for r in rows], 0)
        cosine, sine = turn_cos_sin(turns.astype(F32))
        line = lax.broadcasted_iota(jnp.int32, (tile, size), 0)
        place = line // depth * row_count + line % depth + step * depth
        row_pos = place.astype(F32) - centre
        col_pos = lax.broadcasted_iota(jnp.int32, (tile, size), 1).astype(F32) - centre
        inside = row_pos * row_pos + col_pos * col_pos <= 0.25 * size * size
        real = jnp.where(inside, cosine, 0.0)
        imag = jnp.where(inside, sine, 0.0)
        mixed_real, mixed_imag = butterfly(
            [real[:, b] for b in blocks], [imag[:, b] for b in blocks], -1
        )
        for k in range(RADIX):
            both = jnp.concatenate([mixed_real[k].astype(BF16), mixed_imag[k].astype(BF16)], 1)
            made = jnp.dot(both, right_ref[k], preferred_element_type=F32).astype(BF16)
            for lane in range(lanes):
                lined = slice(lane * depth, (lane + 1) * depth)
                yr[rows[lane], blocks[k]] = made[lined, :quarter]
                yi[rows[lane], blocks[k]] = made[lined, quarter:]
        return carry

    def focal(kind, carry):
        for part in range(parts):
            z_local_copy(kind * parts + part).wait()
            z_arrival(kind * parts + part).wait_recv()
        for side in range(2):
            cols = slice(side * half, (side + 1) * half)
            order = jnp.concatenate([raw[2 * k + side] for k in range(RADIX)], 0)
            turned = lax.dot_general(
                order, ct[kind, :, cols], (((1,), (1,)), ((), ())), preferred_element_type=F32
            )
            ct_turned[...] = turned if side == 0 else ct_turned[...] + turned
        cols = pl.ds(pl.multiple_of(kind * quarter, quarter), quarter)
        mixed_real, mixed_imag = butterfly(
            [yr[b, cols].astype(F32) for b in blocks],
            [yi[b, cols].astype(F32) for b in blocks],
            -1,
        )
        back_real, back_imag = [], []
        for k in range(RADIX):
            both = jnp.concatenate([mixed_real[k].astype(BF16), mixed_imag[k].astype(BF16)], 0)
            field = jnp.dot(left_ref[k], both, preferred_element_type=F32)
            weight = ct_turned[blocks[k], :] * (2.0 * scale)
            grad = (field * jnp.concatenate([weight, weight], 0)).astype(BF16)
            back = jnp.dot(right_ref[k], grad, preferred_element_type=F32)
            back_real.append(back[:quarter])
            back_imag.append(back[quarter:])
        spec_real, spec_imag = butterfly(back_real, back_imag, 1)
        for m in range(RADIX):
            xr[blocks[m], cols] = (spec_real[m] * scale).astype(BF16)
            xi[blocks[m], cols] = (spec_imag[m] * scale).astype(BF16)
        return carry

    column_plan = {chunks // 4: (0, 3), 3 * chunks // 8: (3, 6), 5 * chunks // 8: (6, 8)}
    focal_plan = {chunks - 2: 0, chunks - 1: 1}
    for c in range(chunks):
        route_y(c)
        if c in column_plan:
            first, last = column_plan[c]
            lax.fori_loop(first * steps // 8, last * steps // 8, forward_columns, 0)
        if c in focal_plan:
            focal(focal_plan[c], 0)
        route_z(c)
    lax.fori_loop(len(focal_plan), RADIX, focal, 0)
    sized = raw.at[pl.ds(0, len(places))]
    send(sized, sized, z_send, z_recv.at[0], peers[0]).wait_send()
    send(x_stage, x_stage, x_send, x_recv.at[0], {"star": over_x}).wait_send()
    send(y_stage, y_stage, y_send, y_recv.at[0], {"star": over_y}).wait_send()


def focal_fields(counts, cells, bands, coef_table, feature_maps, cotangent, halves, groups, lanes):
    map_count, row_count, size = feature_maps.shape
    slots = cotangent.shape[0]
    depth = row_count // TURN_STEPS
    half, quarter = size // 2, size // RADIX
    chunks = ROUTE_CHUNKS
    piece = row_count // chunks
    dma = pltpu.SemaphoreType.DMA
    smem = pl.BlockSpec(memory_space=pltpu.SMEM)
    vmem = pl.BlockSpec(memory_space=pltpu.VMEM)
    hbm = pl.BlockSpec(memory_space=pl.ANY)
    square = pltpu.VMEM((size, size), BF16)
    return pl.pallas_call(
        functools.partial(focal_kernel, groups, lanes),
        out_shape=(square,) * 3 + (pltpu.VMEM((RADIX, half, half), BF16),),
        in_specs=[pl.BlockSpec(memory_space=pltpu.HBM)] * 4 + [hbm, hbm, vmem],
        out_specs=(vmem,) * 4,
        scratch_shapes=[
            pltpu.VMEM((RADIX, half, half), BF16),
            pltpu.VMEM((depth // ROWS_STEP, map_count, ROWS_STEP, size), BF16),
            pltpu.VMEM((lanes, row_count, size), BF16),
            pltpu.VMEM((2 * slots, row_count, half), BF16),
            pltpu.VMEM((chunks, 2 * slots, piece, half), BF16),
            pltpu.VMEM((chunks, OVER_X, piece, half), BF16),
            pltpu.VMEM((chunks, OVER_Y, piece, half), BF16),
            pltpu.VMEM((RADIX, quarter, size), BF16),
            pltpu.VMEM((size, quarter), F32),
            pltpu.VMEM((lanes * ROWS_STEP, map_count * ROWS_STEP), BF16),
            pltpu.VMEM((size, size), BF16),
            pltpu.VMEM((size, size), BF16),
        ]
        + [
            pltpu.SMEM((OVER_X + OVER_Y + STARS_CHIP,), jnp.int32),
            pltpu.SMEM(counts.shape, jnp.int32),
            pltpu.SMEM(cells.shape, jnp.int32),
            pltpu.SMEM(bands.shape, jnp.int32),
            pltpu.VMEM(coef_table.shape, BF16),
            dma((4,)),
        ]
        + [pltpu.VMEM((OVER_X, piece, half), BF16)] * chunks
        + [pltpu.VMEM((OVER_Y, piece, half), BF16)] * chunks
        + [
            dma((depth // ROWS_STEP,)),
            dma((TURN_STEPS,)),
            dma((TURN_STEPS,)),
            dma((TURN_STEPS, lanes - 1)),
            dma,
            dma((2,)),
            dma((2,)),
            dma,
            dma((chunks,)),
            dma,
            dma((chunks,)),
            dma((chunks,)),
            dma,
            dma((chunks,)),
        ],
        compiler_params=pltpu.CompilerParams(
            collective_id=0, has_side_effects=True, vmem_limit_bytes=K1_LIMIT << 20
        ),
        name="focal_fields",
    )(counts, cells, bands, coef_table, feature_maps, cotangent, halves)


def gradient_kernel(
    groups, lanes, count_ref, cells_ref, bands_ref, coef_ref, turns_ref, xr, xi, left, maps_ref,
    grad_out, coef_out, cell_ref, gathered, away, maps_buf, score, weights, row_part, star_part,
    m_sem, z_send, z_recv, p_send, p_recv, c_send, c_recv, sr_send, sr_recv, ss_send, ss_recv,
):
    row = lax.axis_index("row")
    me = lax.axis_index("star")
    steps = GATHER_STEPS
    share = grad_out.shape[0]
    map_count, row_count, size = maps_ref.shape
    depth = row_count // steps
    parts = depth // ROWS_STEP
    quarter = size // RADIX
    total = groups * lanes
    core = me + 1 - 2 * (me % 2)
    across = me + 2 - 4 * ((me // 2) % 2)
    along = me + 4 - 8 * ((me // 4) % 2)
    corner = across + 4 - 8 * ((me // 4) % 2)
    row_peers = [{"row": (row + d) % lanes} for d in range(1, lanes)]
    star_peers = [{"star": (me + d) % groups} for d in range(1, groups)]
    to_core, to_across, to_along = {"star": core}, {"star": across}, {"star": along}
    greet(row_peers + star_peers)
    half_lanes = lanes // 2

    def fetch(step, part):
        rows = pl.ds(pl.multiple_of(step * depth + part * ROWS_STEP, ROWS_STEP), ROWS_STEP)
        return pltpu.make_async_copy(maps_ref.at[:, rows], maps_buf.at[part], m_sem.at[part])

    for part in range(parts):
        fetch(0, part).start()

    slots = cells_ref.shape[1]
    routes, cell_at, wave_at = star_plan(slots, count_ref, cells_ref, bands_ref)
    wave = wave_at(me // 2, me % 2 * lanes + row, 2.0 * np.pi)

    def cell_of(group, d):
        return cell_ref[group * lanes + (row + lanes - d) % lanes]

    blocks = [slice(m * quarter, (m + 1) * quarter) for m in range(RADIX)]
    centre = 0.5 * (size - 1)
    tile = lanes * depth

    def rows_at(step):
        return pl.ds(pl.multiple_of(step * depth, depth), depth)

    def block(group, step, first=0, count=lanes):
        return gathered.at[group, pl.ds(first, count), rows_at(step)]

    def z_start(step):
        for d in range(1, lanes):
            send(
                away.at[d - 1, rows_at(step)],
                gathered.at[me, d, rows_at(step)],
                z_send,
                z_recv.at[step],
                row_peers[d - 1],
            ).start()

    def plane(step, way, part, peer):
        send(part, part, p_send, p_recv.at[step, way], peer).start()

    def twin(step, part):
        send(part, part, c_send, c_recv.at[step], to_core).start()

    def sides(step, first, count):
        part = block(me, step, first, count)
        plane(step, 0, part, to_across)
        plane(step, 0, part, to_along)
        twin(step, part)

    def arrived(part, sem):
        send(part, part, p_send, sem, to_core).wait_recv()

    def columns_step(step):
        firsts = [(row + d) % lanes * row_count + step * depth for d in range(lanes)]
        rows = [pl.ds(pl.multiple_of(first, depth), depth) for first in firsts]
        turns = jnp.concatenate([turns_ref[r, :] for r in rows], 0)
        cosine, sine = turn_cos_sin(turns.astype(F32))
        line = lax.broadcasted_iota(jnp.int32, (tile, size), 0)
        place = (line // depth + row) % lanes * row_count + line % depth + step * depth
        row_pos = place.astype(F32) - centre
        col_pos = lax.broadcasted_iota(jnp.int32, (tile, size), 1).astype(F32) - centre
        inside = row_pos * row_pos + col_pos * col_pos <= 0.25 * size * size
        real = jnp.where(inside, cosine, 0.0)
        imag = jnp.where(inside, sine, 0.0)
        part_real, part_imag = [], []
        for k in range(RADIX):
            both = jnp.concatenate(
                [
                    jnp.concatenate([xr[r, blocks[k]] for r in rows], 0),
                    jnp.concatenate([xi[r, blocks[k]] for r in rows], 0),
                ],
                1,
            )
            made = jnp.dot(both, left[k], preferred_element_type=F32)
            part_real.append(made[:, :quarter])
            part_imag.append(made[:, quarter:])
        grad_real, grad_imag = butterfly(part_real, part_imag, 1)
        for m in range(RADIX):
            grad = real[:, blocks[m]] * grad_imag[m] - imag[:, blocks[m]] * grad_real[m]
            grad = (wave * grad).astype(BF16)
            gathered[me, 0, rows_at(step), blocks[m]] = grad[:depth]
            for d in range(1, lanes):
                away[d - 1, rows_at(step), blocks[m]] = grad[d * depth : (d + 1) * depth]

    def score_step(step):
        for part in range(parts):
            fetch(step, part).wait()
            rows = pl.ds(pl.multiple_of(step * depth + part * ROWS_STEP, ROWS_STEP), ROWS_STEP)
            grads = gathered[me, :, rows].reshape(lanes * ROWS_STEP, size)
            maps = maps_buf[part].reshape(map_count * ROWS_STEP, size)
            score[...] += lax.dot_general(
                maps, grads, (((1,), (1,)), ((), ())), preferred_element_type=F32
            )

            @pl.when(step + 1 < steps)
            def _():
                fetch(step + 1, part).start()

    def sums_step(step):
        for part in range(parts):
            rows = pl.ds(pl.multiple_of(step * depth + part * ROWS_STEP, ROWS_STEP), ROWS_STEP)
            grads = gathered[:, :, rows].reshape(wide, size)
            made = jnp.dot(weights[...], grads, preferred_element_type=F32)
            grad_out[:, rows] = made.reshape(share, ROWS_STEP, size)

    def row_copies():
        return [
            send(row_part.at[row], row_part.at[row], sr_send.at[d], sr_recv.at[d], row_peers[d])
            for d in range(lanes - 1)
        ]

    def star_copies():
        return [
            send(star_part.at[me], star_part.at[me], ss_send.at[d], ss_recv.at[d], star_peers[d])
            for d in range(groups - 1)
        ]

    def scores_rows():
        lined = score[...]
        at = lax.broadcasted_iota(jnp.int32, lined.shape, 0)
        to = lax.broadcasted_iota(jnp.int32, lined.shape, 1)
        kept = jnp.where(at % ROWS_STEP == to % ROWS_STEP, lined, 0.0)
        kept = jnp.sum(kept.reshape(map_count, ROWS_STEP, lined.shape[1]), axis=1)
        to = lax.broadcasted_iota(jnp.int32, kept.shape, 1)
        cell = lax.broadcasted_iota(jnp.int32, row_part.shape[1:], 1)
        part = jnp.zeros(row_part.shape[1:], F32)
        for d in range(lanes):
            value = jnp.sum(jnp.where(to // ROWS_STEP == d, kept, 0.0), axis=1, keepdims=True)
            part += jnp.where(cell == cell_of(me, d), value, 0.0)
        row_part[row] = part
        for copy in row_copies():
            copy.start()

    def scores_stars():
        for copy in row_copies():
            copy.wait()
        star_part[me] = jnp.sum(row_part[...], axis=0)
        for copy in star_copies():
            copy.start()

    def scores_end():
        for copy in star_copies():
            copy.wait()
        summed = jnp.sum(star_part[...], axis=0) * (1.0 / (8 * size))
        coef_out[...] = summed.T[: coef_out.shape[0]]

    def between(tick, lag, body):
        @pl.when(jnp.logical_and(tick >= lag, tick < steps + lag))
        def _():
            body(tick - lag)

    def compute(step, carry):
        columns_step(step)
        sides(step, 0, 1)
        return carry

    def own_arrived(step):
        sized = away.at[:, rows_at(step)]
        arrived(sized, z_recv.at[step])

        @pl.when(step + Z_AHEAD < steps)
        def _():
            z_start(step + Z_AHEAD)

        sides(step, 1, lanes - 1)

    def sides_arrived(step):
        arrived(gathered.at[pl.ds(0, 2), :, rows_at(step)], p_recv.at[step, 0])
        plane(step, 1, block(across, step, 0, half_lanes), to_along)
        plane(step, 1, block(along, step, half_lanes, lanes - half_lanes), to_across)
        twin(step, block(across, step))
        twin(step, block(along, step))

    def corners_arrived(step):
        arrived(gathered.at[pl.ds(0, 1), :, rows_at(step)], p_recv.at[step, 1])
        twin(step, block(corner, step))

    def all_arrived(step):
        arrived(gathered.at[pl.ds(0, groups // 2), :, rows_at(step)], c_recv.at[step])
        sums_step(step)

    def tick_body(tick, carry):
        between(tick, 0, own_arrived)
        between(tick, SIDES_LAG, sides_arrived)
        between(tick, SIDES_LAG + CORNERS_LAG, corners_arrived)
        between(tick, 0, score_step)

        @pl.when(tick == steps)
        def _():
            scores_rows()

        @pl.when(tick == steps + 1)
        def _():
            scores_stars()

        between(tick, SIDES_LAG + CORNERS_LAG + 1, all_arrived)
        return carry

    columns_step(0)
    greeted(row_peers + star_peers)
    z_start(0)
    sides(0, 0, 1)
    for step in range(1, Z_AHEAD):
        compute(step, 0)
        z_start(step)
    lax.fori_loop(Z_AHEAD, steps, compute, 0)
    def cell_fill(chip, carry):
        for place in range(STARS_CHIP):
            cell_ref[chip * STARS_CHIP + place] = cell_at(chip, place)
        return carry

    lax.fori_loop(0, total // STARS_CHIP, cell_fill, 0)
    at = lax.broadcasted_iota(jnp.int32, (total, coef_ref.shape[0]), 0)
    to = lax.broadcasted_iota(jnp.int32, (total, coef_ref.shape[0]), 1)
    wanted = jnp.zeros_like(at)
    for group in range(groups):
        for d in range(lanes):
            wanted = jnp.where(at == group * lanes + d, cell_of(group, d), wanted)
    hot = jnp.where(to == wanted, 1.0, 0.0).astype(BF16)
    rows_of = jnp.dot(hot, coef_ref[...], preferred_element_type=F32).astype(BF16)
    lines = share * ROWS_STEP
    wide = total * ROWS_STEP
    at = lax.broadcasted_iota(jnp.int32, (lines, map_count), 0)
    to = lax.broadcasted_iota(jnp.int32, (lines, map_count), 1)
    mine = jnp.where(to == me * share + at // ROWS_STEP, 1.0, 0.0).astype(BF16)
    columns = lax.dot_general(
        mine, rows_of, (((1,), (1,)), ((), ())), preferred_element_type=F32
    ).astype(BF16)
    at = lax.broadcasted_iota(jnp.int32, (total, wide), 0)
    to = lax.broadcasted_iota(jnp.int32, (total, wide), 1)
    repeat = jnp.where(to // ROWS_STEP == at, 1.0, 0.0).astype(BF16)
    repeated = jnp.dot(columns, repeat, preferred_element_type=F32)
    at = lax.broadcasted_iota(jnp.int32, (lines, wide), 0)
    to = lax.broadcasted_iota(jnp.int32, (lines, wide), 1)
    weights[...] = jnp.where(at % ROWS_STEP == to % ROWS_STEP, repeated, 0.0).astype(BF16)
    score[...] = jnp.zeros_like(score)
    lax.fori_loop(0, steps + SIDES_LAG + CORNERS_LAG + 1, tick_body, 0)
    scores_end()
    send(away, away, z_send, z_recv.at[0], to_core).wait_send()
    three, four = gathered.at[pl.ds(0, 3)], gathered.at[pl.ds(0, groups // 2)]
    send(three, three, p_send, z_recv.at[0], to_core).wait_send()
    send(four, four, c_send, z_recv.at[0], to_core).wait_send()


def gradient_sums(counts, cells, bands, coef_table, turns, spec_real, spec_imag, left, feature_maps, groups, lanes):
    map_count, row_count, size = feature_maps.shape
    cell_count = coef_table.shape[0]
    share = map_count // groups
    depth = row_count // GATHER_STEPS
    dma = pltpu.SemaphoreType.DMA
    smem = pl.BlockSpec(memory_space=pltpu.SMEM)
    vmem = pl.BlockSpec(memory_space=pltpu.VMEM)
    hbm = pl.BlockSpec(memory_space=pl.ANY)
    padded = -(-cell_count // 128) * 128
    return pl.pallas_call(
        functools.partial(gradient_kernel, groups, lanes),
        out_shape=(
            pltpu.VMEM((share, row_count, size), F32),
            jax.ShapeDtypeStruct((cell_count, map_count), F32),
        ),
        in_specs=[smem, smem, smem, vmem, vmem, vmem, vmem, vmem, hbm],
        out_specs=(vmem, vmem),
        scratch_shapes=[
            pltpu.SMEM((groups * lanes,), jnp.int32),
            pltpu.VMEM((groups, lanes, row_count, size), BF16),
            pltpu.VMEM((lanes - 1, row_count, size), BF16),
            pltpu.VMEM((depth // ROWS_STEP, map_count, ROWS_STEP, size), BF16),
            pltpu.VMEM((map_count * ROWS_STEP, lanes * ROWS_STEP), F32),
            pltpu.VMEM((share * ROWS_STEP, groups * lanes * ROWS_STEP), BF16),
            pltpu.VMEM((lanes, map_count, padded), F32),
            pltpu.VMEM((groups, map_count, padded), F32),
            dma((depth // ROWS_STEP,)),
            dma,
            dma((GATHER_STEPS,)),
            dma,
            dma((GATHER_STEPS, 2)),
            dma,
            dma((GATHER_STEPS,)),
            dma((lanes - 1,)),
            dma((lanes - 1,)),
            dma((groups - 1,)),
            dma((groups - 1,)),
        ],
        compiler_params=pltpu.CompilerParams(
            collective_id=1, has_side_effects=True, vmem_limit_bytes=K2_LIMIT << 20
        ),
        name="gradient_sums",
    )(counts, cells, bands, coef_table, turns, spec_real, spec_imag, left, feature_maps)


def star_devices(feature_maps, coef_table, star_counts, star_cells, star_bands, psf_cotangent):
    groups = lax.axis_size("star")
    lanes = lax.axis_size("row")
    size = feature_maps.shape[2]
    halves = half_tables(size)
    turns, spec_real, spec_imag, left = focal_fields(
        star_counts, star_cells, star_bands, coef_table, feature_maps, psf_cotangent, halves, groups, lanes
    )
    return gradient_sums(
        star_counts, star_cells, star_bands, coef_table, turns, spec_real, spec_imag, left, feature_maps,
        groups, lanes,
    )


def solution(mesh):
    placed = (P(None, "row", None), P(), P(), P(), P(), P("star", "row", None))
    fits = mesh.shape["row"] == LIVE_DEV and mesh.shape["star"] == PLANE_DEV
    device = star_devices if fits else per_device
    return jax.shard_map(
        device,
        mesh=mesh,
        in_specs=placed,
        out_specs=(P("star", "row", None), P()),
        check_vma=False,
    )
```

```python
import functools

import jax
import jax.numpy as jnp
import numpy as np
from jax import lax
from jax.experimental import pallas as pl
from jax.experimental.pallas import tpu as pltpu
from jax.sharding import PartitionSpec as P

BANDS = 8
LIVE_DEV = 4
PLANE_DEV = 8
RADIX = 4
ROWS_STEP = 16
TURN_STEPS = 8
EARLY_STEPS = 3
ROUTE_CHUNKS = 8
GATHER_STEPS = 8
Z_AHEAD = 2
SIDES_LAG = 2
CORNERS_LAG = 2
OVER_X = 11
OVER_Y = 6
STARS_CHIP = 8
K1_LIMIT = 47
K2_LIMIT = 34
F32 = jnp.float32
BF16 = jnp.bfloat16


def fourier_tables(pupil_size):
    index_row = jnp.arange(pupil_size, dtype=jnp.int32)
    products = index_row[:, None] * index_row[None, :] % pupil_size
    angles = 2.0 * jnp.pi / pupil_size * products.astype(jnp.float32)
    return (jnp.cos(angles).astype(jnp.bfloat16), (-jnp.sin(angles)).astype(jnp.bfloat16))


def aperture_rows(first_row, row_count, pupil_size):
    centre = 0.5 * (pupil_size - 1)
    row_pos = (first_row + jnp.arange(row_count, dtype=jnp.int32)).astype(jnp.float32) - centre
    col_pos = jnp.arange(pupil_size, dtype=jnp.int32).astype(jnp.float32) - centre
    radius = row_pos[:, None] * row_pos[:, None] + col_pos[None, :] * col_pos[None, :]
    return jnp.where(radius <= 0.25 * pupil_size * pupil_size, 1.0, 0.0).astype(jnp.float32)


def wave_numbers(band_ids):
    wavelength = 0.55 + 0.35 * band_ids.astype(jnp.float32) / (BANDS - 1)
    return 2.0 * jnp.pi / wavelength


def table_pick(values, indices):
    positions = jnp.arange(values.shape[0], dtype=jnp.int32)
    chosen = jnp.where(positions[None, :] == indices[:, None], values[None, :], 0)
    return jnp.sum(chosen, axis=1)


def per_device(feature_maps, coef_table, star_counts, star_cells, star_bands, psf_cotangent):
    groups = lax.axis_size("star")
    my_group = lax.axis_index("star")
    slot_count = psf_cotangent.shape[0]
    map_count, row_count, pupil_size = feature_maps.shape
    group_ends = jnp.cumsum(star_counts)
    group_starts = group_ends - star_counts
    flat_cells = star_cells.reshape(-1)
    flat_bands = star_bands.reshape(-1)
    cell_count = coef_table.shape[0]
    capacity = -(-slot_count // groups)
    targets = jnp.arange(groups, dtype=jnp.int32)
    lane_index = jnp.arange(capacity, dtype=jnp.int32)
    my_start = table_pick(group_starts, my_group[None])
    my_count = table_pick(star_counts, my_group[None])
    first_slot = (targets - my_start) % groups
    send_slot = (first_slot[:, None] + lane_index[None, :] * groups).reshape(-1)
    valid_mask = send_slot < my_count
    picked = jnp.take(psf_cotangent, jnp.minimum(send_slot, slot_count - 1), axis=0)
    outgoing = jnp.where(valid_mask[:, None, None], picked, jnp.zeros_like(picked))
    incoming = lax.all_to_all(outgoing, "star", split_axis=0, concat_axis=0, tiled=True)
    star_rank = my_group + jnp.arange(LIVE_DEV, dtype=jnp.int32) * groups
    owner_group = jnp.sum((group_ends[None, :] <= star_rank[:, None]).astype(jnp.int32), axis=1)
    within = star_rank - table_pick(group_starts, owner_group)
    live_mask = jnp.ones((LIVE_DEV,), dtype=bool)
    owner_group, within, live_mask = (owner_group, within, live_mask)
    cotangent = jnp.take(incoming, owner_group * capacity + within // groups, axis=0)
    slot_index = owner_group * slot_count + within
    cell_ids = table_pick(flat_cells, slot_index)
    band_ids = table_pick(flat_bands, slot_index)
    cell_hot = cell_ids[:, None] == jnp.arange(cell_count, dtype=jnp.int32)[None, :]
    coef_rows = jnp.dot(
        cell_hot.astype(jnp.bfloat16), coef_table, preferred_element_type=jnp.float32
    ).astype(jnp.bfloat16)
    flat_maps = feature_maps.reshape(map_count, row_count * pupil_size)
    path_error = jnp.dot(coef_rows, flat_maps, preferred_element_type=jnp.float32).reshape(
        -1, row_count, pupil_size
    )
    wave_number = wave_numbers(band_ids)
    phase_angle = wave_number[:, None, None] * path_error
    aperture = aperture_rows(lax.axis_index("row") * row_count, row_count, pupil_size)
    cos_phase = jnp.cos(phase_angle)
    sin_phase = jnp.sin(phase_angle)
    pupil_field = jnp.stack([aperture * cos_phase, aperture * sin_phase], 1).astype(jnp.bfloat16)
    cos_table, sin_table = fourier_tables(pupil_size)
    inverse = 1.0 / pupil_size
    along_cos = jnp.einsum(
        "sarc,cv->sarv", pupil_field, cos_table, preferred_element_type=jnp.float32
    )
    along_sin = jnp.einsum(
        "sarc,cv->sarv", pupil_field, sin_table, preferred_element_type=jnp.float32
    )
    column_field = jnp.stack(
        [along_cos[:, 0] - along_sin[:, 1], along_sin[:, 0] + along_cos[:, 1]], 1
    ).astype(jnp.bfloat16)
    pieces = lax.all_to_all(column_field, "row", split_axis=3, concat_axis=2, tiled=True)
    row_cos = jnp.einsum("sarv,ru->savu", pieces, cos_table, preferred_element_type=jnp.float32)
    row_sin = jnp.einsum("sarv,ru->savu", pieces, sin_table, preferred_element_type=jnp.float32)
    real_part = (row_cos[:, 0] - row_sin[:, 1]) * inverse
    imag_part = (row_sin[:, 0] + row_cos[:, 1]) * inverse
    focal_field = jnp.stack([real_part, imag_part], 1)
    weight = jnp.where(live_mask, 2.0, 0.0).astype(jnp.float32)[:, None, None, None]
    focal_grad = (weight * cotangent.astype(jnp.float32)[:, None] * focal_field).astype(
        jnp.bfloat16
    )
    back_cos = jnp.einsum(
        "savu,ur->savr", focal_grad, cos_table, preferred_element_type=jnp.float32
    )
    back_sin = jnp.einsum(
        "savu,ur->savr", focal_grad, sin_table, preferred_element_type=jnp.float32
    )
    spectrum_grad = jnp.stack(
        [(back_cos[:, 0] + back_sin[:, 1]) * inverse, (back_cos[:, 1] - back_sin[:, 0]) * inverse],
        1,
    ).astype(jnp.bfloat16)
    pieces = lax.all_to_all(spectrum_grad, "row", split_axis=3, concat_axis=2, tiled=True)
    col_cos = jnp.einsum("savr,vc->sarc", pieces, cos_table, preferred_element_type=jnp.float32)
    col_sin = jnp.einsum("savr,vc->sarc", pieces, sin_table, preferred_element_type=jnp.float32)
    pupil_grad = jnp.stack([col_cos[:, 0] + col_sin[:, 1], col_cos[:, 1] - col_sin[:, 0]], 1)
    phase_grad = aperture * (cos_phase * pupil_grad[:, 1] - sin_phase * pupil_grad[:, 0])
    path_grad = (
        (wave_number[:, None, None] * phase_grad)
        .astype(jnp.bfloat16)
        .reshape(-1, row_count * pupil_size)
    )
    map_scores = lax.dot_general(
        path_grad, flat_maps, (((1,), (1,)), ((), ())), preferred_element_type=jnp.float32
    )
    coef_part = lax.dot_general(
        cell_hot.astype(jnp.float32),
        map_scores * (1.0 / (8 * pupil_size)),
        (((0,), (0,)), ((), ())),
        precision=lax.Precision.HIGHEST,
    )
    coef_grad = lax.psum(coef_part, ("star", "row"))
    share = map_count // groups
    map_grad = lax.psum_scatter(
        lax.dot_general(
            coef_rows, path_grad, (((0,), (0,)), ((), ())), preferred_element_type=jnp.float32
        ),
        "star",
        scatter_dimension=0,
        tiled=True,
    )
    return (map_grad.reshape(share, row_count, pupil_size), coef_grad)


def half_tables(size):
    quarter = size // RADIX
    place = np.arange(quarter)[None, :, None]
    freq = RADIX * np.arange(quarter)[None, None, :] + np.arange(RADIX)[:, None, None]
    angle = 2.0 * np.pi / size * ((place * freq) % size)
    cosine, sine = np.cos(angle), -np.sin(angle)
    table = np.concatenate([cosine, sine], 2).astype(np.float32)
    return jnp.asarray(table.astype(jnp.bfloat16))


def turn_cos_sin(turns):
    half = turns * np.float32(np.pi)
    square = half * half
    sine = jnp.full_like(square, -1.0 / 39916800.0)
    for term in (1.0 / 362880.0, -1.0 / 5040.0, 1.0 / 120.0, -1.0 / 6.0, 1.0):
        sine = sine * square + np.float32(term)
    sine = sine * half
    cosine = jnp.full_like(square, 1.0 / 479001600.0)
    for term in (-1.0 / 3628800.0, 1.0 / 40320.0, -1.0 / 720.0, 1.0 / 24.0, -0.5, 1.0):
        cosine = cosine * square + np.float32(term)
    return 1.0 - 2.0 * sine * sine, 2.0 * sine * cosine


def butterfly(real, imag, sign):
    sr, dr = real[0] + real[2], real[0] - real[2]
    si, di = imag[0] + imag[2], imag[0] - imag[2]
    tr, er = real[1] + real[3], real[1] - real[3]
    ti, ei = imag[1] + imag[3], imag[1] - imag[3]
    if sign < 0:
        er, ei = -er, -ei
    return (
        [sr + tr, dr - ei, sr - tr, dr + ei],
        [si + ti, di + er, si - ti, di - er],
    )


def greet(peers):
    barrier = pltpu.get_barrier_semaphore()
    for peer in peers:
        pl.semaphore_signal(barrier, inc=1, device_id=peer, device_id_type=pl.DeviceIdType.MESH)


def greeted(peers):
    pl.semaphore_wait(pltpu.get_barrier_semaphore(), len(peers))


def send(source, target, send_sem, recv_sem, peer):
    return pltpu.make_async_remote_copy(
        src_ref=source,
        dst_ref=target,
        send_sem=send_sem,
        recv_sem=recv_sem,
        device_id=peer,
        device_id_type=pl.DeviceIdType.MESH,
    )


def right_tables(half_ref, whole_ref):
    quarter = half_ref.shape[1]
    for k in range(RADIX):
        cosine, sine = half_ref[k, :, :quarter], half_ref[k, :, quarter:]
        whole_ref[k, :quarter, :quarter] = cosine
        whole_ref[k, :quarter, quarter:] = sine
        whole_ref[k, quarter:, :quarter] = -sine
        whole_ref[k, quarter:, quarter:] = cosine


def left_tables(half_ref, whole_ref):
    quarter = half_ref.shape[1]
    at = lax.broadcasted_iota(jnp.int32, (quarter, quarter), 0)
    to = lax.broadcasted_iota(jnp.int32, (quarter, quarter), 1)
    same = jnp.where(at == to, 1.0, 0.0).astype(BF16)

    def turned(table):
        made = lax.dot_general(same, table, (((1,), (1,)), ((), ())), preferred_element_type=F32)
        return made.astype(BF16)

    def fill(k, carry):
        cosine, sine = turned(half_ref[k, :, :quarter]), turned(half_ref[k, :, quarter:])
        whole_ref[k, :quarter, :quarter] = cosine
        whole_ref[k, :quarter, quarter:] = -sine
        whole_ref[k, quarter:, :quarter] = sine
        whole_ref[k, quarter:, quarter:] = cosine
        return carry

    lax.fori_loop(0, RADIX, fill, 0)


def star_plan(slots, count_ref, cells_ref, bands_ref):
    chips = count_ref.shape[0] // 2
    first = [count_ref[2 * c] for c in range(chips)]
    held = [first[c] + count_ref[2 * c + 1] for c in range(chips)]
    level = []
    for y in range(chips // 2):
        both = held[2 * y] + held[2 * y + 1]
        if y == 0:
            level += [both // 2, both - both // 2]
        else:
            level += [2 * STARS_CHIP - level[0], 2 * STARS_CHIP - level[1]]
    keep_x = [jnp.minimum(held[c], level[c]) for c in range(chips)]
    keep_y = [jnp.minimum(level[c], STARS_CHIP) for c in range(chips)]

    def choose(values, index):
        out = values[0]
        for c in range(1, chips):
            out = jnp.where(index == c, values[c], out)
        return out

    def routes(chip):
        start, count, reached = choose(first, chip), choose(held, chip), choose(level, chip)
        kept_x, kept_y = choose(keep_x, chip), choose(keep_y, chip)

        def slot_of(place):
            place = jnp.minimum(place, count - 1)
            return jnp.where(place < start, place, slots + place - start)

        def after_x(place):
            place = jnp.minimum(place, reached - 1)
            return jnp.where(place < kept_x, slot_of(place), 2 * slots + place - kept_x)

        def after_y(place):
            return jnp.where(
                place < kept_y, after_x(place), 2 * slots + OVER_X + place - kept_y
            )

        return (
            [jnp.clip(slot_of(kept_x + i), 0, 2 * slots - 1) for i in range(OVER_X)]
            + [after_x(kept_y + i) for i in range(OVER_Y)]
            + [after_y(i) for i in range(STARS_CHIP)]
        )

    def star_at(chip, place):
        over_y = chip + 2 - 4 * (chip // 2)
        kept_y = choose(keep_y, chip)
        here = jnp.where(place < kept_y, chip, over_y)
        place = jnp.where(place < kept_y, place, choose(keep_y, over_y) + place - kept_y)
        over_x = here + 1 - 2 * (here % 2)
        kept_x = choose(keep_x, here)
        origin = jnp.where(place < kept_x, here, over_x)
        place = jnp.where(place < kept_x, place, choose(keep_x, over_x) + place - kept_x)
        inner = place < choose(first, origin)
        group = 2 * origin + jnp.where(inner, 0, 1)
        slot = jnp.where(inner, place, place - choose(first, origin))
        return jnp.clip(group, 0, 2 * chips - 1), jnp.clip(slot, 0, slots - 1)

    def cell_at(chip, place):
        group, slot = star_at(chip, place)
        return cells_ref[group, slot]

    def wave_at(chip, place, scale):
        group, slot = star_at(chip, place)
        band = bands_ref[group, slot]
        value = jnp.float32(0)
        for b in range(BANDS):
            length = 0.55 + 0.35 * b / (BANDS - 1)
            value = jnp.where(band == b, np.float32(scale / length), value)
        return value

    return routes, cell_at, wave_at


def aperture_widths(size, row_count, depth):
    widths = []
    for step in range(row_count // depth):
        lowest = abs(step * depth + depth - 1 - 0.5 * (size - 1))
        reach = 2 * (np.sqrt(0.25 * size * size - lowest * lowest) + 1)
        widths.append(min(size, int(-(-reach // 256) * 256)))
    return widths


def group_rows(step, depth, row_count, lanes):
    return [
        pl.ds(pl.multiple_of(lane * row_count + step * depth, depth), depth)
        for lane in range(lanes)
    ]


def focal_kernel(
    groups, lanes, count_hbm, cells_hbm, bands_hbm, coef_hbm, maps_ref, cot_ref, half_ref,
    turns_out, xr, xi, left_ref, right_ref, maps_buf, stage, raw, pool, x_stage, y_stage, ct, ct_turned,
    spread, yr, yi, route_ref, count_ref, cells_ref, bands_ref, coef_ref,
    small_sem, *scratch,
):
    steps = TURN_STEPS
    small = [
        pltpu.make_async_copy(count_hbm, count_ref, small_sem.at[0]),
        pltpu.make_async_copy(cells_hbm, cells_ref, small_sem.at[1]),
        pltpu.make_async_copy(bands_hbm, bands_ref, small_sem.at[2]),
        pltpu.make_async_copy(coef_hbm, coef_ref, small_sem.at[3]),
    ]
    for copy in small:
        copy.start()
    chunks = pool.shape[0]
    x_got, y_got = scratch[:chunks], scratch[chunks : 2 * chunks]
    (
        m_sem, t_local, t_send, t_recv, r_local, r_send, r_recv, x_send, x_recv,
        y_send, y_recv, z_local, z_send, z_recv,
    ) = scratch[2 * chunks :]
    row = lax.axis_index("row")
    me = lax.axis_index("star")
    core = me % 2
    chip = me // 2
    twin = me + 1 - 2 * core
    over_x = me + 2 - 4 * (chip % 2)
    over_y = me + 4 - 8 * (me // 4)
    map_count, row_count, size = maps_ref.shape
    depth = row_count // steps
    half = size // 2
    quarter = size // RADIX
    slots = raw.shape[0] // 2
    places = [(d, e) for e in range(2) for d in range(lanes)][1:]
    peers = [{"row": (row + d) % lanes, "star": twin if e else me} for d, e in places]
    peers_all = peers + [{"star": over_x}, {"star": over_y}]
    greet(peers_all)

    slot_range = pl.ds(core * slots, slots)
    some = slots // 2
    other = 1 - core
    raw_own = pltpu.make_async_copy(
        cot_ref.at[:, :, pl.ds(pl.multiple_of(core * half, half), half)], raw.at[slot_range], r_local
    )
    raw_twin = [
        send(
            cot_ref.at[
                pl.ds(part * some, some), :, pl.ds(pl.multiple_of(other * half, half), half)
            ],
            raw.at[pl.ds(core * slots + part * some, some)],
            r_send.at[part],
            r_recv.at[part],
            {"star": twin},
        )
        for part in range(2)
    ]
    raw_own.start()

    def fetch(step, part):
        rows = pl.ds(pl.multiple_of(step * depth + part * ROWS_STEP, ROWS_STEP), ROWS_STEP)
        return pltpu.make_async_copy(maps_ref.at[:, rows], maps_buf.at[part], m_sem.at[part])

    for part in range(depth // ROWS_STEP):
        fetch(0, part).start()
    greeted(peers_all)
    for copy in raw_twin:
        copy.start()
    for copy in small:
        copy.wait()
    routes, cell_at, wave_at = star_plan(slots, count_ref, cells_ref, bands_ref)
    places_here = [core * lanes + s for s in range(lanes)]
    cell_here = [cell_at(chip, place) for place in places_here]
    turn_here = [wave_at(chip, place, 1.0) for place in places_here]

    lines = lanes * ROWS_STEP
    wide = map_count * ROWS_STEP
    cells = lax.broadcasted_iota(jnp.int32, (ROWS_STEP, coef_ref.shape[0]), 1)
    hot = jnp.concatenate(
        [
            jnp.where(cells == cell_here[s], 1.0, 0.0).astype(BF16)
            for s in range(lanes)
        ],
        0,
    )
    coefs = jnp.dot(hot, coef_ref[...], preferred_element_type=F32).astype(BF16)
    at = lax.broadcasted_iota(jnp.int32, (map_count, wide), 0)
    to = lax.broadcasted_iota(jnp.int32, (map_count, wide), 1)
    repeat = jnp.where(to // ROWS_STEP == at, 1.0, 0.0).astype(BF16)
    repeated = jnp.dot(coefs, repeat, preferred_element_type=F32)
    at = lax.broadcasted_iota(jnp.int32, (lines, wide), 0)
    to = lax.broadcasted_iota(jnp.int32, (lines, wide), 1)
    spread[...] = jnp.where(at % ROWS_STEP == to % ROWS_STEP, repeated, 0.0).astype(BF16)

    widths = aperture_widths(size, row_count, depth)

    def turn_local(step):
        rows = pl.ds(pl.multiple_of(step * depth, depth), depth)
        place = pl.ds(pl.multiple_of(row * row_count + step * depth, depth), depth)
        return pltpu.make_async_copy(stage.at[row, rows], turns_out.at[place], t_local.at[step])

    def turn_copy(step, d, source, width):
        rows = pl.ds(pl.multiple_of(step * depth, depth), depth)
        place = pl.ds(pl.multiple_of(source * row_count + step * depth, depth), depth)
        cols = pl.ds((size - width) // 2, width)
        return send(
            stage.at[(row + d) % lanes, rows, cols],
            turns_out.at[place, cols],
            t_send.at[step],
            t_recv.at[step, d - 1],
            {"row": (row + d) % lanes},
        )

    def each_width(step, source, body):
        outer = jnp.where(source == 0, step, jnp.where(source == lanes - 1, steps - 1 - step, steps))
        first = 0
        for width in sorted(set(widths) | {size}):
            last = first + widths.count(width) if width < size else steps + 1

            @pl.when(jnp.logical_and(outer >= first, outer < last))
            def _():
                body(width)

            first = last

    def turns_start(step):
        turn_local(step).start()

        def start(width):
            for d in range(1, lanes):
                turn_copy(step, d, row, width).start()

        each_width(step, row, start)

    def turns_wait(step):
        turn_local(step).wait()
        rows = pl.ds(pl.multiple_of(step * depth, depth), depth)

        def sent(width):
            part = stage.at[pl.ds(0, lanes - 1), rows, pl.ds((size - width) // 2, width)]
            send(part, part, t_send.at[step], t_recv.at[step, 0], peers[0]).wait_send()

        each_width(step, row, sent)
        for d in range(1, lanes):
            source = (row + lanes - d) % lanes
            each_width(
                step, source, lambda width: turn_copy(step, d, source, width).wait_recv()
            )

    def phase_turns(step, carry):
        for part in range(depth // ROWS_STEP):
            fetch(step, part).wait()
            maps = maps_buf[part].reshape(wide, size)
            path = jnp.dot(spread[...], maps, preferred_element_type=F32)
            rows = pl.ds(pl.multiple_of(step * depth + part * ROWS_STEP, ROWS_STEP), ROWS_STEP)
            for s in range(lanes):
                turned = path[s * ROWS_STEP : (s + 1) * ROWS_STEP] * turn_here[s]
                stage[s, rows] = (turned - jnp.floor(turned + 0.5)).astype(BF16)

            @pl.when(step + 1 < steps)
            def _():
                fetch(step + 1, part).start()

        return carry

    def phase_step(step, carry):
        phase_turns(step, carry)
        turns_start(step)
        return carry

    def x_copy(c):
        return send(x_stage.at[c], x_got[c], x_send, x_recv.at[c], {"star": over_x})

    def y_copy(c):
        return send(y_stage.at[c], y_got[c], y_send, y_recv.at[c], {"star": over_y})

    tall = quarter // lanes
    piece = tall * RADIX // chunks
    parts = chunks // RADIX

    def star_piece(c, star):
        lined = pl.ds(pl.multiple_of(c * piece, piece), piece)
        return raw.at[2 * RADIX + star, lined]

    def z_target(c):
        kind, part = c // parts, c % parts
        return ct.at[
            kind,
            pl.ds(pl.multiple_of(row * tall + part * piece, piece), piece),
            pl.ds(pl.multiple_of(core * half, half), half),
        ]

    def z_local_copy(c):
        return pltpu.make_async_copy(star_piece(c, core * lanes + row), z_target(c), z_local.at[c])

    def z_start(c):
        z_local_copy(c).start()
        for d, e in places:
            star = (core + e) % 2 * lanes + (row + d) % lanes
            peer = {"row": (row + d) % lanes, "star": twin if e else me}
            send(star_piece(c, star), z_target(c), z_send, z_recv.at[c], peer).start()

    def z_arrival(c):
        sized = raw.at[pl.ds(0, len(places)), pl.ds(0, piece)]
        return send(sized, sized, z_send, z_recv.at[c], peers[0])

    def sort_slot(slot, carry):
        sorted_rows = jnp.dot(sort, raw[slot], preferred_element_type=F32).astype(BF16)
        for c in range(chunks):
            pool[c, slot] = sorted_rows[c * piece : (c + 1) * piece]
        return carry

    phase_turns(0, 0)
    for i, entry in enumerate(routes(chip)):
        route_ref[i] = entry
    at = lax.broadcasted_iota(jnp.int32, (row_count, row_count), 0)
    to = lax.broadcasted_iota(jnp.int32, (row_count, row_count), 1)
    sort = jnp.where(at % tall * RADIX + at // tall == to, 1.0, 0.0).astype(BF16)
    turns_start(0)
    raw_own.wait()
    lax.fori_loop(core * slots, core * slots + slots, sort_slot, 0)
    lax.fori_loop(1, EARLY_STEPS, phase_step, 0)
    for part in range(2):
        raw_twin[part].wait()
        begin = other * slots + part * some
        lax.fori_loop(begin, begin + some, sort_slot, 0)
    for c in range(chunks):
        for i in range(OVER_X):
            x_stage[c, i] = pool[c, route_ref[i]]
        x_copy(c).start()

    lax.fori_loop(EARLY_STEPS, steps, phase_step, 0)
    right_tables(half_ref, right_ref)
    left_tables(half_ref, left_ref)
    at = lax.broadcasted_iota(jnp.int32, (quarter, half), 0)
    to = lax.broadcasted_iota(jnp.int32, (quarter, half), 1)
    for k in range(RADIX):
        for side in range(2):
            raw[2 * k + side] = jnp.where(at * RADIX + k == to + side * half, 1.0, 0.0).astype(BF16)

    def pick_x(c, index):
        mine = pool[c, jnp.clip(index, 0, 2 * slots - 1)]
        far = x_got[c][jnp.clip(index - 2 * slots, 0, OVER_X - 1)]
        return jnp.where(index < 2 * slots, mine, far)

    def route_y(c):
        x_copy(c).wait_recv()
        for i in range(OVER_Y):
            y_stage[c, i] = pick_x(c, route_ref[OVER_X + i])
        y_copy(c).start()

    def route_z(c):
        y_copy(c).wait_recv()
        for i in range(STARS_CHIP):
            index = route_ref[OVER_X + OVER_Y + i]
            far = y_got[c][jnp.clip(index - 2 * slots - OVER_X, 0, OVER_Y - 1)]
            near = pick_x(c, jnp.minimum(index, 2 * slots + OVER_X - 1))
            raw[2 * RADIX + i, c * piece : (c + 1) * piece] = jnp.where(
                index < 2 * slots + OVER_X, near, far
            )
        z_start(c)

    blocks = [slice(m * quarter, (m + 1) * quarter) for m in range(RADIX)]
    centre = 0.5 * (size - 1)
    scale = 1.0 / size
    tile = lanes * depth

    def forward_columns(step, carry):
        turns_wait(step)
        rows = group_rows(step, depth, row_count, lanes)
        turns = jnp.concatenate([turns_out[r, :] for r in rows], 0)
        cosine, sine = turn_cos_sin(turns.astype(F32))
        line = lax.broadcasted_iota(jnp.int32, (tile, size), 0)
        place = line // depth * row_count + line % depth + step * depth
        row_pos = place.astype(F32) - centre
        col_pos = lax.broadcasted_iota(jnp.int32, (tile, size), 1).astype(F32) - centre
        inside = row_pos * row_pos + col_pos * col_pos <= 0.25 * size * size
        real = jnp.where(inside, cosine, 0.0)
        imag = jnp.where(inside, sine, 0.0)
        mixed_real, mixed_imag = butterfly(
            [real[:, b] for b in blocks], [imag[:, b] for b in blocks], -1
        )
        for k in range(RADIX):
            both = jnp.concatenate([mixed_real[k].astype(BF16), mixed_imag[k].astype(BF16)], 1)
            made = jnp.dot(both, right_ref[k], preferred_element_type=F32).astype(BF16)
            for lane in range(lanes):
                lined = slice(lane * depth, (lane + 1) * depth)
                yr[rows[lane], blocks[k]] = made[lined, :quarter]
                yi[rows[lane], blocks[k]] = made[lined, quarter:]
        return carry

    def focal(kind, carry):
        for part in range(parts):
            z_local_copy(kind * parts + part).wait()
            z_arrival(kind * parts + part).wait_recv()
        for side in range(2):
            cols = slice(side * half, (side + 1) * half)
            order = jnp.concatenate([raw[2 * k + side] for k in range(RADIX)], 0)
            turned = lax.dot_general(
                order, ct[kind, :, cols], (((1,), (1,)), ((), ())), preferred_element_type=F32
            )
            ct_turned[...] = turned if side == 0 else ct_turned[...] + turned
        cols = pl.ds(pl.multiple_of(kind * quarter, quarter), quarter)
        mixed_real, mixed_imag = butterfly(
            [yr[b, cols].astype(F32) for b in blocks],
            [yi[b, cols].astype(F32) for b in blocks],
            -1,
        )
        back_real, back_imag = [], []
        for k in range(RADIX):
            both = jnp.concatenate([mixed_real[k].astype(BF16), mixed_imag[k].astype(BF16)], 0)
            field = jnp.dot(left_ref[k], both, preferred_element_type=F32)
            weight = ct_turned[blocks[k], :] * (2.0 * scale)
            grad = (field * jnp.concatenate([weight, weight], 0)).astype(BF16)
            back = jnp.dot(right_ref[k], grad, preferred_element_type=F32)
            back_real.append(back[:quarter])
            back_imag.append(back[quarter:])
        spec_real, spec_imag = butterfly(back_real, back_imag, 1)
        for m in range(RADIX):
            xr[blocks[m], cols] = (spec_real[m] * scale).astype(BF16)
            xi[blocks[m], cols] = (spec_imag[m] * scale).astype(BF16)
        return carry

    column_plan = {chunks // 4: (0, 3), 3 * chunks // 8: (3, 6), 5 * chunks // 8: (6, 8)}
    focal_plan = {chunks - 2: 0, chunks - 1: 1}
    for c in range(chunks):
        route_y(c)
        if c in column_plan:
            first, last = column_plan[c]
            lax.fori_loop(first * steps // 8, last * steps // 8, forward_columns, 0)
        if c in focal_plan:
            focal(focal_plan[c], 0)
        route_z(c)
    lax.fori_loop(len(focal_plan), RADIX, focal, 0)
    sized = raw.at[pl.ds(0, len(places))]
    send(sized, sized, z_send, z_recv.at[0], peers[0]).wait_send()
    send(x_stage, x_stage, x_send, x_recv.at[0], {"star": over_x}).wait_send()
    send(y_stage, y_stage, y_send, y_recv.at[0], {"star": over_y}).wait_send()


def focal_fields(counts, cells, bands, coef_table, feature_maps, cotangent, halves, groups, lanes):
    map_count, row_count, size = feature_maps.shape
    slots = cotangent.shape[0]
    depth = row_count // TURN_STEPS
    half, quarter = size // 2, size // RADIX
    chunks = ROUTE_CHUNKS
    piece = row_count // chunks
    dma = pltpu.SemaphoreType.DMA
    smem = pl.BlockSpec(memory_space=pltpu.SMEM)
    vmem = pl.BlockSpec(memory_space=pltpu.VMEM)
    hbm = pl.BlockSpec(memory_space=pl.ANY)
    square = pltpu.VMEM((size, size), BF16)
    return pl.pallas_call(
        functools.partial(focal_kernel, groups, lanes),
        out_shape=(square,) * 3 + (pltpu.VMEM((RADIX, half, half), BF16),),
        in_specs=[pl.BlockSpec(memory_space=pltpu.HBM)] * 4 + [hbm, hbm, vmem],
        out_specs=(vmem,) * 4,
        scratch_shapes=[
            pltpu.VMEM((RADIX, half, half), BF16),
            pltpu.VMEM((depth // ROWS_STEP, map_count, ROWS_STEP, size), BF16),
            pltpu.VMEM((lanes, row_count, size), BF16),
            pltpu.VMEM((2 * slots, row_count, half), BF16),
            pltpu.VMEM((chunks, 2 * slots, piece, half), BF16),
            pltpu.VMEM((chunks, OVER_X, piece, half), BF16),
            pltpu.VMEM((chunks, OVER_Y, piece, half), BF16),
            pltpu.VMEM((RADIX, quarter, size), BF16),
            pltpu.VMEM((size, quarter), F32),
            pltpu.VMEM((lanes * ROWS_STEP, map_count * ROWS_STEP), BF16),
            pltpu.VMEM((size, size), BF16),
            pltpu.VMEM((size, size), BF16),
        ]
        + [
            pltpu.SMEM((OVER_X + OVER_Y + STARS_CHIP,), jnp.int32),
            pltpu.SMEM(counts.shape, jnp.int32),
            pltpu.SMEM(cells.shape, jnp.int32),
            pltpu.SMEM(bands.shape, jnp.int32),
            pltpu.VMEM(coef_table.shape, BF16),
            dma((4,)),
        ]
        + [pltpu.VMEM((OVER_X, piece, half), BF16)] * chunks
        + [pltpu.VMEM((OVER_Y, piece, half), BF16)] * chunks
        + [
            dma((depth // ROWS_STEP,)),
            dma((TURN_STEPS,)),
            dma((TURN_STEPS,)),
            dma((TURN_STEPS, lanes - 1)),
            dma,
            dma((2,)),
            dma((2,)),
            dma,
            dma((chunks,)),
            dma,
            dma((chunks,)),
            dma((chunks,)),
            dma,
            dma((chunks,)),
        ],
        compiler_params=pltpu.CompilerParams(
            collective_id=0, has_side_effects=True, vmem_limit_bytes=K1_LIMIT << 20
        ),
        name="focal_fields",
    )(counts, cells, bands, coef_table, feature_maps, cotangent, halves)


def gradient_kernel(
    groups, lanes, count_ref, cells_ref, bands_ref, coef_ref, turns_ref, xr, xi, left, maps_ref,
    grad_out, coef_out, cell_ref, gathered, away, maps_buf, score, weights, row_part, star_part,
    m_sem, z_send, z_recv, p_send, p_recv, c_send, c_recv, sr_send, sr_recv, ss_send, ss_recv,
):
    row = lax.axis_index("row")
    me = lax.axis_index("star")
    steps = GATHER_STEPS
    share = grad_out.shape[0]
    map_count, row_count, size = maps_ref.shape
    depth = row_count // steps
    parts = depth // ROWS_STEP
    quarter = size // RADIX
    total = groups * lanes
    core = me + 1 - 2 * (me % 2)
    across = me + 2 - 4 * ((me // 2) % 2)
    along = me + 4 - 8 * ((me // 4) % 2)
    corner = across + 4 - 8 * ((me // 4) % 2)
    row_peers = [{"row": (row + d) % lanes} for d in range(1, lanes)]
    star_peers = [{"star": (me + d) % groups} for d in range(1, groups)]
    to_core, to_across, to_along = {"star": core}, {"star": across}, {"star": along}
    greet(row_peers + star_peers)
    half_lanes = lanes // 2

    def fetch(step, part):
        rows = pl.ds(pl.multiple_of(step * depth + part * ROWS_STEP, ROWS_STEP), ROWS_STEP)
        return pltpu.make_async_copy(maps_ref.at[:, rows], maps_buf.at[part], m_sem.at[part])

    for part in range(parts):
        fetch(0, part).start()

    slots = cells_ref.shape[1]
    routes, cell_at, wave_at = star_plan(slots, count_ref, cells_ref, bands_ref)
    wave = wave_at(me // 2, me % 2 * lanes + row, 2.0 * np.pi)

    def cell_of(group, d):
        return cell_ref[group * lanes + (row + lanes - d) % lanes]

    blocks = [slice(m * quarter, (m + 1) * quarter) for m in range(RADIX)]
    centre = 0.5 * (size - 1)
    tile = lanes * depth

    def rows_at(step):
        return pl.ds(pl.multiple_of(step * depth, depth), depth)

    def block(group, step, first=0, count=lanes):
        return gathered.at[group, pl.ds(first, count), rows_at(step)]

    def z_start(step):
        for d in range(1, lanes):
            send(
                away.at[d - 1, rows_at(step)],
                gathered.at[me, d, rows_at(step)],
                z_send,
                z_recv.at[step],
                row_peers[d - 1],
            ).start()

    def plane(step, way, part, peer):
        send(part, part, p_send, p_recv.at[step, way], peer).start()

    def twin(step, part):
        send(part, part, c_send, c_recv.at[step], to_core).start()

    def sides(step, first, count):
        part = block(me, step, first, count)
        plane(step, 0, part, to_across)
        plane(step, 0, part, to_along)
        twin(step, part)

    def arrived(part, sem):
        send(part, part, p_send, sem, to_core).wait_recv()

    def columns_step(step):
        firsts = [(row + d) % lanes * row_count + step * depth for d in range(lanes)]
        rows = [pl.ds(pl.multiple_of(first, depth), depth) for first in firsts]
        turns = jnp.concatenate([turns_ref[r, :] for r in rows], 0)
        cosine, sine = turn_cos_sin(turns.astype(F32))
        line = lax.broadcasted_iota(jnp.int32, (tile, size), 0)
        place = (line // depth + row) % lanes * row_count + line % depth + step * depth
        row_pos = place.astype(F32) - centre
        col_pos = lax.broadcasted_iota(jnp.int32, (tile, size), 1).astype(F32) - centre
        inside = row_pos * row_pos + col_pos * col_pos <= 0.25 * size * size
        real = jnp.where(inside, cosine, 0.0)
        imag = jnp.where(inside, sine, 0.0)
        part_real, part_imag = [], []
        for k in range(RADIX):
            both = jnp.concatenate(
                [
                    jnp.concatenate([xr[r, blocks[k]] for r in rows], 0),
                    jnp.concatenate([xi[r, blocks[k]] for r in rows], 0),
                ],
                1,
            )
            made = jnp.dot(both, left[k], preferred_element_type=F32)
            part_real.append(made[:, :quarter])
            part_imag.append(made[:, quarter:])
        grad_real, grad_imag = butterfly(part_real, part_imag, 1)
        for m in range(RADIX):
            grad = real[:, blocks[m]] * grad_imag[m] - imag[:, blocks[m]] * grad_real[m]
            grad = (wave * grad).astype(BF16)
            gathered[me, 0, rows_at(step), blocks[m]] = grad[:depth]
            for d in range(1, lanes):
                away[d - 1, rows_at(step), blocks[m]] = grad[d * depth : (d + 1) * depth]

    def score_step(step):
        for part in range(parts):
            fetch(step, part).wait()
            rows = pl.ds(pl.multiple_of(step * depth + part * ROWS_STEP, ROWS_STEP), ROWS_STEP)
            grads = gathered[me, :, rows].reshape(lanes * ROWS_STEP, size)
            maps = maps_buf[part].reshape(map_count * ROWS_STEP, size)
            score[...] += lax.dot_general(
                maps, grads, (((1,), (1,)), ((), ())), preferred_element_type=F32
            )

            @pl.when(step + 1 < steps)
            def _():
                fetch(step + 1, part).start()

    def sums_step(step):
        for part in range(parts):
            rows = pl.ds(pl.multiple_of(step * depth + part * ROWS_STEP, ROWS_STEP), ROWS_STEP)
            grads = gathered[:, :, rows].reshape(wide, size)
            made = jnp.dot(weights[...], grads, preferred_element_type=F32)
            grad_out[:, rows] = made.reshape(share, ROWS_STEP, size)

    def row_copies():
        return [
            send(row_part.at[row], row_part.at[row], sr_send.at[d], sr_recv.at[d], row_peers[d])
            for d in range(lanes - 1)
        ]

    def star_copies():
        return [
            send(star_part.at[me], star_part.at[me], ss_send.at[d], ss_recv.at[d], star_peers[d])
            for d in range(groups - 1)
        ]

    def scores_rows():
        lined = score[...]
        at = lax.broadcasted_iota(jnp.int32, lined.shape, 0)
        to = lax.broadcasted_iota(jnp.int32, lined.shape, 1)
        kept = jnp.where(at % ROWS_STEP == to % ROWS_STEP, lined, 0.0)
        kept = jnp.sum(kept.reshape(map_count, ROWS_STEP, lined.shape[1]), axis=1)
        to = lax.broadcasted_iota(jnp.int32, kept.shape, 1)
        cell = lax.broadcasted_iota(jnp.int32, row_part.shape[1:], 1)
        part = jnp.zeros(row_part.shape[1:], F32)
        for d in range(lanes):
            value = jnp.sum(jnp.where(to // ROWS_STEP == d, kept, 0.0), axis=1, keepdims=True)
            part += jnp.where(cell == cell_of(me, d), value, 0.0)
        row_part[row] = part
        for copy in row_copies():
            copy.start()

    def scores_stars():
        for copy in row_copies():
            copy.wait()
        star_part[me] = jnp.sum(row_part[...], axis=0)
        for copy in star_copies():
            copy.start()

    def scores_end():
        for copy in star_copies():
            copy.wait()
        summed = jnp.sum(star_part[...], axis=0) * (1.0 / (8 * size))
        coef_out[...] = summed.T[: coef_out.shape[0]]

    def between(tick, lag, body):
        @pl.when(jnp.logical_and(tick >= lag, tick < steps + lag))
        def _():
            body(tick - lag)

    def compute(step, carry):
        columns_step(step)
        sides(step, 0, 1)
        return carry

    def own_arrived(step):
        sized = away.at[:, rows_at(step)]
        arrived(sized, z_recv.at[step])

        @pl.when(step + Z_AHEAD < steps)
        def _():
            z_start(step + Z_AHEAD)

        sides(step, 1, lanes - 1)

    def sides_arrived(step):
        arrived(gathered.at[pl.ds(0, 2), :, rows_at(step)], p_recv.at[step, 0])
        plane(step, 1, block(across, step, 0, half_lanes), to_along)
        plane(step, 1, block(along, step, half_lanes, lanes - half_lanes), to_across)
        twin(step, block(across, step))
        twin(step, block(along, step))

    def corners_arrived(step):
        arrived(gathered.at[pl.ds(0, 1), :, rows_at(step)], p_recv.at[step, 1])
        twin(step, block(corner, step))

    def all_arrived(step):
        arrived(gathered.at[pl.ds(0, groups // 2), :, rows_at(step)], c_recv.at[step])
        sums_step(step)

    def tick_body(tick, carry):
        between(tick, 0, own_arrived)
        between(tick, SIDES_LAG, sides_arrived)
        between(tick, SIDES_LAG + CORNERS_LAG, corners_arrived)
        between(tick, 0, score_step)

        @pl.when(tick == steps)
        def _():
            scores_rows()

        @pl.when(tick == steps + 1)
        def _():
            scores_stars()

        between(tick, SIDES_LAG + CORNERS_LAG + 1, all_arrived)
        return carry

    columns_step(0)
    greeted(row_peers + star_peers)
    z_start(0)
    sides(0, 0, 1)
    for step in range(1, Z_AHEAD):
        compute(step, 0)
        z_start(step)
    lax.fori_loop(Z_AHEAD, steps, compute, 0)
    def cell_fill(chip, carry):
        for place in range(STARS_CHIP):
            cell_ref[chip * STARS_CHIP + place] = cell_at(chip, place)
        return carry

    lax.fori_loop(0, total // STARS_CHIP, cell_fill, 0)
    at = lax.broadcasted_iota(jnp.int32, (total, coef_ref.shape[0]), 0)
    to = lax.broadcasted_iota(jnp.int32, (total, coef_ref.shape[0]), 1)
    wanted = jnp.zeros_like(at)
    for group in range(groups):
        for d in range(lanes):
            wanted = jnp.where(at == group * lanes + d, cell_of(group, d), wanted)
    hot = jnp.where(to == wanted, 1.0, 0.0).astype(BF16)
    rows_of = jnp.dot(hot, coef_ref[...], preferred_element_type=F32).astype(BF16)
    lines = share * ROWS_STEP
    wide = total * ROWS_STEP
    at = lax.broadcasted_iota(jnp.int32, (lines, map_count), 0)
    to = lax.broadcasted_iota(jnp.int32, (lines, map_count), 1)
    mine = jnp.where(to == me * share + at // ROWS_STEP, 1.0, 0.0).astype(BF16)
    columns = lax.dot_general(
        mine, rows_of, (((1,), (1,)), ((), ())), preferred_element_type=F32
    ).astype(BF16)
    at = lax.broadcasted_iota(jnp.int32, (total, wide), 0)
    to = lax.broadcasted_iota(jnp.int32, (total, wide), 1)
    repeat = jnp.where(to // ROWS_STEP == at, 1.0, 0.0).astype(BF16)
    repeated = jnp.dot(columns, repeat, preferred_element_type=F32)
    at = lax.broadcasted_iota(jnp.int32, (lines, wide), 0)
    to = lax.broadcasted_iota(jnp.int32, (lines, wide), 1)
    weights[...] = jnp.where(at % ROWS_STEP == to % ROWS_STEP, repeated, 0.0).astype(BF16)
    score[...] = jnp.zeros_like(score)
    lax.fori_loop(0, steps + SIDES_LAG + CORNERS_LAG + 1, tick_body, 0)
    scores_end()
    send(away, away, z_send, z_recv.at[0], to_core).wait_send()
    three, four = gathered.at[pl.ds(0, 3)], gathered.at[pl.ds(0, groups // 2)]
    send(three, three, p_send, z_recv.at[0], to_core).wait_send()
    send(four, four, c_send, z_recv.at[0], to_core).wait_send()


def gradient_sums(counts, cells, bands, coef_table, turns, spec_real, spec_imag, left, feature_maps, groups, lanes):
    map_count, row_count, size = feature_maps.shape
    cell_count = coef_table.shape[0]
    share = map_count // groups
    depth = row_count // GATHER_STEPS
    dma = pltpu.SemaphoreType.DMA
    smem = pl.BlockSpec(memory_space=pltpu.SMEM)
    vmem = pl.BlockSpec(memory_space=pltpu.VMEM)
    hbm = pl.BlockSpec(memory_space=pl.ANY)
    padded = -(-cell_count // 128) * 128
    return pl.pallas_call(
        functools.partial(gradient_kernel, groups, lanes),
        out_shape=(
            pltpu.VMEM((share, row_count, size), F32),
            jax.ShapeDtypeStruct((cell_count, map_count), F32),
        ),
        in_specs=[smem, smem, smem, vmem, vmem, vmem, vmem, vmem, hbm],
        out_specs=(vmem, vmem),
        scratch_shapes=[
            pltpu.SMEM((groups * lanes,), jnp.int32),
            pltpu.VMEM((groups, lanes, row_count, size), BF16),
            pltpu.VMEM((lanes - 1, row_count, size), BF16),
            pltpu.VMEM((depth // ROWS_STEP, map_count, ROWS_STEP, size), BF16),
            pltpu.VMEM((map_count * ROWS_STEP, lanes * ROWS_STEP), F32),
            pltpu.VMEM((share * ROWS_STEP, groups * lanes * ROWS_STEP), BF16),
            pltpu.VMEM((lanes, map_count, padded), F32),
            pltpu.VMEM((groups, map_count, padded), F32),
            dma((depth // ROWS_STEP,)),
            dma,
            dma((GATHER_STEPS,)),
            dma,
            dma((GATHER_STEPS, 2)),
            dma,
            dma((GATHER_STEPS,)),
            dma((lanes - 1,)),
            dma((lanes - 1,)),
            dma((groups - 1,)),
            dma((groups - 1,)),
        ],
        compiler_params=pltpu.CompilerParams(
            collective_id=1, has_side_effects=True, vmem_limit_bytes=K2_LIMIT << 20
        ),
        name="gradient_sums",
    )(counts, cells, bands, coef_table, turns, spec_real, spec_imag, left, feature_maps)


def star_devices(feature_maps, coef_table, star_counts, star_cells, star_bands, psf_cotangent):
    groups = lax.axis_size("star")
    lanes = lax.axis_size("row")
    size = feature_maps.shape[2]
    halves = half_tables(size)
    turns, spec_real, spec_imag, left = focal_fields(
        star_counts, star_cells, star_bands, coef_table, feature_maps, psf_cotangent, halves, groups, lanes
    )
    return gradient_sums(
        star_counts, star_cells, star_bands, coef_table, turns, spec_real, spec_imag, left, feature_maps,
        groups, lanes,
    )


def solution(mesh):
    placed = (P(None, "row", None), P(), P(), P(), P(), P("star", "row", None))
    fits = mesh.shape["row"] == LIVE_DEV and mesh.shape["star"] == PLANE_DEV
    device = star_devices if fits else per_device
    return jax.shard_map(
        device,
        mesh=mesh,
        in_specs=placed,
        out_specs=(P("star", "row", None), P()),
        check_vma=False,
    )
```
